32 devices in a mesh: dp: 2 (over core), bal: 16 (over z, y, x).
Axes of the slice: x: 2, y: 2, z: 4, core: 2. Of those that a mesh axis runs over, the one named last changes fastest.
Arguments:
- tokens: bfloat16 [64, 512, 768], P(('dp', 'bal')), may hold values from -6 to 6
- cotangent: bfloat16 [64, 512, 768], P(('dp', 'bal')), may hold values from -6 to 6
- seq_lengths: int32 [64], P(('dp', 'bal')), may hold values from 256 to 512, as said below
- token_mask: int32 [64, 512], P(('dp', 'bal')), may hold values from 0 to 1, as said below
- step_count: int32 [1], replicated, may hold values from 1 to 20
- attn_master: float32 [2, 4, 768, 768], P(None, None, 'bal')
- attn_first: float32 [2, 4, 768, 768], P(None, None, 'bal'), may hold values from -0.00018310547 to 0.00018310547
- attn_second: float32 [2, 4, 768, 768], P(None, None, 'bal'), may hold values from 7.0550676e-11 to 2.822027e-10
- up_master: float32 [2, 768, 3072], P(None, 'bal'), may hold values from -0.21875 to 0.21875
- up_first: float32 [2, 768, 3072], P(None, 'bal'), may hold values from -0.00018310547 to 0.00018310547
- up_second: float32 [2, 768, 3072], P(None, 'bal'), may hold values from 7.0550676e-11 to 2.822027e-10
- down_master: float32 [2, 3072, 768], P(None, 'bal'), may hold values from -0.109375 to 0.109375
- down_first: float32 [2, 3072, 768], P(None, 'bal'), may hold values from -0.00018310547 to 0.00018310547
- down_second: float32 [2, 3072, 768], P(None, 'bal'), may hold values from 7.0550676e-11 to 2.822027e-10
- small_master: float32 [2, 12, 768], P(None, None, 'bal')
- small_first: float32 [2, 12, 768], P(None, None, 'bal'), may hold values from -0.00048828125 to 0.00048828125
- small_second: float32 [2, 12, 768], P(None, None, 'bal'), may hold values from 6.349561e-10 to 2.5398244e-09
Outputs:
- output: bfloat16 [64, 512, 768], P(('dp', 'bal'))
- input_grad: bfloat16 [64, 512, 768], P(('dp', 'bal'))
- grad_norm: float32 [1], replicated
- attn_weight: float32 [2, 4, 768, 768], P(None, None, 'bal')
- attn_first_new: float32 [2, 4, 768, 768], P(None, None, 'bal')
- attn_second_new: float32 [2, 4, 768, 768], P(None, None, 'bal')
- attn_copy: bfloat16 [2, 4, 768, 768], P(None, None, 'bal')
- up_weight: float32 [2, 768, 3072], P(None, 'bal')
- up_first_new: float32 [2, 768, 3072], P(None, 'bal')
- up_second_new: float32 [2, 768, 3072], P(None, 'bal')
- up_copy: bfloat16 [2, 768, 3072], P(None, 'bal')
- down_weight: float32 [2, 3072, 768], P(None, 'bal')
- down_first_new: float32 [2, 3072, 768], P(None, 'bal')
- down_second_new: float32 [2, 3072, 768], P(None, 'bal')
- down_copy: bfloat16 [2, 3072, 768], P(None, 'bal')
- small_weight: float32 [2, 12, 768], P(None, None, 'bal')
- small_first_new: float32 [2, 12, 768], P(None, None, 'bal')
- small_second_new: float32 [2, 12, 768], P(None, None, 'bal')
- small_copy: bfloat16 [2, 12, 768], P(None, None, 'bal')
The draws below stay inside these ranges and needn't reach their ends.
Inputs may be any that keep to these rules, and one draw needn't show every extreme that they name: `seq_lengths`: among the 2 sequences of each device one has length 512. `token_mask`: ones stand only at positions below the sequence's length. In every aligned run of 16 devices along bal one device holds exactly 384 ones among its 1024 positions and each other device holds at least 1 and at most 128.
All inputs are finite; a program needn't handle non-finite values.
Results may differ from the reference program's by a relative error of at most 0.019.
The reference program's roundings to bfloat16 on the way count: a program that leaves them out, or rounds other values in their place, can miss the bound.
Values may be sent and summed in bfloat16 or wider, within the bound.
No kernel may reach another device: no remote copies, remote signals or barrier semaphores. Data moves between devices by JAX's collectives and lax.ppermute only.
A program may use at most 384 MiB of HBM per device.

```python
import math
import jax
import jax.numpy as jnp
from jax import lax

D = 768
HEADS = 12
HEAD_DIM = 64
FF = 3072
LAYERS = 2
LEN = 512
SEQ_DEV = 2
TOK_DEV = 1024
SEQS = 64
MCAP = 384
PEERS = 16
PARAMS = 14174208


def lengths_of(key):
    base_key = jax.random.fold_in(key, 101)
    first_key, second_key = jax.random.split(base_key)
    devices_all = SEQS // SEQ_DEV
    drawn_lengths = jax.random.randint(first_key, (SEQS,), LEN // 2, LEN + 1)
    chosen = jax.random.randint(second_key, (devices_all, 1), 0, SEQ_DEV)
    full_seq = (jnp.arange(SEQ_DEV)[None, :] == chosen).reshape(-1)
    return jnp.where(full_seq, LEN, drawn_lengths).astype(jnp.int32)


def draw_seq_lengths(key, part):
    return lengths_of(key)


def draw_token_mask(key, part):
    lengths = lengths_of(key)
    base_key = jax.random.fold_in(key, 202)
    count_key, busy_key, order_key = jax.random.split(base_key, 3)
    devices_all = SEQS // SEQ_DEV
    counts = jax.random.randint(count_key, (devices_all,), 1, TOK_DEV // 8 + 1)
    busy_device = jax.random.randint(busy_key, (devices_all // PEERS, 1), 0, PEERS)
    busiest = (jnp.arange(PEERS)[None, :] == busy_device).reshape(-1)
    counts = jnp.where(busiest, MCAP, counts)
    order_rank = jax.vmap(lambda sub_key: jax.random.permutation(sub_key, TOK_DEV))(jax.random.split(order_key, devices_all))
    inside = (jnp.arange(LEN)[None, :] < lengths[:, None]).reshape(devices_all, TOK_DEV)
    scores = order_rank.astype(jnp.int32) + TOK_DEV * (1 - inside.astype(jnp.int32))
    rank_table = jnp.argsort(jnp.argsort(scores, axis=1), axis=1)
    chosen = rank_table < counts[:, None]
    return chosen.reshape(SEQS, LEN).astype(jnp.int32)


def draw_attn_master(key, part):
    base_key = jax.random.fold_in(key, 303)
    raw_draw = jax.random.normal(base_key, (LAYERS, 4, D, D), jnp.float32)
    slab_index = jnp.arange(4)[None, :, None, None]
    return raw_draw * jnp.where(slab_index == 3, 8.0, 1.0) * D ** (-0.5)


def draw_small_master(key, part):
    base_key = jax.random.fold_in(key, 404)
    raw_draw = jax.random.normal(base_key, (LAYERS, 12, D), jnp.float32)
    row_index = jnp.arange(12)[None, :, None]
    gain_row = (row_index == 3) | (row_index == 10)
    return jnp.where(gain_row, 1.0 + 0.1 * raw_draw, 0.2 * raw_draw)


def shard_levels(stream_key, extent, cuts, low, top_value):
    def one(axis_at, blocks):
        steps = jax.random.uniform(jax.random.fold_in(jax.random.fold_in(stream_key, 6), axis_at), (blocks,), jnp.float32, low / len(cuts), top_value / len(cuts))
        return jnp.repeat(jnp.exp(steps), extent[axis_at] // blocks).reshape((-1,) + (1,) * (len(extent) - axis_at - 1))

    factor_of = one(*cuts[0])
    for cut in cuts[1:]:
        factor_of = factor_of * one(*cut)
    return factor_of


def noise(key, dims, spread, reach, cuts=(), held_as=jnp.bfloat16):
    drawn = spread * jax.random.normal(key, dims, jnp.float32)
    if cuts:
        drawn = drawn * shard_levels(key, dims, cuts, -0.22, 0.18)
    return jnp.clip(drawn, -reach, reach).astype(held_as)


def setup_inputs(seed: int = 0) -> dict:
    key_list = jax.random.split(jax.random.key(seed), 18)
    return {
        "tokens": noise(key_list[0], (SEQS, LEN, D), 1.0, 6.0, ((0, 32),)),
        "cotangent": noise(key_list[1], (SEQS, LEN, D), 1.0, 6.0, ((0, 32),)),
        "seq_lengths": draw_seq_lengths(jax.random.fold_in(key_list[17], 71), 0),
        "token_mask": draw_token_mask(jax.random.fold_in(key_list[17], 71), 0),
        "step_count": jax.random.randint(key_list[4], (1,), 1, 21).astype(jnp.int32),
        "attn_master": draw_attn_master(jax.random.fold_in(key_list[17], 71), 0),
        "attn_first": noise(key_list[6], (LAYERS, 4, D, D), (0.111 / PARAMS ** 0.5), 0.00018310547, ((2, 16),), jnp.float32),
        "attn_second": jnp.clip(jnp.exp(math.log(2.822027056481602e-10) - 1.3862944 * jax.random.uniform(key_list[7], (LAYERS, 4, D, D), jnp.float32) ** shard_levels(key_list[7], (LAYERS, 4, D, D), ((2, 16),), -0.2, 0.2)), 7.055067641204005e-11, 2.822027056481602e-10),
        "up_master": noise(key_list[8], (LAYERS, D, FF), D ** -0.5, 0.21875, ((1, 16),), jnp.float32),
        "up_first": noise(key_list[9], (LAYERS, D, FF), (0.111 / PARAMS ** 0.5), 0.00018310547, ((1, 16),), jnp.float32),
        "up_second": jnp.clip(jnp.exp(math.log(2.822027056481602e-10) - 1.3862944 * jax.random.uniform(key_list[10], (LAYERS, D, FF), jnp.float32) ** shard_levels(key_list[10], (LAYERS, D, FF), ((1, 16),), -0.2, 0.2)), 7.055067641204005e-11, 2.822027056481602e-10),
        "down_master": noise(key_list[11], (LAYERS, FF, D), FF ** -0.5, 0.109375, ((1, 16),), jnp.float32),
        "down_first": noise(key_list[12], (LAYERS, FF, D), (0.111 / PARAMS ** 0.5), 0.00018310547, ((1, 16),), jnp.float32),
        "down_second": jnp.clip(jnp.exp(math.log(2.822027056481602e-10) - 1.3862944 * jax.random.uniform(key_list[13], (LAYERS, FF, D), jnp.float32) ** shard_levels(key_list[13], (LAYERS, FF, D), ((1, 16),), -0.2, 0.2)), 7.055067641204005e-11, 2.822027056481602e-10),
        "small_master": draw_small_master(jax.random.fold_in(key_list[17], 71), 0),
        "small_first": noise(key_list[15], (LAYERS, 12, D), (0.333 / PARAMS ** 0.5), 0.00048828125, ((2, 16),), jnp.float32),
        "small_second": jnp.clip(jnp.exp(math.log(2.5398243508334417e-09) - 1.3862944 * jax.random.uniform(key_list[16], (LAYERS, 12, D), jnp.float32) ** shard_levels(key_list[16], (LAYERS, 12, D), ((2, 16),), -0.2, 0.2)), 6.349560877083604e-10, 2.5398243508334417e-09),
    }


LN_EPS = 1e-06
NEG_FILL = -1000000000.0
CLIP_NORM = 1.0
LEARN_RATE = 0.05
SMALL_RATE = 0.25
BETA_FIRST = 0.9
BETA_SECOND = 0.999
ADAM_EPS = 1e-08
WEIGHT_DECAY = 0.01

@jax.custom_vjp
def low(v):
    return lax.optimization_barrier(v.astype(jnp.bfloat16)).astype(jnp.float32)

@jax.custom_vjp
def low_back(v):
    return v

def low_keep(v):
    return (low(v), None)

def low_pass(kept, grad):
    return (grad,)

def back_keep(v):
    return (v, None)

def back_low(kept, grad):
    return (low(grad),)
low.defvjp(low_keep, low_pass)
low_back.defvjp(back_keep, back_low)

def both_round(value):
    return low(low_back(value))

def product(left_side, right_side):
    return jnp.dot(left_side, right_side, precision=lax.Precision.HIGHEST, preferred_element_type=jnp.float32)

def layer_norm(residual, norm_gain, norm_shift):
    centered = residual - lax.optimization_barrier(jnp.mean(residual, axis=-1, keepdims=True))
    variance = lax.optimization_barrier(jnp.mean(centered * centered, axis=-1, keepdims=True))
    return centered * lax.rsqrt(variance + LN_EPS) * norm_gain + norm_shift

def attention_layer(hidden, attn_layer, small_layer, lengths):
    group_size, length, model_width = hidden.shape
    shape_heads = (group_size, length, HEADS, HEAD_DIM)
    hidden_low = low(hidden)
    queries = both_round(product(hidden_low, attn_layer[0]) + small_layer[0]).reshape(shape_heads)
    key_rows = both_round(product(hidden_low, attn_layer[1])).reshape(shape_heads)
    values = both_round(product(hidden_low, attn_layer[2]) + small_layer[1]).reshape(shape_heads)
    scores = low_back(jnp.einsum('gqhd,gkhd->ghqk', queries, key_rows, precision=lax.Precision.HIGHEST) * (1.0 / math.sqrt(HEAD_DIM)))
    key_ok = (jnp.arange(length)[None, :] < lengths[:, None])[:, None, None, :]
    scores = jnp.where(key_ok, scores, NEG_FILL)
    exp_scores = jnp.exp(scores - lax.optimization_barrier(jnp.max(scores, axis=-1, keepdims=True)))
    attn_probs = exp_scores / lax.optimization_barrier(jnp.sum(exp_scores, axis=-1, keepdims=True))
    mixed_heads = jnp.einsum('ghqk,gkhd->gqhd', low(attn_probs), values, precision=lax.Precision.HIGHEST)
    mixed_heads = both_round(mixed_heads.reshape(group_size, length, model_width))
    branch = low_back(product(mixed_heads, attn_layer[3]) + small_layer[2])
    return layer_norm(hidden + branch, small_layer[3], small_layer[4])

def feed_layer(attended, up_layer, down_layer, small_layer):
    pre_act = low_back(product(low(attended), up_layer) + small_layer[5:9].reshape(-1))
    act_low = low(jax.nn.gelu(pre_act, approximate=False))
    branch = low_back(product(act_low, down_layer) + small_layer[9])
    return layer_norm(attended + branch, small_layer[10], small_layer[11])

def forward_group(weight_set, tokens_group, lengths, mask_rows):
    attn_all, up_all, down_all, small_all = weight_set
    hidden = attention_layer(tokens_group, attn_all[0], small_all[0], lengths)
    hidden = feed_layer(hidden, up_all[0], down_all[0], small_all[0])
    middle = attention_layer(hidden, attn_all[1], small_all[1], lengths)
    served = feed_layer(middle, up_all[1], down_all[1], small_all[1])
    return jnp.where(mask_rows[:, :, None] == 1, served, middle)

def adam_update(master, first_moment, second_moment, gradient, clip_scale, step_value, decay_rate, rate_value):
    clipped = gradient * clip_scale
    first_new = BETA_FIRST * first_moment + (1.0 - BETA_FIRST) * clipped
    second_new = BETA_SECOND * second_moment + (1.0 - BETA_SECOND) * clipped * clipped
    first_hat = first_new / (1.0 - jnp.power(BETA_FIRST, step_value))
    second_hat = second_new / (1.0 - jnp.power(BETA_SECOND, step_value))
    master_new = master - rate_value * (first_hat / (jnp.sqrt(second_hat) + ADAM_EPS) + decay_rate * master)
    return (master_new, first_new, second_new, master_new.astype(jnp.bfloat16))

def reference(tokens, cotangent, seq_lengths, token_mask, step_count, attn_master, attn_first, attn_second, up_master, up_first, up_second, down_master, down_first, down_second, small_master, small_first, small_second):
    masters = (attn_master, up_master, down_master, small_master)
    weight_set = tuple((master.astype(jnp.bfloat16).astype(jnp.float32) for master in masters))
    group_size = math.gcd(SEQS, 8)
    blocks_len = seq_lengths.reshape(-1, group_size)
    blocks_mask = token_mask.reshape(-1, group_size, LEN)

    def run(weights_in, tokens_in):

        def one_group(pieces):
            return forward_group(weights_in, pieces[0], pieces[1], pieces[2])
        results = lax.map(jax.checkpoint(one_group), (tokens_in.reshape(-1, group_size, LEN, D), blocks_len, blocks_mask))
        return results.reshape(SEQS, LEN, D)
    result, pull_back = jax.vjp(run, weight_set, tokens.astype(jnp.float32))
    grad_set, d_tokens = pull_back(cotangent.astype(jnp.float32))
    square_total = jnp.sum(grad_set[0] * grad_set[0]) + jnp.sum(grad_set[1] * grad_set[1]) + jnp.sum(grad_set[2] * grad_set[2]) + jnp.sum(grad_set[3] * grad_set[3])
    grad_norm = jnp.sqrt(square_total).reshape(1)
    clip_scale = jnp.minimum(1.0, CLIP_NORM / (grad_norm[0] + 1e-06))
    step_value = step_count[0].astype(jnp.float32)
    attn_new = adam_update(attn_master, attn_first, attn_second, grad_set[0], clip_scale, step_value, WEIGHT_DECAY, LEARN_RATE)
    up_new = adam_update(up_master, up_first, up_second, grad_set[1], clip_scale, step_value, WEIGHT_DECAY, LEARN_RATE)
    down_new = adam_update(down_master, down_first, down_second, grad_set[2], clip_scale, step_value, WEIGHT_DECAY, LEARN_RATE)
    small_new = adam_update(small_master, small_first, small_second, grad_set[3], clip_scale, step_value, 0.0, SMALL_RATE)
    return (result.astype(jnp.bfloat16), d_tokens.astype(jnp.bfloat16), grad_norm, attn_new[0], attn_new[1], attn_new[2], attn_new[3], up_new[0], up_new[1], up_new[2], up_new[3], down_new[0], down_new[1], down_new[2], down_new[3], small_new[0], small_new[1], small_new[2], small_new[3])
```

```python
import math

import jax
import jax.numpy as jnp
from jax import lax
from jax.experimental.layout import Layout, with_layout_constraint
from jax.sharding import PartitionSpec as P

HEADS = 12
HEAD_DIM = 64
MCAP = 384


LN_EPS = 1e-06
NEG_FILL = -1000000000.0
CLIP_NORM = 1.0
LEARN_RATE = 0.05
SMALL_RATE = 0.25
BETA_FIRST = 0.9
BETA_SECOND = 0.999
ADAM_EPS = 1e-08
WEIGHT_DECAY = 0.01


def forward_product(left_side, right_side):
    return jnp.dot(left_side, right_side, preferred_element_type=jnp.float32)


def weight_grad(left_side, right_side):
    return lax.dot_general(
        left_side, right_side, (((0,), (0,)), ((), ())), preferred_element_type=jnp.float32
    )


def back_product(left_side, right_side):
    return lax.dot_general(
        left_side, right_side, (((1,), (1,)), ((), ())), preferred_element_type=jnp.float32
    )


def norm_forward(residual, norm_gain, norm_shift):
    centered = residual - jnp.mean(residual, axis=-1, keepdims=True)
    variance = jnp.mean(centered * centered, axis=-1, keepdims=True)
    inv_std = lax.rsqrt(variance + LN_EPS)
    normal_part = centered * inv_std
    return (normal_part * norm_gain + norm_shift, normal_part, inv_std)


def norm_backward(d_out, normal_part, inv_std, norm_gain):
    d_normal = d_out * norm_gain
    d_resid = inv_std * (
        d_normal
        - jnp.mean(d_normal, axis=-1, keepdims=True)
        - normal_part * jnp.mean(d_normal * normal_part, axis=-1, keepdims=True)
    )
    return (d_resid, jnp.sum(d_out * normal_part, axis=0), jnp.sum(d_out, axis=0))


def gelu_slope(pre_act):
    return (
        0.5 * (1.0 + lax.erf(pre_act * 0.7071067811865476))
        + pre_act * jnp.exp(-0.5 * pre_act * pre_act) * 0.3989422804014327
    )


def head_split(flat_rows, seq_count):
    return flat_rows.reshape(seq_count, -1, HEADS, HEAD_DIM)


def key_mask(seq_lengths, length):
    return (jnp.arange(length)[None, :] < seq_lengths[:, None])[:, None, None, :]


def score_block(query_heads, key_heads, mask_keys):
    scores = jnp.einsum(
        "sqhd,skhd->shqk", query_heads, key_heads, preferred_element_type=jnp.float32
    ) * (1.0 / math.sqrt(HEAD_DIM))
    return jnp.where(mask_keys, scores, NEG_FILL)


def attend_forward(hidden, attn_layer, small_layer, seq_lengths):
    seq_count, length, model_width = hidden.shape
    flat_rows = hidden.reshape(seq_count * length, model_width)
    flat_low = flat_rows.astype(jnp.bfloat16)
    queries = (forward_product(flat_low, attn_layer[0]) + small_layer[0]).astype(jnp.bfloat16)
    key_rows = forward_product(flat_low, attn_layer[1]).astype(jnp.bfloat16)
    values = (forward_product(flat_low, attn_layer[2]) + small_layer[1]).astype(jnp.bfloat16)
    scores = score_block(
        head_split(queries, seq_count),
        head_split(key_rows, seq_count),
        key_mask(seq_lengths, length),
    )
    row_top = jnp.max(scores, axis=-1, keepdims=True)
    exp_scores = jnp.exp(scores - row_top)
    row_total = jnp.sum(exp_scores, axis=-1, keepdims=True)
    probs_low = (exp_scores / row_total).astype(jnp.bfloat16)
    log_total = row_top + jnp.log(row_total)
    mixed_heads = jnp.einsum(
        "shqk,skhd->sqhd",
        probs_low,
        head_split(values, seq_count),
        preferred_element_type=jnp.float32,
    )
    mixed_heads = mixed_heads.reshape(seq_count * length, model_width).astype(jnp.bfloat16)
    branch = forward_product(mixed_heads, attn_layer[3]) + small_layer[2]
    normed, normal_part, inv_std = norm_forward(flat_rows + branch, small_layer[3], small_layer[4])
    return (
        normed,
        (flat_low, queries, key_rows, values, log_total, mixed_heads, normal_part, inv_std),
    )


def attend_backward(d_normed, kept_state, attn_layer, small_layer, seq_lengths, seq_count, length):
    flat_low, queries, key_rows, values, log_total, mixed_heads, normal_part, inv_std = kept_state
    row_count, model_width = flat_low.shape
    d_resid, d_gain, d_shift = norm_backward(d_normed, normal_part, inv_std, small_layer[3])
    d_branch = d_resid.astype(jnp.bfloat16)
    d_out_bias = jnp.sum(d_branch.astype(jnp.float32), axis=0)
    d_out_weight = weight_grad(mixed_heads, d_branch)
    d_mixed = head_split(back_product(d_branch, attn_layer[3]).astype(jnp.bfloat16), seq_count)
    query_heads = head_split(queries, seq_count)
    key_heads = head_split(key_rows, seq_count)
    value_heads = head_split(values, seq_count)
    scores = score_block(query_heads, key_heads, key_mask(seq_lengths, length))
    attn_probs = jnp.exp(scores - log_total)
    d_values = jnp.einsum(
        "shqk,sqhd->skhd",
        attn_probs.astype(jnp.bfloat16),
        d_mixed,
        preferred_element_type=jnp.float32,
    )
    d_values = d_values.reshape(row_count, model_width).astype(jnp.bfloat16)
    d_probs = jnp.einsum(
        "sqhd,skhd->shqk", d_mixed, value_heads, preferred_element_type=jnp.float32
    )
    d_scores = (
        attn_probs * (d_probs - jnp.sum(attn_probs * d_probs, axis=-1, keepdims=True))
    ).astype(jnp.bfloat16)
    scale_factor = 1.0 / math.sqrt(HEAD_DIM)
    d_queries = (
        jnp.einsum("shqk,skhd->sqhd", d_scores, key_heads, preferred_element_type=jnp.float32)
        * scale_factor
    )
    d_queries = d_queries.reshape(row_count, model_width).astype(jnp.bfloat16)
    d_keys = (
        jnp.einsum("shqk,sqhd->skhd", d_scores, query_heads, preferred_element_type=jnp.float32)
        * scale_factor
    )
    d_keys = d_keys.reshape(row_count, model_width).astype(jnp.bfloat16)
    weight_set = jnp.concatenate(
        [
            weight_grad(flat_low, d_queries),
            weight_grad(flat_low, d_keys),
            weight_grad(flat_low, d_values),
            d_out_weight,
        ],
        axis=1,
    )
    d_hidden = (
        d_resid
        + back_product(d_queries, attn_layer[0])
        + back_product(d_keys, attn_layer[1])
        + back_product(d_values, attn_layer[2])
    )
    small_rows = jnp.stack(
        [
            jnp.sum(d_queries.astype(jnp.float32), axis=0),
            jnp.sum(d_values.astype(jnp.float32), axis=0),
            d_out_bias,
            d_gain,
            d_shift,
        ]
    )
    return (d_hidden, weight_set, small_rows)


def feed_forward(rows_in, up_layer, down_layer, small_layer):
    rows_low = rows_in.astype(jnp.bfloat16)
    pre_act = forward_product(rows_low, up_layer) + small_layer[5:9].reshape(-1)
    act_low = jax.nn.gelu(pre_act, approximate=False).astype(jnp.bfloat16)
    branch = forward_product(act_low, down_layer) + small_layer[9]
    normed, normal_part, inv_std = norm_forward(rows_in + branch, small_layer[10], small_layer[11])
    return (normed, (rows_low, pre_act, act_low, normal_part, inv_std))


def feed_backward(d_normed, kept_state, up_layer, down_layer, small_layer):
    rows_low, pre_act, act_low, normal_part, inv_std = kept_state
    d_resid, d_gain, d_shift = norm_backward(d_normed, normal_part, inv_std, small_layer[10])
    d_branch = d_resid.astype(jnp.bfloat16)
    d_down = weight_grad(act_low, d_branch)
    d_pre = (back_product(d_branch, down_layer) * gelu_slope(pre_act)).astype(jnp.bfloat16)
    d_up = weight_grad(rows_low, d_pre)
    d_rows = d_resid + back_product(d_pre, up_layer)
    model_width = d_resid.shape[1]
    small_rows = jnp.concatenate(
        [
            jnp.sum(d_pre.astype(jnp.float32), axis=0).reshape(4, model_width),
            jnp.stack([jnp.sum(d_branch.astype(jnp.float32), axis=0), d_gain, d_shift]),
        ],
        axis=0,
    )
    return (d_rows, d_up, d_down, small_rows)


def row_select(token_mask, capacity):
    flat_mask = token_mask.reshape(1, -1)
    row_total = flat_mask.shape[1]
    before = (
        lax.broadcasted_iota(jnp.int32, (row_total, row_total), 0)
        < lax.broadcasted_iota(jnp.int32, (row_total, row_total), 1)
    ).astype(jnp.bfloat16)
    rank = forward_product(flat_mask.astype(jnp.bfloat16), before).astype(jnp.int32)
    slots = lax.broadcasted_iota(jnp.int32, (capacity, row_total), 0)
    return ((slots == rank) & (flat_mask == 1)).astype(jnp.bfloat16)


def split_low(wide, parts):
    pieces = []
    left = wide
    for _ in range(parts - 1):
        piece = lax.reduce_precision(left, 8, 7)
        pieces.append(piece.astype(jnp.bfloat16))
        left = left - piece
    pieces.append(left.astype(jnp.bfloat16))
    return jnp.concatenate(pieces, axis=1)


def join_low(joined, parts):
    width = joined.shape[1] // parts
    total = joined[:, :width]
    for number in range(1, parts):
        total = total + joined[:, number * width : (number + 1) * width]
    return total


def adam_update(
    master, first_moment, second_moment, gradient, clip_scale, step_value, decay_rate, rate_value
):
    clipped = gradient * clip_scale
    first_new = BETA_FIRST * first_moment + (1.0 - BETA_FIRST) * clipped
    second_new = BETA_SECOND * second_moment + (1.0 - BETA_SECOND) * clipped * clipped
    first_hat = first_new / (1.0 - jnp.power(BETA_FIRST, step_value))
    second_hat = second_new / (1.0 - jnp.power(BETA_SECOND, step_value))
    master_new = master - rate_value * (
        first_hat / (jnp.sqrt(second_hat) + ADAM_EPS) + decay_rate * master
    )
    return (master_new, first_new, second_new, master_new.astype(jnp.bfloat16))


def gather_rows(rows, core):
    half = rows.shape[0] // 2
    mine = lax.dynamic_slice_in_dim(rows, core * half, half, 0)
    return lax.all_gather(mine, ("bal", "dp"), axis=0, tiled=True)


def scatter_rows(grads):
    rows = with_layout_constraint(grads.astype(jnp.bfloat16), Layout(major_to_minor=(0, 1)))
    return lax.psum_scatter(rows, ("bal", "dp"), scatter_dimension=0, tiled=True)


def pair_rows(mine, core):
    other = lax.ppermute(mine, "dp", [(0, 1), (1, 0)])
    return jnp.where(
        core == 0,
        jnp.concatenate([mine, other], axis=0),
        jnp.concatenate([other, mine], axis=0),
    )


def sum_all(value):
    total = value.reshape(1, 1)
    total = total + lax.ppermute(total, "dp", [(0, 1), (1, 0)])
    peers = lax.axis_size("bal")
    step = 1
    while step < peers:
        moved = []
        for turn in range(1, 4):
            pairs = [
                (at, (at // (4 * step)) * 4 * step + (at + turn * step) % (4 * step))
                for at in range(peers)
            ]
            moved.append(lax.ppermute(total, "bal", pairs))
        place = (lax.axis_index("bal") // step) % 4
        ring = jnp.concatenate([total] + moved, axis=1)
        order = (place - jnp.arange(4)) % 4
        total = jnp.sum(ring[:, order], axis=1, keepdims=True)
        step *= 4
    return total[0, 0]


def attn_parts(joined):
    width = joined.shape[0]
    return [joined[:, number * width : (number + 1) * width] for number in range(4)]


def per_device(
    tokens,
    cotangent,
    seq_lengths,
    token_mask,
    step_count,
    attn_master,
    attn_first,
    attn_second,
    up_master,
    up_first,
    up_second,
    down_master,
    down_first,
    down_second,
    small_master,
    small_first,
    small_second,
):
    core = lax.axis_index("dp")
    attn_rows = attn_master.astype(jnp.bfloat16).transpose(0, 2, 1, 3)
    attn_rows = attn_rows.reshape(2, attn_rows.shape[1], -1)
    small_cols = small_master.astype(jnp.bfloat16).reshape(24, -1).T
    small_cols = jnp.pad(small_cols, ((0, 0), (0, 104)))
    up_rows = up_master.astype(jnp.bfloat16)
    down_rows = down_master.astype(jnp.bfloat16)
    first_piece = gather_rows(jnp.concatenate([attn_rows[0], small_cols], axis=1), core)
    wide = attn_rows.shape[2]
    up_low, down_low = [None, None], [None, None]
    up_low[0] = gather_rows(up_rows[0], core)
    down_low[0] = gather_rows(down_rows[0], core)
    attn_low = [attn_parts(first_piece[:, :wide]), attn_parts(gather_rows(attn_rows[1], core))]
    up_low[1] = gather_rows(up_rows[1], core)
    down_low[1] = gather_rows(down_rows[1], core)
    small_low = first_piece[:, wide : wide + 24].T.reshape(2, 12, -1)
    small_vals = small_low.astype(jnp.float32)
    seq_count, length, model_width = tokens.shape
    rows_total = seq_count * length
    hidden = tokens.astype(jnp.float32)
    attended_one, kept_attend_one = attend_forward(hidden, attn_low[0], small_vals[0], seq_lengths)
    layer_one, kept_feed_one = feed_forward(attended_one, up_low[0], down_low[0], small_vals[0])
    attended_two, kept_attend_two = attend_forward(
        layer_one.reshape(seq_count, length, model_width), attn_low[1], small_vals[1], seq_lengths
    )
    cot_flat = cotangent.reshape(rows_total, model_width).astype(jnp.float32)
    select_rows = row_select(token_mask, MCAP)
    rows_in = join_low(forward_product(select_rows, split_low(attended_two, 3)), 3)
    d_rows_out = forward_product(select_rows, cotangent.reshape(rows_total, model_width))
    out_rows, kept_feed_two = feed_forward(rows_in, up_low[1], down_low[1], small_vals[1])
    d_in_rows, d_up_two, d_down_two, feed_small_two = feed_backward(
        d_rows_out, kept_feed_two, up_low[1], down_low[1], small_vals[1]
    )
    flat_mask = token_mask.reshape(-1, 1) == 1
    output_flat = jnp.where(
        flat_mask,
        weight_grad(select_rows, out_rows.astype(jnp.bfloat16)),
        attended_two,
    )
    d_attended_two = jnp.where(
        flat_mask, join_low(weight_grad(select_rows, split_low(d_in_rows, 2)), 2), cot_flat
    )
    d_layer_one, d_attn_two, attn_small_two = attend_backward(
        d_attended_two, kept_attend_two, attn_low[1], small_vals[1], seq_lengths, seq_count, length
    )
    grads_two = (
        d_attn_two,
        d_up_two,
        d_down_two,
        jnp.concatenate([attn_small_two, feed_small_two], axis=0),
    )
    d_attended_one, d_up_one, d_down_one, feed_small_one = feed_backward(
        d_layer_one, kept_feed_one, up_low[0], down_low[0], small_vals[0]
    )
    d_tokens, d_attn_one, attn_small_one = attend_backward(
        d_attended_one, kept_attend_one, attn_low[0], small_vals[0], seq_lengths, seq_count, length
    )
    grads_one = (
        d_attn_one,
        d_up_one,
        d_down_one,
        jnp.concatenate([attn_small_one, feed_small_one], axis=0),
    )
    small_grads = jnp.stack([grads_one[3], grads_two[3]]).reshape(24, -1).T
    small_grads = jnp.pad(small_grads, ((0, 0), (0, 104)))
    owned = {}
    owned["up1"] = scatter_rows(d_up_two)
    owned["down1"] = scatter_rows(d_down_two)
    owned["attn1"] = scatter_rows(d_attn_two)
    owned["down0"] = scatter_rows(d_down_one)
    owned["up0"] = scatter_rows(d_up_one)
    owned["attn0"] = scatter_rows(jnp.concatenate([d_attn_one, small_grads], axis=1))
    partial_squares = sum(jnp.sum(jnp.square(owned[name].astype(jnp.float32))) for name in owned)
    square_total = sum_all(partial_squares)
    both = {name: pair_rows(owned[name], core).astype(jnp.float32) for name in owned}
    attn_both = jnp.stack([both["attn0"][:, :wide], both["attn1"]])
    reduced = (
        attn_both.reshape(2, -1, 4, model_width).transpose(0, 2, 1, 3),
        jnp.stack([both["up0"], both["up1"]]),
        jnp.stack([both["down0"], both["down1"]]),
        both["attn0"][:, wide : wide + 24].T.reshape(2, 12, -1),
    )
    grad_norm = jnp.sqrt(square_total).reshape(1)
    clip_scale = jnp.minimum(1.0, CLIP_NORM / (grad_norm[0] + 1e-06))
    step_value = step_count[0].astype(jnp.float32)
    attn_new = adam_update(
        attn_master,
        attn_first,
        attn_second,
        reduced[0],
        clip_scale,
        step_value,
        WEIGHT_DECAY,
        LEARN_RATE,
    )
    up_new = adam_update(
        up_master, up_first, up_second, reduced[1], clip_scale, step_value, WEIGHT_DECAY, LEARN_RATE
    )
    down_new = adam_update(
        down_master,
        down_first,
        down_second,
        reduced[2],
        clip_scale,
        step_value,
        WEIGHT_DECAY,
        LEARN_RATE,
    )
    small_new = adam_update(
        small_master, small_first, small_second, reduced[3], clip_scale, step_value, 0.0, SMALL_RATE
    )
    output = output_flat.reshape(seq_count, length, model_width).astype(jnp.bfloat16)
    input_grad = d_tokens.reshape(seq_count, length, model_width).astype(jnp.bfloat16)
    return (output, input_grad, grad_norm) + attn_new + up_new + down_new + small_new


def solution(mesh):
    return jax.shard_map(
        per_device,
        mesh=mesh,
        in_specs=(
            P(("dp", "bal"), None, None),
            P(("dp", "bal"), None, None),
            P(("dp", "bal")),
            P(("dp", "bal"), None),
            P(),
            P(None, None, "bal", None),
            P(None, None, "bal", None),
            P(None, None, "bal", None),
            P(None, "bal", None),
            P(None, "bal", None),
            P(None, "bal", None),
            P(None, "bal", None),
            P(None, "bal", None),
            P(None, "bal", None),
            P(None, None, "bal"),
            P(None, None, "bal"),
            P(None, None, "bal"),
        ),
        out_specs=(
            P(("dp", "bal"), None, None),
            P(("dp", "bal"), None, None),
            P(),
            P(None, None, "bal", None),
            P(None, None, "bal", None),
            P(None, None, "bal", None),
            P(None, None, "bal", None),
            P(None, "bal", None),
            P(None, "bal", None),
            P(None, "bal", None),
            P(None, "bal", None),
            P(None, "bal", None),
            P(None, "bal", None),
            P(None, "bal", None),
            P(None, "bal", None),
            P(None, None, "bal"),
            P(None, None, "bal"),
            P(None, None, "bal"),
            P(None, None, "bal"),
        ),
        check_vma=False,
    )
```

```python
import math

import jax
import jax.numpy as jnp
import numpy as np
from jax import lax
from jax.experimental import pallas as pl
from jax.experimental.pallas import tpu as pltpu
from jax.sharding import PartitionSpec as P

HEADS = 12
HEAD_DIM = 64
MCAP = 384
LANES = 128
QUERY_BLOCK = 256


LN_EPS = 1e-06
NEG_FILL = -1000000000.0
CLIP_NORM = 1.0
LEARN_RATE = 0.05
SMALL_RATE = 0.25
BETA_FIRST = 0.9
BETA_SECOND = 0.999
ADAM_EPS = 1e-08
WEIGHT_DECAY = 0.01


def forward_product(left_side, right_side):
    return jnp.dot(left_side, right_side, preferred_element_type=jnp.float32)


def weight_grad(left_side, right_side):
    return lax.dot_general(
        left_side, right_side, (((0,), (0,)), ((), ())), preferred_element_type=jnp.float32
    )


def back_product(left_side, right_side):
    return lax.dot_general(
        left_side, right_side, (((1,), (1,)), ((), ())), preferred_element_type=jnp.float32
    )


def norm_forward(residual, norm_gain, norm_shift):
    centered = residual - jnp.mean(residual, axis=-1, keepdims=True)
    variance = jnp.mean(centered * centered, axis=-1, keepdims=True)
    inv_std = lax.rsqrt(variance + LN_EPS)
    normal_part = centered * inv_std
    return (normal_part * norm_gain + norm_shift, normal_part, inv_std)


def norm_backward(d_out, normal_part, inv_std, norm_gain):
    d_normal = d_out * norm_gain
    d_resid = inv_std * (
        d_normal
        - jnp.mean(d_normal, axis=-1, keepdims=True)
        - normal_part * jnp.mean(d_normal * normal_part, axis=-1, keepdims=True)
    )
    return (d_resid, jnp.sum(d_out * normal_part, axis=0), jnp.sum(d_out, axis=0))


def gelu_slope(pre_act):
    return (
        0.5 * (1.0 + lax.erf(pre_act * 0.7071067811865476))
        + pre_act * jnp.exp(-0.5 * pre_act * pre_act) * 0.3989422804014327
    )


def key_side(keys, bias, lane, half):
    own = (lane < HEAD_DIM) if half == 0 else (lane >= HEAD_DIM)
    spare = HEAD_DIM if half == 0 else 0
    return jnp.where(own, keys, jnp.where(lane == spare, bias, 0.0)).astype(jnp.bfloat16)


def query_side(queries, lane, half):
    own = (lane < HEAD_DIM) if half == 0 else (lane >= HEAD_DIM)
    spare = HEAD_DIM if half == 0 else 0
    return jnp.where(own, queries, jnp.where(lane == spare, 1.0, 0.0)).astype(jnp.bfloat16)


def one_head(rows, lane, half):
    own = (lane < HEAD_DIM) if half == 0 else (lane >= HEAD_DIM)
    return jnp.where(own, rows, 0.0).astype(jnp.bfloat16)


def pair_of(ref, part, pair):
    width = ref.shape[1] // 3
    at = pl.multiple_of(part * width + pair * LANES, LANES)
    return ref[:, pl.ds(at, LANES)].astype(jnp.float32)


def attend_kernel(len_ref, qkv_lo, qkv_hi, mixed_ref, lse_ref, ot_ref):
    rows = mixed_ref.shape[0]
    width = qkv_lo.shape[1] // 3
    pairs = width // LANES
    real = len_ref[pl.program_id(0)]
    lane = lax.broadcasted_iota(jnp.int32, (rows, LANES), 1)
    place_key = lax.broadcasted_iota(jnp.int32, (rows, LANES), 0)
    bias = jnp.where(place_key < real, 0.0, NEG_FILL)
    for side, qkv_ref in enumerate((qkv_lo, qkv_hi)):

        def one_pair(pair, carry, side=side, qkv_ref=qkv_ref):
            queries = pair_of(qkv_ref, 0, pair) * (1.0 / math.sqrt(HEAD_DIM))
            keys = pair_of(qkv_ref, 1, pair)
            values_t = pair_of(qkv_ref, 2, pair).T.astype(jnp.bfloat16)
            for half in range(2):
                keys_one = key_side(keys, bias, lane, half)
                queries_one = query_side(queries, lane, half)
                lanes = slice(half * HEAD_DIM, (half + 1) * HEAD_DIM)
                head = side * 2 * pairs + 2 * pair + half
                for at in range(0, rows, QUERY_BLOCK):
                    cols = slice(at, at + QUERY_BLOCK)
                    scores = back_product(keys_one, queries_one[cols])
                    top = jnp.max(scores, axis=0, keepdims=True)
                    exps = jnp.exp(scores - top)
                    total = jnp.sum(exps, axis=0, keepdims=True)
                    mixed_t = forward_product(values_t[lanes], exps.astype(jnp.bfloat16))
                    ot_ref[lanes, cols] = mixed_t / total
                    lse_ref[pl.ds(head, 1), cols] = top + jnp.log(total)
            at = pl.multiple_of(side * width + pair * LANES, LANES)
            mixed_ref[:, pl.ds(at, LANES)] = ot_ref[...].T.astype(jnp.bfloat16)
            return carry

        lax.fori_loop(0, pairs, one_pair, 0)


def attend_core(qkv_lo, qkv_hi, seq_lengths):
    total, wide = qkv_lo.shape
    seqs = seq_lengths.shape[0]
    rows, width = total // seqs, 2 * wide // 3
    heads = width // HEAD_DIM
    lse_rows = -(-heads // 8) * 8
    side = pl.BlockSpec((rows, wide), lambda seq, lens: (seq, 0))
    return pl.pallas_call(
        attend_kernel,
        out_shape=(
            jax.ShapeDtypeStruct((total, width), jnp.bfloat16),
            jax.ShapeDtypeStruct((seqs, lse_rows, rows), jnp.float32),
        ),
        grid_spec=pltpu.PrefetchScalarGridSpec(
            num_scalar_prefetch=1,
            grid=(seqs,),
            in_specs=[side, side],
            out_specs=[
                pl.BlockSpec((rows, width), lambda seq, lens: (seq, 0)),
                pl.BlockSpec((None, lse_rows, rows), lambda seq, lens: (seq, 0, 0)),
            ],
            scratch_shapes=[pltpu.VMEM((LANES, rows), jnp.float32)],
        ),
        compiler_params=pltpu.CompilerParams(vmem_limit_bytes=32 << 20),
        cost_estimate=pl.CostEstimate(
            flops=16 * total * rows * width,
            bytes_accessed=8 * total * width,
            transcendentals=total * rows * heads,
        ),
        name="attend",
    )(seq_lengths, qkv_lo, qkv_hi)


def attend_back_kernel(
    len_ref, qkv_lo, qkv_hi, d_mixed_ref, lse_ref, d_qkv_ref, dqt_ref, dk_ref, dv_ref
):
    rows = d_mixed_ref.shape[0]
    width = qkv_lo.shape[1] // 3
    pairs = width // LANES
    scale = 1.0 / math.sqrt(HEAD_DIM)
    real = len_ref[pl.program_id(0)]
    lane = lax.broadcasted_iota(jnp.int32, (rows, LANES), 1)
    place_key = lax.broadcasted_iota(jnp.int32, (rows, LANES), 0)
    bias = jnp.where(place_key < real, 0.0, NEG_FILL)
    for side, qkv_ref in enumerate((qkv_lo, qkv_hi)):

        def one_pair(pair, carry, side=side, qkv_ref=qkv_ref):
            queries = pair_of(qkv_ref, 0, pair) * scale
            keys = pair_of(qkv_ref, 1, pair)
            values = pair_of(qkv_ref, 2, pair)
            at_mixed = pl.multiple_of(side * width + pair * LANES, LANES)
            d_mixed = d_mixed_ref[:, pl.ds(at_mixed, LANES)].astype(jnp.float32)
            keys_t = keys.T.astype(jnp.bfloat16)
            started = False
            for half in range(2):
                keys_one = key_side(keys, bias, lane, half)
                queries_one = query_side(queries, lane, half)
                values_only = one_head(values, lane, half)
                queries_only = one_head(queries, lane, half)
                d_mixed_only = one_head(d_mixed, lane, half)
                lanes = slice(half * HEAD_DIM, (half + 1) * HEAD_DIM)
                head = side * 2 * pairs + 2 * pair + half
                for at in range(0, rows, QUERY_BLOCK):
                    cols = slice(at, at + QUERY_BLOCK)
                    scores = back_product(keys_one, queries_one[cols])
                    d_probs = back_product(values_only, d_mixed_only[cols])
                    probs = jnp.exp(scores - lse_ref[pl.ds(head, 1), cols])
                    row_part = jnp.sum(probs * d_probs, axis=0, keepdims=True)
                    d_scores = (probs * (d_probs - row_part)).astype(jnp.bfloat16)
                    d_values = forward_product(probs.astype(jnp.bfloat16), d_mixed_only[cols])
                    d_keys = forward_product(d_scores, queries_only[cols])
                    if started:
                        dv_ref[...] += d_values
                        dk_ref[...] += d_keys
                    else:
                        dv_ref[...] = d_values
                        dk_ref[...] = d_keys
                        started = True
                    dqt_ref[lanes, cols] = forward_product(keys_t[lanes], d_scores)
            outs = ((dqt_ref[...].T * scale), dk_ref[...], dv_ref[...])
            for part, value in enumerate(outs):
                at = pl.multiple_of(part * width + pair * LANES, LANES)
                d_qkv_ref[side, :, pl.ds(at, LANES)] = value.astype(jnp.bfloat16)
            return carry

        lax.fori_loop(0, pairs, one_pair, 0)


def attend_core_back(qkv_lo, qkv_hi, d_mixed, lse, seq_lengths):
    total, wide = qkv_lo.shape
    seqs = seq_lengths.shape[0]
    rows, width = total // seqs, 2 * wide // 3
    heads = width // HEAD_DIM
    side = pl.BlockSpec((rows, wide), lambda seq, lens: (seq, 0))
    return pl.pallas_call(
        attend_back_kernel,
        out_shape=jax.ShapeDtypeStruct((2, total, wide), jnp.bfloat16),
        grid_spec=pltpu.PrefetchScalarGridSpec(
            num_scalar_prefetch=1,
            grid=(seqs,),
            in_specs=[
                side,
                side,
                pl.BlockSpec((rows, width), lambda seq, lens: (seq, 0)),
                pl.BlockSpec((None, lse.shape[1], rows), lambda seq, lens: (seq, 0, 0)),
            ],
            out_specs=pl.BlockSpec((2, rows, wide), lambda seq, lens: (0, seq, 0)),
            scratch_shapes=[
                pltpu.VMEM((LANES, rows), jnp.float32),
                pltpu.VMEM((rows, LANES), jnp.float32),
                pltpu.VMEM((rows, LANES), jnp.float32),
            ],
        ),
        compiler_params=pltpu.CompilerParams(vmem_limit_bytes=40 << 20),
        cost_estimate=pl.CostEstimate(
            flops=40 * total * rows * width,
            bytes_accessed=14 * total * width,
            transcendentals=total * rows * heads,
        ),
        name="attend_back",
    )(seq_lengths, qkv_lo, qkv_hi, d_mixed, lse)


def half_of(rows, side):
    width = rows.shape[1] // 2
    return lax.dynamic_slice_in_dim(rows, side * width, width, 1)


def attend_forward(flat_rows, flat_low, attn_layer, small_layer, seq_lengths):
    model_width = flat_rows.shape[1]
    third = model_width // 2
    qkv = []
    for side in range(2):
        cols = slice(side * third, (side + 1) * third)
        bias = jnp.concatenate(
            [small_layer[0, cols], jnp.zeros((third,), jnp.float32), small_layer[1, cols]]
        )
        part = forward_product(flat_low, attn_layer[side, :, : 3 * third]) + bias
        qkv.append(part.astype(jnp.bfloat16))
    mixed_heads, lse = attend_core(qkv[0], qkv[1], seq_lengths)
    branch = jnp.concatenate(
        [
            forward_product(mixed_heads, attn_layer[side, :, 3 * third : 4 * third])
            for side in range(2)
        ],
        axis=1,
    )
    normed, normal_part, inv_std = norm_forward(
        flat_rows + branch + small_layer[2], small_layer[3], small_layer[4]
    )
    return (normed, (flat_low, qkv, lse, mixed_heads, normal_part, inv_std))


def attend_backward(d_normed, kept_state, attn_layer, small_layer, seq_lengths, core):
    flat_low, qkv, lse, mixed_heads, normal_part, inv_std = kept_state
    row_count, model_width = flat_low.shape
    third = model_width // 2
    d_resid, d_gain, d_shift = norm_backward(d_normed, normal_part, inv_std, small_layer[3])
    d_branch = d_resid.astype(jnp.bfloat16)
    d_out_bias = jnp.sum(d_branch.astype(jnp.float32), axis=0)
    d_mixed = sum(
        back_product(
            d_branch[:, side * third : (side + 1) * third],
            attn_layer[side, :, 3 * third : 4 * third],
        )
        for side in range(2)
    ).astype(jnp.bfloat16)
    d_qkv = attend_core_back(qkv[0], qkv[1], d_mixed, lse, seq_lengths)

    def weights_of(side):
        return jnp.concatenate(
            [
                weight_grad(flat_low, lax.dynamic_index_in_dim(d_qkv, side, 0, False)),
                weight_grad(mixed_heads, half_of(d_branch, side)),
            ],
            axis=1,
        )

    far = weights_of(1 - core)
    own = weights_of(core)
    d_hidden = d_resid + sum(
        back_product(d_qkv[side], attn_layer[side, :, : 3 * third]) for side in range(2)
    )
    sums = jnp.sum(d_qkv.astype(jnp.float32), axis=1)
    small_rows = jnp.stack(
        [
            sums[:, :third].reshape(model_width),
            sums[:, 2 * third :].reshape(model_width),
            d_out_bias,
            d_gain,
            d_shift,
        ]
    )
    return (d_hidden, own, far, small_rows)


def feed_forward(rows_in, up_layer, down_layer, small_layer):
    rows_low = rows_in.astype(jnp.bfloat16)
    pre_act = forward_product(rows_low, up_layer) + small_layer[5:9].reshape(-1)
    act_low = jax.nn.gelu(pre_act, approximate=False).astype(jnp.bfloat16)
    branch = forward_product(act_low, down_layer) + small_layer[9]
    normed, normal_part, inv_std = norm_forward(rows_in + branch, small_layer[10], small_layer[11])
    return (normed, (rows_low, pre_act, act_low, normal_part, inv_std))


def feed_backward(d_normed, kept_state, up_layer, down_layer, small_layer, core):
    rows_low, pre_act, act_low, normal_part, inv_std = kept_state
    d_resid, d_gain, d_shift = norm_backward(d_normed, normal_part, inv_std, small_layer[10])
    d_branch = d_resid.astype(jnp.bfloat16)
    d_down = [weight_grad(act_low, half_of(d_branch, side)) for side in (1 - core, core)]
    d_pre = (back_product(d_branch, down_layer) * gelu_slope(pre_act)).astype(jnp.bfloat16)
    d_up = [weight_grad(rows_low, half_of(d_pre, side)) for side in (1 - core, core)]
    d_rows = d_resid + back_product(d_pre, up_layer)
    model_width = d_resid.shape[1]
    small_rows = jnp.concatenate(
        [
            jnp.sum(d_pre.astype(jnp.float32), axis=0).reshape(4, model_width),
            jnp.stack([jnp.sum(d_branch.astype(jnp.float32), axis=0), d_gain, d_shift]),
        ],
        axis=0,
    )
    return (d_rows, d_up, d_down, small_rows)


def row_select(token_mask, capacity):
    flat_mask = token_mask.reshape(1, -1)
    row_total = flat_mask.shape[1]
    before = (
        lax.broadcasted_iota(jnp.int32, (row_total, row_total), 0)
        < lax.broadcasted_iota(jnp.int32, (row_total, row_total), 1)
    ).astype(jnp.bfloat16)
    rank = forward_product(flat_mask.astype(jnp.bfloat16), before).astype(jnp.int32)
    slots = lax.broadcasted_iota(jnp.int32, (capacity, row_total), 0)
    return ((slots == rank) & (flat_mask == 1)).astype(jnp.bfloat16)


def split_low(wide, parts):
    pieces = []
    left = wide
    for _ in range(parts - 1):
        piece = lax.reduce_precision(left, 8, 7)
        pieces.append(piece.astype(jnp.bfloat16))
        left = left - piece
    pieces.append(left.astype(jnp.bfloat16))
    return jnp.concatenate(pieces, axis=1)


def join_low(joined, parts):
    width = joined.shape[1] // parts
    total = joined[:, :width]
    for number in range(1, parts):
        total = total + joined[:, number * width : (number + 1) * width]
    return total


def adam_update(
    master, first_moment, second_moment, gradient, clip_scale, step_value, decay_rate, rate_value
):
    clipped = gradient * clip_scale
    first_new = BETA_FIRST * first_moment + (1.0 - BETA_FIRST) * clipped
    second_new = BETA_SECOND * second_moment + (1.0 - BETA_SECOND) * clipped * clipped
    first_hat = first_new / (1.0 - jnp.power(BETA_FIRST, step_value))
    second_hat = second_new / (1.0 - jnp.power(BETA_SECOND, step_value))
    master_new = master - rate_value * (
        first_hat / (jnp.sqrt(second_hat) + ADAM_EPS) + decay_rate * master
    )
    return (master_new, first_new, second_new, master_new.astype(jnp.bfloat16))


def routes(peers):
    bits = peers.bit_length() - 1
    deep = min(2, bits)
    rest = bits - deep
    x_bits = [1 << at for at in range(rest - rest // 2)]
    y_bits = [1 << at for at in range(rest - rest // 2, rest)]
    z_bits = [1 << at for at in range(rest, bits)]
    first = z_bits + y_bits + x_bits
    second = z_bits + x_bits + y_bits
    return (first, second if len(x_bits) == len(y_bits) else first)


def shift(value, step, peers):
    pairs = []
    for core, path in enumerate(routes(peers)):
        pairs += [(core * peers + at, core * peers + (at ^ path[step])) for at in range(peers)]
    return lax.ppermute(value, ("dp", "bal"), pairs)


def swap(value):
    return lax.ppermute(value, "dp", [(0, 1), (1, 0)])


def place_table(peers, core):
    masks = [
        [sum(bit for at, bit in enumerate(path) if spot >> at & 1) for spot in range(peers)]
        for path in routes(peers)
    ]
    masks = jnp.asarray(np.array(masks, np.int32))
    mine = lax.axis_index("bal")
    own = jnp.where(core == 0, masks[0], masks[1])
    far = jnp.where(core == 0, masks[1], masks[0])
    return jnp.concatenate([mine ^ own, mine ^ far, core.reshape(1).astype(jnp.int32)])


def place_kernel(spots, own_lo, own_hi, far_lo, far_hi, out, held, in_sems, out_sems):
    half, rows, width = own_lo.shape
    core = spots[4 * half]
    loads = []
    for number, part in enumerate((own_lo, own_hi, far_lo, far_hi)):
        loads.append(pltpu.make_async_copy(part, held.at[number], in_sems.at[number]))
        loads[-1].start()
    stores = []
    for number, load in enumerate(loads):
        load.wait()
        side = core if number < 2 else 1 - core
        for at in range(half):
            spot = spots[number * half + at]
            if len(out.shape) == 4:
                target = out.at[side, spot]
            else:
                target = out.at[spot, :, pl.ds(pl.multiple_of(side * width, LANES), width)]
            stores.append(
                pltpu.make_async_copy(held.at[number, at], target, out_sems.at[number, at])
            )
            stores[-1].start()
    for store in stores:
        store.wait()


def place(spots, parts, stacked):
    half, rows, width = parts[0].shape
    peers = 2 * half
    shape = (2, peers, rows, width) if stacked else (peers, rows, 2 * width)
    return pl.pallas_call(
        place_kernel,
        out_shape=jax.ShapeDtypeStruct(shape, parts[0].dtype),
        grid_spec=pltpu.PrefetchScalarGridSpec(
            num_scalar_prefetch=1,
            grid=(),
            in_specs=[pl.BlockSpec(memory_space=pl.ANY)] * 4,
            out_specs=pl.BlockSpec(memory_space=pl.ANY),
            scratch_shapes=[
                pltpu.VMEM((4, half, rows, width), parts[0].dtype),
                pltpu.SemaphoreType.DMA((4,)),
                pltpu.SemaphoreType.DMA((4, half)),
            ],
        ),
        compiler_params=pltpu.CompilerParams(vmem_limit_bytes=16 << 20),
        cost_estimate=pl.CostEstimate(
            flops=0, bytes_accessed=8 * peers * rows * width, transcendentals=0
        ),
        name="place",
    )(spots, *parts)


def gather(mine, spots, peers, stacked):
    buffer = mine[None]
    steps = peers.bit_length() - 1
    for step in range(steps - 1):
        buffer = jnp.concatenate([buffer, shift(buffer, step, peers)], axis=0)
    moved = shift(buffer, steps - 1, peers)
    whole = place(spots, (buffer, moved, swap(buffer), swap(moved)), stacked)
    if stacked:
        return whole.reshape(2, -1, whole.shape[-1])
    return whole.reshape(-1, whole.shape[-1])


def fold_kernel(spots, own_a, far_a, own_b, far_b, keep, send):
    keep[...] = (own_a[...].astype(jnp.float32) + far_a[...].astype(jnp.float32)).astype(keep.dtype)
    send[...] = (own_b[...].astype(jnp.float32) + far_b[...].astype(jnp.float32)).astype(send.dtype)


def fold(spots, own, far):
    peers, rows, width = own.shape
    half = peers // 2
    near = pl.BlockSpec((1, rows, width), lambda at, spots: (spots[at], 0, 0))
    apart = pl.BlockSpec((1, rows, width), lambda at, spots: (spots[at + half], 0, 0))
    there = pl.BlockSpec((1, rows, width), lambda at, spots: (at, 0, 0))
    shape = jax.ShapeDtypeStruct((half, rows, width), own.dtype)
    return pl.pallas_call(
        fold_kernel,
        out_shape=(shape, shape),
        grid_spec=pltpu.PrefetchScalarGridSpec(
            num_scalar_prefetch=1,
            grid=(half,),
            in_specs=[near, near, apart, apart],
            out_specs=[there, there],
        ),
        cost_estimate=pl.CostEstimate(
            flops=peers * rows * width,
            bytes_accessed=6 * peers * rows * width,
            transcendentals=0,
        ),
        name="fold",
    )(spots, own, far, own, far)


def scatter(far, own, spots, peers):
    def blocks(grads):
        return grads.astype(jnp.bfloat16).reshape(peers, -1, grads.shape[1])

    keep, send = fold(spots, blocks(own), swap(blocks(far)))
    for step in range(peers.bit_length() - 2, -1, -1):
        total = keep.astype(jnp.float32) + shift(send, step, peers).astype(jnp.float32)
        half = total.shape[0] // 2
        if step == 0:
            return total[0].astype(jnp.bfloat16)
        keep = total[:half].astype(jnp.bfloat16)
        send = total[half:].astype(jnp.bfloat16)


def both_sides(own, core):
    other = swap(own)
    return (jnp.where(core == 0, own, other), jnp.where(core == 0, other, own))


def sum_all(value, peers):
    total = value.reshape(1, 1)
    total = total + swap(total)
    step = 1
    while step < peers:
        span = min(4, peers // step)
        moved = [
            lax.ppermute(total, "bal", [(at, at ^ (turn * step)) for at in range(peers)])
            for turn in range(1, span)
        ]
        if span == 4:
            total = (total + moved[0]) + (moved[1] + moved[2])
        else:
            total = total + moved[0]
        step *= span
    return total[0, 0]


def per_device(
    tokens,
    cotangent,
    seq_lengths,
    token_mask,
    step_count,
    attn_master,
    attn_first,
    attn_second,
    up_master,
    up_first,
    up_second,
    down_master,
    down_first,
    down_second,
    small_master,
    small_first,
    small_second,
):
    core = lax.axis_index("dp")
    peers = lax.axis_size("bal")
    seq_count, length, model_width = tokens.shape
    rows_total = seq_count * length
    spots = place_table(peers, core)
    shard = attn_master.shape[2]
    attn_half = lax.dynamic_slice_in_dim(attn_master, core * (model_width // 2), model_width // 2, 3)
    attn_half = attn_half.astype(jnp.bfloat16).transpose(0, 2, 1, 3).reshape(2, shard, -1)
    small_half = lax.dynamic_slice_in_dim(small_master.reshape(24, shard), core * 12, 12, 0)
    small_half = jnp.pad(small_half.astype(jnp.bfloat16).T, ((0, 0), (0, LANES - 12)))
    wide = attn_half.shape[2]
    first_piece = gather(
        jnp.concatenate([attn_half[0], small_half], axis=1), spots, peers, True
    )
    up_low, down_low = [None, None], [None, None]
    up_low[0] = gather(half_of(up_master[0], core).astype(jnp.bfloat16), spots, peers, False)
    down_low[0] = gather(half_of(down_master[0], core).astype(jnp.bfloat16), spots, peers, False)
    attn_low = [first_piece[:, :, :wide], gather(attn_half[1], spots, peers, True)]
    up_low[1] = gather(half_of(up_master[1], core).astype(jnp.bfloat16), spots, peers, False)
    down_low[1] = gather(half_of(down_master[1], core).astype(jnp.bfloat16), spots, peers, False)
    small_vals = first_piece[:, :, wide : wide + 12].transpose(0, 2, 1).astype(jnp.float32)
    flat_low = tokens.reshape(rows_total, model_width)
    attended_one, kept_attend_one = attend_forward(
        flat_low.astype(jnp.float32), flat_low, attn_low[0], small_vals[0], seq_lengths
    )
    layer_one, kept_feed_one = feed_forward(attended_one, up_low[0], down_low[0], small_vals[0])
    attended_two, kept_attend_two = attend_forward(
        layer_one, layer_one.astype(jnp.bfloat16), attn_low[1], small_vals[1], seq_lengths
    )
    cot_flat = cotangent.reshape(rows_total, model_width).astype(jnp.float32)
    select_rows = row_select(token_mask, MCAP)
    rows_in = join_low(forward_product(select_rows, split_low(attended_two, 3)), 3)
    d_rows_out = forward_product(select_rows, cotangent.reshape(rows_total, model_width))
    out_rows, kept_feed_two = feed_forward(rows_in, up_low[1], down_low[1], small_vals[1])
    d_in_rows, d_up_two, d_down_two, feed_small_two = feed_backward(
        d_rows_out, kept_feed_two, up_low[1], down_low[1], small_vals[1], core
    )
    flat_mask = token_mask.reshape(-1, 1) == 1
    output_flat = jnp.where(
        flat_mask,
        weight_grad(select_rows, out_rows.astype(jnp.bfloat16)),
        attended_two,
    )
    d_attended_two = jnp.where(
        flat_mask, join_low(weight_grad(select_rows, split_low(d_in_rows, 2)), 2), cot_flat
    )
    owned = {}
    owned["up1"] = scatter(*d_up_two, spots, peers)
    owned["down1"] = scatter(*d_down_two, spots, peers)
    d_layer_one, own_attn, far_attn, attn_small_two = attend_backward(
        d_attended_two, kept_attend_two, attn_low[1], small_vals[1], seq_lengths, core
    )
    owned["attn1"] = scatter(far_attn, own_attn, spots, peers)
    d_attended_one, d_up_one, d_down_one, feed_small_one = feed_backward(
        d_layer_one, kept_feed_one, up_low[0], down_low[0], small_vals[0], core
    )
    owned["down0"] = scatter(*d_down_one, spots, peers)
    owned["up0"] = scatter(*d_up_one, spots, peers)
    d_tokens, own_attn, far_attn, attn_small_one = attend_backward(
        d_attended_one, kept_attend_one, attn_low[0], small_vals[0], seq_lengths, core
    )
    small_grads = jnp.stack(
        [
            jnp.concatenate([attn_small_one, feed_small_one], axis=0),
            jnp.concatenate([attn_small_two, feed_small_two], axis=0),
        ]
    )

    def with_small(grads, side):
        picked = lax.dynamic_index_in_dim(small_grads, side, 0, False).T
        picked = jnp.pad(picked, ((0, 0), (0, LANES - 12)))
        return jnp.concatenate([grads, picked], axis=1)

    owned["attn0"] = scatter(
        with_small(far_attn, 1 - core), with_small(own_attn, core), spots, peers
    )
    partial_squares = sum(jnp.sum(jnp.square(owned[name].astype(jnp.float32))) for name in owned)
    square_total = sum_all(partial_squares, peers)
    both = {name: both_sides(owned[name], core) for name in owned}

    def attn_rows(name):
        sides = jnp.stack([part[:, :wide] for part in both[name]])
        return sides.reshape(2, shard, 4, -1).transpose(2, 1, 0, 3).reshape(4, shard, model_width)

    def wide_rows(name):
        return jnp.concatenate(both[name], axis=1)

    reduced = (
        jnp.stack([attn_rows("attn0"), attn_rows("attn1")]).astype(jnp.float32),
        jnp.stack([wide_rows("up0"), wide_rows("up1")]).astype(jnp.float32),
        jnp.stack([wide_rows("down0"), wide_rows("down1")]).astype(jnp.float32),
        jnp.stack([part[:, wide : wide + 12].T for part in both["attn0"]]).astype(jnp.float32),
    )
    grad_norm = jnp.sqrt(square_total).reshape(1)
    clip_scale = jnp.minimum(1.0, CLIP_NORM / (grad_norm[0] + 1e-06))
    step_value = step_count[0].astype(jnp.float32)
    attn_new = adam_update(
        attn_master,
        attn_first,
        attn_second,
        reduced[0],
        clip_scale,
        step_value,
        WEIGHT_DECAY,
        LEARN_RATE,
    )
    up_new = adam_update(
        up_master, up_first, up_second, reduced[1], clip_scale, step_value, WEIGHT_DECAY, LEARN_RATE
    )
    down_new = adam_update(
        down_master,
        down_first,
        down_second,
        reduced[2],
        clip_scale,
        step_value,
        WEIGHT_DECAY,
        LEARN_RATE,
    )
    small_new = adam_update(
        small_master, small_first, small_second, reduced[3], clip_scale, step_value, 0.0, SMALL_RATE
    )
    output = output_flat.reshape(seq_count, length, model_width).astype(jnp.bfloat16)
    input_grad = d_tokens.reshape(seq_count, length, model_width).astype(jnp.bfloat16)
    return (output, input_grad, grad_norm) + attn_new + up_new + down_new + small_new


def solution(mesh):
    return jax.shard_map(
        per_device,
        mesh=mesh,
        in_specs=(
            P(("dp", "bal"), None, None),
            P(("dp", "bal"), None, None),
            P(("dp", "bal")),
            P(("dp", "bal"), None),
            P(),
            P(None, None, "bal", None),
            P(None, None, "bal", None),
            P(None, None, "bal", None),
            P(None, "bal", None),
            P(None, "bal", None),
            P(None, "bal", None),
            P(None, "bal", None),
            P(None, "bal", None),
            P(None, "bal", None),
            P(None, None, "bal"),
            P(None, None, "bal"),
            P(None, None, "bal"),
        ),
        out_specs=(
            P(("dp", "bal"), None, None),
            P(("dp", "bal"), None, None),
            P(),
            P(None, None, "bal", None),
            P(None, None, "bal", None),
            P(None, None, "bal", None),
            P(None, None, "bal", None),
            P(None, "bal", None),
            P(None, "bal", None),
            P(None, "bal", None),
            P(None, "bal", None),
            P(None, "bal", None),
            P(None, "bal", None),
            P(None, "bal", None),
            P(None, "bal", None),
            P(None, None, "bal"),
            P(None, None, "bal"),
            P(None, None, "bal"),
            P(None, None, "bal"),
        ),
        check_vma=False,
    )
```

```python
import functools
import math

import jax
import jax.numpy as jnp
import numpy as np
from jax import lax
from jax.experimental import pallas as pl
from jax.experimental.pallas import tpu as pltpu
from jax.sharding import PartitionSpec as P

HEADS = 12
HEAD_DIM = 64
MCAP = 384
LANES = 128
QUERY_BLOCK = 256
HIDDEN_BLOCK = 512


LN_EPS = 1e-06
NEG_FILL = -1000000000.0
CLIP_NORM = 1.0
LEARN_RATE = 0.05
SMALL_RATE = 0.25
BETA_FIRST = 0.9
BETA_SECOND = 0.999
ADAM_EPS = 1e-08
WEIGHT_DECAY = 0.01


def forward_product(left_side, right_side):
    return jnp.dot(left_side, right_side, preferred_element_type=jnp.float32)


def weight_grad(left_side, right_side):
    return lax.dot_general(
        left_side, right_side, (((0,), (0,)), ((), ())), preferred_element_type=jnp.float32
    )


def back_product(left_side, right_side):
    return lax.dot_general(
        left_side, right_side, (((1,), (1,)), ((), ())), preferred_element_type=jnp.float32
    )


def norm_forward(residual, norm_gain, norm_shift):
    centered = residual - jnp.mean(residual, axis=-1, keepdims=True)
    variance = jnp.mean(centered * centered, axis=-1, keepdims=True)
    inv_std = lax.rsqrt(variance + LN_EPS)
    normal_part = centered * inv_std
    return (normal_part * norm_gain + norm_shift, normal_part, inv_std)


def norm_backward(d_out, normal_part, inv_std, norm_gain):
    d_normal = d_out * norm_gain
    d_resid = inv_std * (
        d_normal
        - jnp.mean(d_normal, axis=-1, keepdims=True)
        - normal_part * jnp.mean(d_normal * normal_part, axis=-1, keepdims=True)
    )
    return (d_resid, jnp.sum(d_out * normal_part, axis=0), jnp.sum(d_out, axis=0))


def gelu_slope(pre_act):
    return (
        0.5 * (1.0 + lax.erf(pre_act * 0.7071067811865476))
        + pre_act * jnp.exp(-0.5 * pre_act * pre_act) * 0.3989422804014327
    )


def key_side(keys, bias, lane, half):
    own = (lane < HEAD_DIM) if half == 0 else (lane >= HEAD_DIM)
    spare = HEAD_DIM if half == 0 else 0
    return jnp.where(own, keys, jnp.where(lane == spare, bias, 0.0)).astype(jnp.bfloat16)


def query_side(queries, lane, half):
    own = (lane < HEAD_DIM) if half == 0 else (lane >= HEAD_DIM)
    spare = HEAD_DIM if half == 0 else 0
    return jnp.where(own, queries, jnp.where(lane == spare, 1.0, 0.0)).astype(jnp.bfloat16)


def one_head(rows, lane, half):
    own = (lane < HEAD_DIM) if half == 0 else (lane >= HEAD_DIM)
    return jnp.where(own, rows, 0.0).astype(jnp.bfloat16)


def pair_of(ref, part, pair):
    width = ref.shape[1] // 3
    at = pl.multiple_of(part * width + pair * LANES, LANES)
    return ref[:, pl.ds(at, LANES)].astype(jnp.float32)


def attend_kernel(seq, len_ref, qkv_lo, qkv_hi, mixed_ref, lse_ref, ot_ref):
    rows = mixed_ref.shape[0]
    width = qkv_lo.shape[1] // 3
    pairs = width // LANES
    real = len_ref[seq]
    lane = lax.broadcasted_iota(jnp.int32, (rows, LANES), 1)
    place_key = lax.broadcasted_iota(jnp.int32, (rows, LANES), 0)
    bias = jnp.where(place_key < real, 0.0, NEG_FILL)
    for side, qkv_ref in enumerate((qkv_lo, qkv_hi)):

        def one_pair(pair, carry, side=side, qkv_ref=qkv_ref):
            queries = pair_of(qkv_ref, 0, pair) * (1.0 / math.sqrt(HEAD_DIM))
            keys = pair_of(qkv_ref, 1, pair)
            values_t = pair_of(qkv_ref, 2, pair).T.astype(jnp.bfloat16)
            for half in range(2):
                keys_one = key_side(keys, bias, lane, half)
                queries_one = query_side(queries, lane, half)
                lanes = slice(half * HEAD_DIM, (half + 1) * HEAD_DIM)
                head = side * 2 * pairs + 2 * pair + half
                for at in range(0, rows, QUERY_BLOCK):
                    cols = slice(at, at + QUERY_BLOCK)
                    scores = back_product(keys_one, queries_one[cols])
                    top = jnp.max(scores, axis=0, keepdims=True)
                    exps = jnp.exp(scores - top)
                    total = jnp.sum(exps, axis=0, keepdims=True)
                    mixed_t = forward_product(values_t[lanes], exps.astype(jnp.bfloat16))
                    ot_ref[lanes, cols] = mixed_t / total
                    lse_ref[pl.ds(head, 1), cols] = top + jnp.log(total)
            at = pl.multiple_of(side * width + pair * LANES, LANES)
            mixed_ref[:, pl.ds(at, LANES)] = ot_ref[...].T.astype(jnp.bfloat16)
            return carry

        lax.fori_loop(0, pairs, one_pair, 0)


def attend_core(qkv_lo, qkv_hi, seq_lengths, seq, filled=None):
    total, wide = qkv_lo.shape
    seqs = seq_lengths.shape[0]
    rows, width = total // seqs, 2 * wide // 3
    heads = width // HEAD_DIM
    lse_rows = -(-heads // 8) * 8
    side = pl.BlockSpec((rows, wide), lambda at, lens: (seq, 0))
    kept = [] if filled is None else list(filled)
    anywhere = pl.BlockSpec(memory_space=pl.ANY)

    def kernel(len_ref, lo_ref, hi_ref, *rest):
        attend_kernel(seq, len_ref, lo_ref, hi_ref, *rest[len(kept) :])

    return pl.pallas_call(
        kernel,
        out_shape=(
            jax.ShapeDtypeStruct((total, width), jnp.bfloat16),
            jax.ShapeDtypeStruct((seqs, lse_rows, rows), jnp.float32),
        ),
        grid_spec=pltpu.PrefetchScalarGridSpec(
            num_scalar_prefetch=1,
            grid=(1,),
            in_specs=[side, side] + [anywhere] * len(kept),
            out_specs=[
                pl.BlockSpec((rows, width), lambda at, lens: (seq, 0)),
                pl.BlockSpec((None, lse_rows, rows), lambda at, lens: (seq, 0, 0)),
            ],
            scratch_shapes=[pltpu.VMEM((LANES, rows), jnp.float32)],
        ),
        input_output_aliases={3 + at: at for at in range(len(kept))},
        compiler_params=pltpu.CompilerParams(vmem_limit_bytes=24 << 20),
        cost_estimate=pl.CostEstimate(
            flops=16 * rows * rows * width,
            bytes_accessed=8 * rows * width,
            transcendentals=rows * rows * heads,
        ),
        name="attend",
    )(seq_lengths, qkv_lo, qkv_hi, *kept)


def attend_back_kernel(
    len_ref, qkv_lo, qkv_hi, d_mixed_ref, lse_ref, d_qkv_ref, dqt_ref, dk_ref, dv_ref
):
    rows = d_mixed_ref.shape[0]
    width = qkv_lo.shape[1] // 3
    pairs = width // LANES
    scale = 1.0 / math.sqrt(HEAD_DIM)
    real = len_ref[pl.program_id(0)]
    lane = lax.broadcasted_iota(jnp.int32, (rows, LANES), 1)
    place_key = lax.broadcasted_iota(jnp.int32, (rows, LANES), 0)
    bias = jnp.where(place_key < real, 0.0, NEG_FILL)
    for side, qkv_ref in enumerate((qkv_lo, qkv_hi)):

        def one_pair(pair, carry, side=side, qkv_ref=qkv_ref):
            queries = pair_of(qkv_ref, 0, pair) * scale
            keys = pair_of(qkv_ref, 1, pair)
            values = pair_of(qkv_ref, 2, pair)
            at_mixed = pl.multiple_of(side * width + pair * LANES, LANES)
            d_mixed = d_mixed_ref[:, pl.ds(at_mixed, LANES)].astype(jnp.float32)
            keys_t = keys.T.astype(jnp.bfloat16)
            started = False
            for half in range(2):
                keys_one = key_side(keys, bias, lane, half)
                queries_one = query_side(queries, lane, half)
                values_only = one_head(values, lane, half)
                queries_only = one_head(queries, lane, half)
                d_mixed_only = one_head(d_mixed, lane, half)
                lanes = slice(half * HEAD_DIM, (half + 1) * HEAD_DIM)
                head = side * 2 * pairs + 2 * pair + half
                for at in range(0, rows, QUERY_BLOCK):
                    cols = slice(at, at + QUERY_BLOCK)
                    scores = back_product(keys_one, queries_one[cols])
                    d_probs = back_product(values_only, d_mixed_only[cols])
                    probs = jnp.exp(scores - lse_ref[pl.ds(head, 1), cols])
                    row_part = jnp.sum(probs * d_probs, axis=0, keepdims=True)
                    d_scores = (probs * (d_probs - row_part)).astype(jnp.bfloat16)
                    d_values = forward_product(probs.astype(jnp.bfloat16), d_mixed_only[cols])
                    d_keys = forward_product(d_scores, queries_only[cols])
                    if started:
                        dv_ref[...] += d_values
                        dk_ref[...] += d_keys
                    else:
                        dv_ref[...] = d_values
                        dk_ref[...] = d_keys
                        started = True
                    dqt_ref[lanes, cols] = forward_product(keys_t[lanes], d_scores)
            outs = ((dqt_ref[...].T * scale), dk_ref[...], dv_ref[...])
            for part, value in enumerate(outs):
                at = pl.multiple_of(part * width + pair * LANES, LANES)
                d_qkv_ref[side, :, pl.ds(at, LANES)] = value.astype(jnp.bfloat16)
            return carry

        lax.fori_loop(0, pairs, one_pair, 0)


def attend_core_back(qkv_lo, qkv_hi, d_mixed, lse, seq_lengths):
    total, wide = qkv_lo.shape
    seqs = seq_lengths.shape[0]
    rows, width = total // seqs, 2 * wide // 3
    heads = width // HEAD_DIM
    side = pl.BlockSpec((rows, wide), lambda seq, lens: (seq, 0))
    return pl.pallas_call(
        attend_back_kernel,
        out_shape=jax.ShapeDtypeStruct((2, total, wide), jnp.bfloat16),
        grid_spec=pltpu.PrefetchScalarGridSpec(
            num_scalar_prefetch=1,
            grid=(seqs,),
            in_specs=[
                side,
                side,
                pl.BlockSpec((rows, width), lambda seq, lens: (seq, 0)),
                pl.BlockSpec((None, lse.shape[1], rows), lambda seq, lens: (seq, 0, 0)),
            ],
            out_specs=pl.BlockSpec((2, rows, wide), lambda seq, lens: (0, seq, 0)),
            scratch_shapes=[
                pltpu.VMEM((LANES, rows), jnp.float32),
                pltpu.VMEM((rows, LANES), jnp.float32),
                pltpu.VMEM((rows, LANES), jnp.float32),
            ],
        ),
        compiler_params=pltpu.CompilerParams(vmem_limit_bytes=40 << 20),
        cost_estimate=pl.CostEstimate(
            flops=40 * total * rows * width,
            bytes_accessed=14 * total * width,
            transcendentals=total * rows * heads,
        ),
        name="attend_back",
    )(seq_lengths, qkv_lo, qkv_hi, d_mixed, lse)


def half_of(rows, side):
    width = rows.shape[1] // 2
    return lax.dynamic_slice_in_dim(rows, side * width, width, 1)


def project_in(flat_low, in_layer, small_layer):
    third = flat_low.shape[1] // 2
    qkv = []
    for side in range(2):
        cols = slice(side * third, (side + 1) * third)
        bias = jnp.concatenate(
            [small_layer[0, cols], jnp.zeros((third,), jnp.float32), small_layer[1, cols]]
        )
        part = forward_product(flat_low, in_layer[side]) + bias
        qkv.append(part.astype(jnp.bfloat16))
    return qkv


def project_out(flat_rows, mixed_heads, out_layer, small_layer):
    branch = forward_product(mixed_heads, out_layer)
    return norm_forward(flat_rows + branch + small_layer[2], small_layer[3], small_layer[4])


def project_out_back(d_normed, normal_part, inv_std, out_layer, small_layer):
    d_resid, d_gain, d_shift = norm_backward(d_normed, normal_part, inv_std, small_layer[3])
    d_branch = d_resid.astype(jnp.bfloat16)
    d_out_bias = jnp.sum(d_branch.astype(jnp.float32), axis=0)
    d_mixed = back_product(d_branch, out_layer).astype(jnp.bfloat16)
    return (d_resid, d_branch, d_mixed, (d_out_bias, d_gain, d_shift))


def project_in_back(d_resid, d_qkv, in_layer):
    return d_resid + sum(back_product(d_qkv[side], in_layer[side]) for side in range(2))


def attn_small(d_qkv, sums_out):
    third = d_qkv.shape[2] // 3
    sums = jnp.sum(d_qkv.astype(jnp.float32), axis=1)
    return jnp.stack(
        [sums[:, :third].reshape(-1), sums[:, 2 * third :].reshape(-1)] + list(sums_out)
    )


def attn_grads_kernel(core, x_ref, mixed_ref, d_qkv_ref, d_branch_ref, *rest):
    small_ref = rest[0] if len(rest) == 5 else None
    far_ref, own_ref, xt_ref, mixed_t_ref = rest[-4:]
    third = d_branch_ref.shape[1]

    @pl.when(pl.program_id(0) == 0)
    def _():
        xt_ref[...] = x_ref[...].T
        mixed_t_ref[...] = mixed_ref[...].T

    def fill(out_ref):
        out_ref[:, : 3 * third] = forward_product(xt_ref[...], d_qkv_ref[...]).astype(jnp.bfloat16)
        out_ref[:, 3 * third : 4 * third] = forward_product(
            mixed_t_ref[...], d_branch_ref[...]
        ).astype(jnp.bfloat16)
        if small_ref is not None:
            out_ref[:, 4 * third :] = small_ref[...]

    @pl.when(pl.program_id(0) == 0)
    def _():
        fill(far_ref)

    @pl.when(pl.program_id(0) == 1)
    def _():
        fill(own_ref)


def attn_grads(core, x_low, mixed_heads, d_qkv, d_branch, small=None):
    total, width = x_low.shape
    third = width // 2
    extra = 0 if small is None else small.shape[2]

    def side(at, core):
        return jnp.where(at == 0, 1 - core[0], core[0])

    specs = [pl.BlockSpec((total, width), lambda at, core: (0, 0))] * 2 + [
        pl.BlockSpec((None, total, 3 * third), lambda at, core: (side(at, core), 0, 0)),
        pl.BlockSpec((total, third), lambda at, core: (0, side(at, core))),
    ]
    given = [x_low, mixed_heads, d_qkv, d_branch]
    if small is not None:
        specs.append(
            pl.BlockSpec((None, width, extra), lambda at, core: (side(at, core), 0, 0))
        )
        given.append(small)
    shape = jax.ShapeDtypeStruct((width, 4 * third + extra), jnp.bfloat16)
    return pl.pallas_call(
        attn_grads_kernel,
        out_shape=(shape, shape),
        grid_spec=pltpu.PrefetchScalarGridSpec(
            num_scalar_prefetch=1,
            grid=(2,),
            in_specs=specs,
            out_specs=[pl.BlockSpec(shape.shape, lambda at, core: (0, 0))] * 2,
            scratch_shapes=[pltpu.VMEM((width, total), jnp.bfloat16)] * 2,
        ),
        compiler_params=pltpu.CompilerParams(vmem_limit_bytes=36 << 20),
        cost_estimate=pl.CostEstimate(
            flops=8 * total * width * width,
            bytes_accessed=2 * (8 * total * width + 4 * width * width),
            transcendentals=0,
        ),
        name="attn_grads",
    )(core.reshape(1).astype(jnp.int32), *given)


def feed_up_kernel(rows_ref, up_ref, bias_ref, act_ref, slope_ref):
    low_rows = rows_ref[...]
    for at in range(0, up_ref.shape[1], HIDDEN_BLOCK):
        cols = slice(at, at + HIDDEN_BLOCK)
        pre_act = forward_product(low_rows, up_ref[:, cols]) + bias_ref[:, cols]
        below = 0.5 * (1.0 + lax.erf(pre_act * 0.7071067811865476))
        density = jnp.exp(-0.5 * pre_act * pre_act) * 0.3989422804014327
        act_ref[:, cols] = (pre_act * below).astype(jnp.bfloat16)
        slope_ref[:, cols] = (below + pre_act * density).astype(jnp.bfloat16)


def feed_up(rows_in, up_layer, small_layer):
    rows_low = rows_in.astype(jnp.bfloat16)
    total, width = rows_low.shape
    hidden = up_layer.shape[1]
    block = math.gcd(total, 256)
    bias = small_layer[5:9].reshape(1, hidden)
    shape = jax.ShapeDtypeStruct((total, hidden), jnp.bfloat16)
    act_low, slope = pl.pallas_call(
        feed_up_kernel,
        out_shape=(shape, shape),
        grid=(total // block,),
        in_specs=[
            pl.BlockSpec((block, width), lambda at: (at, 0)),
            pl.BlockSpec((width, hidden), lambda at: (0, 0)),
            pl.BlockSpec((1, hidden), lambda at: (0, 0)),
        ],
        out_specs=[pl.BlockSpec((block, hidden), lambda at: (at, 0))] * 2,
        compiler_params=pltpu.CompilerParams(vmem_limit_bytes=32 << 20),
        cost_estimate=pl.CostEstimate(
            flops=2 * total * width * hidden,
            bytes_accessed=2 * (width * hidden + 2 * total * hidden),
            transcendentals=2 * total * hidden,
        ),
        name="feed_up",
    )(rows_low, up_layer, bias)
    return (rows_low, act_low, slope)


def feed_down(rows_in, act_low, down_layer, small_layer):
    branch = forward_product(act_low, down_layer) + small_layer[9]
    return norm_forward(rows_in + branch, small_layer[10], small_layer[11])


def feed_down_back(d_normed, normal_part, inv_std, slope, down_layer, small_layer):
    d_resid, d_gain, d_shift = norm_backward(d_normed, normal_part, inv_std, small_layer[10])
    d_branch = d_resid.astype(jnp.bfloat16)
    d_pre = (back_product(d_branch, down_layer) * slope.astype(jnp.float32)).astype(jnp.bfloat16)
    model_width = d_resid.shape[1]
    small_rows = jnp.concatenate(
        [
            jnp.sum(d_pre.astype(jnp.float32), axis=0).reshape(4, model_width),
            jnp.stack([jnp.sum(d_branch.astype(jnp.float32), axis=0), d_gain, d_shift]),
        ],
        axis=0,
    )
    return (d_resid, d_branch, d_pre, small_rows)


def feed_grads_kernel(shard, core, low_ref, d_pre_ref, act_ref, d_branch_ref, *rest):
    far_ref, own_ref, low_t_ref, down_ref = rest
    at = pl.program_id(0)
    width = low_ref.shape[1]
    third = width // 2

    @pl.when(at == 0)
    def _():
        low_t_ref[...] = low_ref[...].T

    for step in range(4):

        @pl.when(at == step)
        def _(step=step):
            out_ref = far_ref if step < 2 else own_ref
            cols = slice((step % 2) * width, (step % 2 + 1) * width)
            out_ref[:, cols] = forward_product(low_t_ref[...], d_pre_ref[...]).astype(jnp.bfloat16)

    @pl.when(at >= 4)
    def _():
        down_ref[...] = weight_grad(act_ref[...], d_branch_ref[...])
        blocks = width // (4 * shard)
        for out_ref, side in ((far_ref, 1 - core[0]), (own_ref, core[0])):
            from_cols = pl.ds(pl.multiple_of(side * third, LANES), third)
            for block in range(blocks):
                row = pl.multiple_of(((at - 4) * blocks + block) * shard, 16)
                for part in range(4):
                    start = (block * 4 + part) * shard
                    cols = slice(2 * width + part * third, 2 * width + (part + 1) * third)
                    out_ref[pl.ds(row, shard), cols] = down_ref[
                        start : start + shard, from_cols
                    ].astype(jnp.bfloat16)


def feed_grads_plain(core, rows_low, d_pre, act_low, d_branch, shard):
    sides = []
    width = rows_low.shape[1]
    for side in (1 - core, core):
        d_up = weight_grad(rows_low, half_of(d_pre, side))
        d_down = weight_grad(act_low, half_of(d_branch, side))
        d_down = d_down.reshape(-1, 4, shard, width // 2).transpose(0, 2, 1, 3)
        sides.append(jnp.concatenate([d_up, d_down.reshape(width, -1)], axis=1))
    return [part.astype(jnp.bfloat16) for part in sides]


def feed_grads(core, rows_low, d_pre, act_low, d_branch, shard):
    total, width = rows_low.shape
    hidden = act_low.shape[1]
    if shard % 16 or hidden != 4 * width:
        return feed_grads_plain(core, rows_low, d_pre, act_low, d_branch, shard)

    def pre_at(at, core):
        step = jnp.minimum(at, 3)
        return (0, jnp.where(step < 2, 1 - core[0], core[0]) * 2 + step % 2)

    shape = jax.ShapeDtypeStruct((width, hidden), jnp.bfloat16)
    return pl.pallas_call(
        functools.partial(feed_grads_kernel, shard),
        out_shape=(shape, shape),
        grid_spec=pltpu.PrefetchScalarGridSpec(
            num_scalar_prefetch=1,
            grid=(8,),
            in_specs=[
                pl.BlockSpec((total, width), lambda at, core: (0, 0)),
                pl.BlockSpec((total, width), pre_at),
                pl.BlockSpec((total, width), lambda at, core: (0, jnp.maximum(at - 4, 0))),
                pl.BlockSpec((total, width), lambda at, core: (0, 0)),
            ],
            out_specs=[pl.BlockSpec((width, hidden), lambda at, core: (0, 0))] * 2,
            scratch_shapes=[
                pltpu.VMEM((width, total), jnp.bfloat16),
                pltpu.VMEM((width, width), jnp.float32),
            ],
        ),
        compiler_params=pltpu.CompilerParams(vmem_limit_bytes=40 << 20),
        cost_estimate=pl.CostEstimate(
            flops=4 * total * width * hidden,
            bytes_accessed=2 * (4 * total * hidden + 2 * width * hidden),
            transcendentals=0,
        ),
        name="feed_grads",
    )(core.reshape(1).astype(jnp.int32), rows_low, d_pre, act_low, d_branch)


def row_select(token_mask, capacity):
    flat_mask = token_mask.reshape(1, -1)
    row_total = flat_mask.shape[1]
    before = (
        lax.broadcasted_iota(jnp.int32, (row_total, row_total), 0)
        < lax.broadcasted_iota(jnp.int32, (row_total, row_total), 1)
    ).astype(jnp.bfloat16)
    rank = forward_product(flat_mask.astype(jnp.bfloat16), before).astype(jnp.int32)
    slots = lax.broadcasted_iota(jnp.int32, (capacity, row_total), 0)
    return ((slots == rank) & (flat_mask == 1)).astype(jnp.bfloat16)


def split_low(wide, parts):
    pieces = []
    left = wide
    for _ in range(parts - 1):
        piece = lax.reduce_precision(left, 8, 7)
        pieces.append(piece.astype(jnp.bfloat16))
        left = left - piece
    pieces.append(left.astype(jnp.bfloat16))
    return jnp.concatenate(pieces, axis=1)


def join_low(joined, parts):
    width = joined.shape[1] // parts
    total = joined[:, :width]
    for number in range(1, parts):
        total = total + joined[:, number * width : (number + 1) * width]
    return total


def adam_update(
    master, first_moment, second_moment, gradient, clip_scale, step_value, decay_rate, rate_value
):
    clipped = gradient * clip_scale
    first_new = BETA_FIRST * first_moment + (1.0 - BETA_FIRST) * clipped
    second_new = BETA_SECOND * second_moment + (1.0 - BETA_SECOND) * clipped * clipped
    first_hat = first_new / (1.0 - jnp.power(BETA_FIRST, step_value))
    second_hat = second_new / (1.0 - jnp.power(BETA_SECOND, step_value))
    master_new = master - rate_value * (
        first_hat / (jnp.sqrt(second_hat) + ADAM_EPS) + decay_rate * master
    )
    return (master_new, first_new, second_new, master_new.astype(jnp.bfloat16))


def routes(peers):
    bits = peers.bit_length() - 1
    deep = min(2, bits)
    rest = bits - deep
    x_bits = [1 << at for at in range(rest - rest // 2)]
    y_bits = [1 << at for at in range(rest - rest // 2, rest)]
    z_bits = [1 << at for at in reversed(range(rest, bits))]
    first = z_bits + y_bits + x_bits
    second = z_bits + x_bits + y_bits
    return (first, second if len(x_bits) == len(y_bits) else first)


def shift(value, step, peers):
    pairs = []
    for core, path in enumerate(routes(peers)):
        pairs += [(core * peers + at, core * peers + (at ^ path[step])) for at in range(peers)]
    return lax.ppermute(value, ("dp", "bal"), pairs)


def swap(value):
    return lax.ppermute(value, "dp", [(0, 1), (1, 0)])


def place_table(peers, core):
    masks = [
        [sum(bit for at, bit in enumerate(path) if spot >> at & 1) for spot in range(peers)]
        for path in routes(peers)
    ]
    masks = jnp.asarray(np.array(masks, np.int32))
    mine = lax.axis_index("bal")
    own = jnp.where(core == 0, masks[0], masks[1])
    far = jnp.where(core == 0, masks[1], masks[0])
    return jnp.concatenate([mine ^ own, mine ^ far, core.reshape(1).astype(jnp.int32)])


def place_kernel(plan, spots, *refs):
    parts, outs = refs[:4], refs[4:]
    half, rows, _ = parts[0].shape
    core = spots[4 * half]

    for number, part in enumerate(parts):
        side = core if number < 2 else 1 - core

        def one_block(at, carry, number=number, part=part, side=side):
            spot = spots[number * half + at]
            for (start, width, kind), out in zip(plan, outs):
                cols = pl.ds(pl.multiple_of(side * width, LANES), width)
                if kind == "stack":
                    out[side, spot] = part[at, :, start : start + width]
                elif kind == "wide":
                    out[spot, :, cols] = part[at, :, start : start + width]
                else:
                    for piece in range(4):
                        begin = start + piece * width
                        out[spot, piece * rows : (piece + 1) * rows, cols] = part[
                            at, :, begin : begin + width
                        ]
            return carry

        lax.fori_loop(0, half, one_block, 0)


def place(spots, parts, plan):
    half, rows, whole = parts[0].shape
    peers = 2 * half
    kinds = [
        (start, 4 * width, "stack") if kind == "down" and rows % 16 else (start, width, kind)
        for start, width, kind in plan
    ]
    shapes = {
        "stack": lambda width: (2, peers, rows, width),
        "wide": lambda width: (peers, rows, 2 * width),
        "down": lambda width: (peers, 4 * rows, 2 * width),
    }
    local = pl.BlockSpec(memory_space=pltpu.VMEM)
    placed = pl.pallas_call(
        functools.partial(place_kernel, kinds),
        out_shape=[
            jax.ShapeDtypeStruct(shapes[kind](width), parts[0].dtype) for _, width, kind in kinds
        ],
        grid_spec=pltpu.PrefetchScalarGridSpec(
            num_scalar_prefetch=1,
            grid=(),
            in_specs=[local] * 4,
            out_specs=[local] * len(kinds),
        ),
        compiler_params=pltpu.CompilerParams(vmem_limit_bytes=40 << 20),
        cost_estimate=pl.CostEstimate(
            flops=0, bytes_accessed=8 * peers * rows * whole, transcendentals=0
        ),
        name="place",
    )(spots, *parts)
    results = []
    for part, (_, width, kind), (_, _, asked) in zip(placed, kinds, plan):
        if kind != asked:
            part = part.reshape(2, peers, rows, 4, width // 4).transpose(1, 3, 2, 0, 4)
            results.append(part.reshape(peers * rows * 4, width // 2))
        elif kind == "stack":
            results.append(part.reshape(2, peers * rows, width))
        else:
            results.append(part.reshape(-1, 2 * width))
    return results


class Gather:
    def __init__(self, mine, spots, peers, plan):
        self.kept = [mine[None]]
        self.spots, self.peers, self.plan = spots, peers, plan
        self.step, self.last = 0, peers.bit_length()

    def launch(self):
        if self.step < self.last - 1:
            return [shift(self.kept[0], self.step, self.peers)]
        return [swap(part) for part in self.kept]

    def land(self, moved):
        if self.step < self.last - 2:
            self.kept = [jnp.concatenate([self.kept[0], moved[0]], axis=0)]
        else:
            self.kept = self.kept + moved
        self.step += 1

    def result(self):
        return place(self.spots, self.kept, self.plan)


class Scatter:
    def __init__(self, far, own, spots, peers):
        self.kept = [grads.reshape(peers, -1, grads.shape[1]) for grads in (own, far)]
        self.spots, self.peers = spots, peers
        self.step, self.last = 0, peers.bit_length()

    def launch(self):
        if self.step == 0:
            return [swap(self.kept[1])]
        return [shift(self.kept[1], self.last - 1 - self.step, self.peers)]

    def land(self, moved):
        if self.step == 0:
            self.kept = list(fold(self.spots, self.kept[0], moved[0]))
        else:
            total = self.kept[0].astype(jnp.float32) + moved[0].astype(jnp.float32)
            half = total.shape[0] // 2
            low_sum = total.astype(jnp.bfloat16)
            self.kept = [low_sum[:half], low_sum[half:]] if half else [low_sum]
        self.step += 1

    def result(self):
        return self.kept[0][0]


class Lanes:
    def __init__(self):
        self.flying = {}

    def launch(self, *moves):
        for move in moves:
            if move.step < move.last:
                self.flying[move] = move.launch()

    def meet(self, work, *landing, ready=()):
        moves = [move for move in landing if move in self.flying]
        flown = [self.flying.pop(move) for move in moves]
        waiting = [move.kept for move in ready]
        work, flown, waiting = lax.optimization_barrier((work, flown, waiting))
        for move, moved in zip(moves, flown):
            move.land(moved)
        for move, kept in zip(ready, waiting):
            move.kept = kept
        return work

    def finish(self, work, *moves):
        work = self.meet(work, *moves)
        while any(move.step < move.last for move in moves):
            self.launch(*moves)
            work = self.meet(work, *moves)
        return work


def fold_kernel(spots, own, far, keep, send):
    half = keep.shape[0]

    def one_block(at, carry):
        for out, spot in ((keep, spots[at]), (send, spots[half + at])):
            out[at] = (own[spot].astype(jnp.float32) + far[spot].astype(jnp.float32)).astype(
                out.dtype
            )
        return carry

    lax.fori_loop(0, half, one_block, 0)


def fold(spots, own, far):
    peers, rows, width = own.shape
    shape = jax.ShapeDtypeStruct((peers // 2, rows, width), own.dtype)
    local = pl.BlockSpec(memory_space=pltpu.VMEM)
    return pl.pallas_call(
        fold_kernel,
        out_shape=(shape, shape),
        grid_spec=pltpu.PrefetchScalarGridSpec(
            num_scalar_prefetch=1, grid=(), in_specs=[local, local], out_specs=[local, local]
        ),
        compiler_params=pltpu.CompilerParams(vmem_limit_bytes=32 << 20),
        cost_estimate=pl.CostEstimate(
            flops=peers * rows * width,
            bytes_accessed=6 * peers * rows * width,
            transcendentals=0,
        ),
        name="fold",
    )(spots, own, far)


def both_sides(own, core):
    other = swap(own)
    return (jnp.where(core == 0, own, other), jnp.where(core == 0, other, own))


def sum_all(value, peers):
    total = value.reshape(1, 1)
    total = total + swap(total)
    step = 1
    while step < peers:
        span = min(4, peers // step)
        moved = [
            lax.ppermute(total, "bal", [(at, at ^ (turn * step)) for at in range(peers)])
            for turn in range(1, span)
        ]
        if span == 4:
            total = (total + moved[0]) + (moved[1] + moved[2])
        else:
            total = total + moved[0]
        step *= span
    return total[0, 0]


def per_device(
    tokens,
    cotangent,
    seq_lengths,
    token_mask,
    step_count,
    attn_master,
    attn_first,
    attn_second,
    up_master,
    up_first,
    up_second,
    down_master,
    down_first,
    down_second,
    small_master,
    small_first,
    small_second,
):
    core = lax.axis_index("dp")
    peers = lax.axis_size("bal")
    seq_count, length, model_width = tokens.shape
    rows_total = seq_count * length
    spots = place_table(peers, core)
    shard = attn_master.shape[2]
    attn_half = lax.dynamic_slice_in_dim(attn_master, core * (model_width // 2), model_width // 2, 3)
    attn_half = attn_half.astype(jnp.bfloat16).transpose(0, 2, 1, 3).reshape(2, shard, -1)
    small_half = lax.dynamic_slice_in_dim(small_master.reshape(24, shard), core * 12, 12, 0)
    small_half = jnp.pad(small_half.astype(jnp.bfloat16).T, ((0, 0), (0, LANES - 12)))
    wide = attn_half.shape[2]
    lanes = Lanes()
    third = model_width // 2
    hidden_half = up_master.shape[2] // 2

    def down_half(layer):
        half = half_of(down_master[layer], core).astype(jnp.bfloat16)
        return [half[part * shard : (part + 1) * shard] for part in range(4)]

    up_half = [half_of(up_master[layer], core).astype(jnp.bfloat16) for layer in range(2)]
    in_one = Gather(
        jnp.concatenate([attn_half[0, :, : 3 * third], small_half], axis=1),
        spots,
        peers,
        [(0, 3 * third, "stack"), (3 * third, LANES, "stack")],
    )
    out_up_one = Gather(
        jnp.concatenate([attn_half[0, :, 3 * third :], up_half[0]], axis=1),
        spots,
        peers,
        [(0, third, "wide"), (third, hidden_half, "wide")],
    )
    down_one = Gather(
        jnp.concatenate(down_half(0), axis=1), spots, peers, [(0, third, "down")]
    )
    attn_two = Gather(
        attn_half[1], spots, peers, [(0, 3 * third, "stack"), (3 * third, third, "wide")]
    )
    feed_two = Gather(
        jnp.concatenate([up_half[1]] + down_half(1), axis=1),
        spots,
        peers,
        [(0, hidden_half, "wide"), (hidden_half, third, "down")],
    )
    flat_low = tokens.reshape(rows_total, model_width)
    cot_flat = cotangent.reshape(rows_total, model_width)
    select_rows = row_select(token_mask, MCAP)
    flat_mask = token_mask.reshape(-1, 1) == 1

    lanes.launch(in_one)
    lanes.meet((), in_one)
    lanes.launch(in_one)
    lanes.meet((), in_one, ready=(out_up_one,))
    lanes.launch(in_one, out_up_one)
    lanes.meet((), in_one, out_up_one)
    lanes.launch(in_one, out_up_one)
    lanes.meet((), in_one, out_up_one, ready=(down_one,))
    lanes.launch(in_one, out_up_one, down_one)
    lanes.finish((), in_one)
    first = in_one.result()
    (w_in_one, small_rows), = lanes.meet((first,), out_up_one, down_one, ready=(attn_two,))
    small_vals = small_rows[:, :, :12].transpose(0, 2, 1).astype(jnp.float32)
    lanes.launch(out_up_one, down_one, attn_two)
    qkv_one = project_in(flat_low, w_in_one, small_vals[0])
    seqs = seq_lengths.shape[0]
    attended = attend_core(qkv_one[0], qkv_one[1], seq_lengths, 0)
    attended = lanes.meet(attended, out_up_one, down_one, attn_two, ready=(feed_two,))
    lanes.launch(out_up_one, down_one, attn_two)
    for seq in range(1, seqs):
        attended = attend_core(qkv_one[0], qkv_one[1], seq_lengths, seq, attended)
    attended = lanes.meet(attended, out_up_one, down_one, attn_two)
    mixed_one, lse_one = lanes.finish(attended, out_up_one)
    lanes.launch(down_one, feed_two)
    w_out_one, w_up_one = out_up_one.result()
    attended_one = project_out(flat_low.astype(jnp.float32), mixed_one, w_out_one, small_vals[0])
    attended_one, attn_xhat_one, attn_inv_one = lanes.meet(attended_one, down_one)
    lanes.launch(down_one, attn_two)
    act_one = feed_up(attended_one, w_up_one, small_vals[0])
    act_one = lanes.meet(act_one, down_one, attn_two, feed_two)
    low_one, act_one, slope_one = lanes.finish(act_one, down_one)
    lanes.launch(attn_two, feed_two)
    (w_down_one,) = down_one.result()
    layer_one = feed_down(attended_one, act_one, w_down_one, small_vals[0])
    layer_one = lanes.meet(layer_one, attn_two, feed_two)
    lanes.launch(attn_two, feed_two)
    layer_one, feed_xhat_one, feed_inv_one = lanes.finish(layer_one, attn_two)
    w_in_two, w_out_two = attn_two.result()
    layer_low = layer_one.astype(jnp.bfloat16)
    qkv_two = project_in(layer_low, w_in_two, small_vals[1])
    attended = attend_core(qkv_two[0], qkv_two[1], seq_lengths, 0)
    attended = lanes.meet(attended, feed_two)
    lanes.launch(feed_two)
    for seq in range(1, seqs):
        attended = attend_core(qkv_two[0], qkv_two[1], seq_lengths, seq, attended)
    mixed_two, lse_two = attended
    attended_two = project_out(layer_one, mixed_two, w_out_two, small_vals[1])
    attended_two = lanes.meet((attended_two, mixed_two, lse_two), feed_two)
    (attended_two, attn_xhat_two, attn_inv_two), mixed_two, lse_two = attended_two
    lanes.launch(feed_two)
    rows_in = join_low(forward_product(select_rows, split_low(attended_two, 3)), 3)
    d_rows_out = forward_product(select_rows, cot_flat)
    rows_in = lanes.finish(rows_in, feed_two)
    w_up_two, w_down_two = feed_two.result()
    rows_low, act_two, slope_two = feed_up(rows_in, w_up_two, small_vals[1])
    out_rows, feed_xhat_two, feed_inv_two = feed_down(rows_in, act_two, w_down_two, small_vals[1])
    d_resid, d_branch, d_pre, feed_small_two = feed_down_back(
        d_rows_out, feed_xhat_two, feed_inv_two, slope_two, w_down_two, small_vals[1]
    )
    grads = feed_grads(core, rows_low, d_pre, act_two, d_branch, shard)
    grads, d_resid, d_pre = lanes.meet((grads, d_resid, d_pre))
    g_feed_two = Scatter(*grads, spots, peers)
    lanes.launch(g_feed_two)
    d_in_rows = d_resid + back_product(d_pre, w_up_two)
    d_attended_two = jnp.where(
        flat_mask,
        join_low(weight_grad(select_rows, split_low(d_in_rows, 2)), 2),
        cot_flat.astype(jnp.float32),
    )
    back = project_out_back(d_attended_two, attn_xhat_two, attn_inv_two, w_out_two, small_vals[1])
    d_resid, d_branch, d_mixed, sums_out = lanes.meet(back, g_feed_two)
    lanes.launch(g_feed_two)
    d_qkv = attend_core_back(qkv_two[0], qkv_two[1], d_mixed, lse_two, seq_lengths)
    d_qkv = lanes.meet(d_qkv, g_feed_two)
    lanes.launch(g_feed_two)
    grads = attn_grads(core, layer_low, mixed_two, d_qkv, d_branch)
    d_layer_one = project_in_back(d_resid, d_qkv, w_in_two)
    attn_small_two = attn_small(d_qkv, sums_out)
    grads, d_layer_one = lanes.meet((grads, d_layer_one), g_feed_two)
    g_attn_two = Scatter(*grads, spots, peers)
    lanes.launch(g_attn_two, g_feed_two)
    back = feed_down_back(
        d_layer_one, feed_xhat_one, feed_inv_one, slope_one, w_down_one, small_vals[0]
    )
    d_resid, d_branch, d_pre, feed_small_one = lanes.meet(back, g_attn_two, g_feed_two)
    lanes.launch(g_attn_two, g_feed_two)
    grads = feed_grads(core, low_one, d_pre, act_one, d_branch, shard)
    grads = lanes.meet(grads, g_attn_two, g_feed_two)
    g_feed_one = Scatter(*grads, spots, peers)
    lanes.launch(g_feed_one, g_attn_two)
    d_attended_one = d_resid + back_product(d_pre, w_up_one)
    back = project_out_back(d_attended_one, attn_xhat_one, attn_inv_one, w_out_one, small_vals[0])
    d_resid, d_branch, d_mixed, sums_out = lanes.meet(back, g_feed_one, g_attn_two)
    lanes.launch(g_feed_one, g_attn_two)
    d_qkv = attend_core_back(qkv_one[0], qkv_one[1], d_mixed, lse_one, seq_lengths)
    d_qkv = lanes.meet(d_qkv, g_feed_one, g_attn_two)
    lanes.launch(g_feed_one, g_attn_two)
    attn_small_one = attn_small(d_qkv, sums_out)
    small_grads = jnp.stack(
        [
            jnp.concatenate([attn_small_one, feed_small_one], axis=0),
            jnp.concatenate([attn_small_two, feed_small_two], axis=0),
        ]
    )

    small_cols = jnp.pad(
        small_grads.astype(jnp.bfloat16).transpose(0, 2, 1), ((0, 0), (0, 0), (0, LANES - 12))
    )
    grads = attn_grads(core, flat_low, mixed_one, d_qkv, d_branch, small_cols)
    grads, d_resid, d_qkv = lanes.meet((grads, d_resid, d_qkv), g_feed_one, g_attn_two)
    g_attn_one = Scatter(*grads, spots, peers)
    lanes.launch(g_attn_one, g_feed_one)
    d_tokens = project_in_back(d_resid, d_qkv, w_in_one).astype(jnp.bfloat16)
    d_tokens = lanes.meet(d_tokens, g_attn_one)
    lanes.launch(g_attn_one)
    output_flat = jnp.where(
        flat_mask,
        weight_grad(select_rows, out_rows.astype(jnp.bfloat16)),
        attended_two,
    ).astype(jnp.bfloat16)
    output_flat = lanes.meet(output_flat, g_attn_one, g_feed_one)
    lanes.launch(g_attn_one, g_feed_one)
    lanes.meet((), g_attn_one)
    lanes.launch(g_attn_one)
    lanes.meet((), g_attn_one, g_feed_one)
    lanes.finish((), g_attn_one, g_feed_one, g_attn_two, g_feed_two)
    owned = {
        "attn0": g_attn_one.result(),
        "feed0": g_feed_one.result(),
        "attn1": g_attn_two.result(),
        "feed1": g_feed_two.result(),
    }
    partial_squares = sum(jnp.sum(jnp.square(owned[name].astype(jnp.float32))) for name in owned)
    both = {name: both_sides(owned[name], core) for name in owned}
    square_total = sum_all(partial_squares, peers)

    def joined(name, start, width):
        return jnp.concatenate([part[:, start : start + width] for part in both[name]], axis=1)

    def down_rows(name):
        return jnp.concatenate(
            [joined(name, hidden_half + part * third, third) for part in range(4)], axis=0
        )

    reduced = (
        jnp.stack(
            [
                jnp.stack([joined(name, part * third, third) for part in range(4)])
                for name in ("attn0", "attn1")
            ]
        ).astype(jnp.float32),
        jnp.stack([joined(name, 0, hidden_half) for name in ("feed0", "feed1")]).astype(
            jnp.float32
        ),
        jnp.stack([down_rows(name) for name in ("feed0", "feed1")]).astype(jnp.float32),
        jnp.stack([part[:, wide : wide + 12].T for part in both["attn0"]]).astype(jnp.float32),
    )
    grad_norm = jnp.sqrt(square_total).reshape(1)
    clip_scale = jnp.minimum(1.0, CLIP_NORM / (grad_norm[0] + 1e-06))
    step_value = step_count[0].astype(jnp.float32)
    attn_new = adam_update(
        attn_master,
        attn_first,
        attn_second,
        reduced[0],
        clip_scale,
        step_value,
        WEIGHT_DECAY,
        LEARN_RATE,
    )
    up_new = adam_update(
        up_master, up_first, up_second, reduced[1], clip_scale, step_value, WEIGHT_DECAY, LEARN_RATE
    )
    down_new = adam_update(
        down_master,
        down_first,
        down_second,
        reduced[2],
        clip_scale,
        step_value,
        WEIGHT_DECAY,
        LEARN_RATE,
    )
    small_new = adam_update(
        small_master, small_first, small_second, reduced[3], clip_scale, step_value, 0.0, SMALL_RATE
    )
    output = output_flat.reshape(seq_count, length, model_width)
    input_grad = d_tokens.reshape(seq_count, length, model_width)
    return (output, input_grad, grad_norm) + attn_new + up_new + down_new + small_new


def solution(mesh):
    return jax.shard_map(
        per_device,
        mesh=mesh,
        in_specs=(
            P(("dp", "bal"), None, None),
            P(("dp", "bal"), None, None),
            P(("dp", "bal")),
            P(("dp", "bal"), None),
            P(),
            P(None, None, "bal", None),
            P(None, None, "bal", None),
            P(None, None, "bal", None),
            P(None, "bal", None),
            P(None, "bal", None),
            P(None, "bal", None),
            P(None, "bal", None),
            P(None, "bal", None),
            P(None, "bal", None),
            P(None, None, "bal"),
            P(None, None, "bal"),
            P(None, None, "bal"),
        ),
        out_specs=(
            P(("dp", "bal"), None, None),
            P(("dp", "bal"), None, None),
            P(),
            P(None, None, "bal", None),
            P(None, None, "bal", None),
            P(None, None, "bal", None),
            P(None, None, "bal", None),
            P(None, "bal", None),
            P(None, "bal", None),
            P(None, "bal", None),
            P(None, "bal", None),
            P(None, "bal", None),
            P(None, "bal", None),
            P(None, "bal", None),
            P(None, "bal", None),
            P(None, None, "bal"),
            P(None, None, "bal"),
            P(None, None, "bal"),
            P(None, None, "bal"),
        ),
        check_vma=False,
    )
```

```python
import functools
import math

import jax
import jax.numpy as jnp
import numpy as np
from jax import lax
from jax.experimental import pallas as pl
from jax.experimental.pallas import tpu as pltpu
from jax.sharding import PartitionSpec as P

HEADS = 12
HEAD_DIM = 64
MCAP = 384
LANES = 128
QUERY_BLOCK = 256
HIDDEN_BLOCK = 512
LIGHT = pl.CostEstimate(flops=3000000000, bytes_accessed=8000000, transcendentals=0)


LN_EPS = 1e-06
NEG_FILL = -1000000000.0
CLIP_NORM = 1.0
LEARN_RATE = 0.05
SMALL_RATE = 0.25
BETA_FIRST = 0.9
BETA_SECOND = 0.999
ADAM_EPS = 1e-08
WEIGHT_DECAY = 0.01


def forward_product(left_side, right_side):
    return jnp.dot(left_side, right_side, preferred_element_type=jnp.float32)


def weight_grad(left_side, right_side):
    return lax.dot_general(
        left_side, right_side, (((0,), (0,)), ((), ())), preferred_element_type=jnp.float32
    )


def back_product(left_side, right_side):
    return lax.dot_general(
        left_side, right_side, (((1,), (1,)), ((), ())), preferred_element_type=jnp.float32
    )


def norm_forward(residual, norm_gain, norm_shift):
    centered = residual - jnp.mean(residual, axis=-1, keepdims=True)
    variance = jnp.mean(centered * centered, axis=-1, keepdims=True)
    inv_std = lax.rsqrt(variance + LN_EPS)
    normal_part = centered * inv_std
    return (normal_part * norm_gain + norm_shift, normal_part, inv_std)


def norm_backward(d_out, normal_part, inv_std, norm_gain):
    d_normal = d_out * norm_gain
    d_resid = inv_std * (
        d_normal
        - jnp.mean(d_normal, axis=-1, keepdims=True)
        - normal_part * jnp.mean(d_normal * normal_part, axis=-1, keepdims=True)
    )
    return (
        d_resid,
        jnp.sum(d_out * normal_part, axis=0, keepdims=True),
        jnp.sum(d_out, axis=0, keepdims=True),
    )


def gelu_slope(pre_act):
    return (
        0.5 * (1.0 + lax.erf(pre_act * 0.7071067811865476))
        + pre_act * jnp.exp(-0.5 * pre_act * pre_act) * 0.3989422804014327
    )


def key_side(keys, bias, lane, half):
    own = (lane < HEAD_DIM) if half == 0 else (lane >= HEAD_DIM)
    spare = HEAD_DIM if half == 0 else 0
    return jnp.where(own, keys, jnp.where(lane == spare, bias, 0.0)).astype(jnp.bfloat16)


def query_side(queries, lane, half):
    own = (lane < HEAD_DIM) if half == 0 else (lane >= HEAD_DIM)
    spare = HEAD_DIM if half == 0 else 0
    return jnp.where(own, queries, jnp.where(lane == spare, 1.0, 0.0)).astype(jnp.bfloat16)


def one_head(rows, lane, half):
    own = (lane < HEAD_DIM) if half == 0 else (lane >= HEAD_DIM)
    return jnp.where(own, rows, 0.0).astype(jnp.bfloat16)


def pair_of(ref, part, pair):
    width = ref.shape[1] // 3
    at = pl.multiple_of(part * width + pair * LANES, LANES)
    return ref[:, pl.ds(at, LANES)].astype(jnp.float32)


def attend_kernel(len_ref, qkv_lo, qkv_hi, mixed_ref, lse_ref, ot_ref):
    rows = mixed_ref.shape[0]
    width = qkv_lo.shape[1] // 3
    pairs = width // LANES
    real = len_ref[pl.program_id(0)]
    lane = lax.broadcasted_iota(jnp.int32, (rows, LANES), 1)
    place_key = lax.broadcasted_iota(jnp.int32, (rows, LANES), 0)
    bias = jnp.where(place_key < real, 0.0, NEG_FILL)
    for side, qkv_ref in enumerate((qkv_lo, qkv_hi)):

        def one_pair(pair, carry, side=side, qkv_ref=qkv_ref):
            queries = pair_of(qkv_ref, 0, pair) * (1.0 / math.sqrt(HEAD_DIM))
            keys = pair_of(qkv_ref, 1, pair)
            values_t = pair_of(qkv_ref, 2, pair).T.astype(jnp.bfloat16)
            scored = []
            for half in range(2):
                keys_one = key_side(keys, bias, lane, half)
                queries_one = query_side(queries, lane, half)
                for at in range(0, rows, QUERY_BLOCK):
                    cols = slice(at, at + QUERY_BLOCK)
                    scored.append((half, cols, back_product(keys_one, queries_one[cols])))
            weighed = []
            for half, cols, scores in scored:
                head = side * 2 * pairs + 2 * pair + half
                top = jnp.max(scores, axis=0, keepdims=True)
                exps = jnp.exp(scores - top)
                total = jnp.sum(exps, axis=0, keepdims=True)
                lse_ref[pl.ds(head, 1), cols] = top + jnp.log(total)
                weighed.append((half, cols, exps.astype(jnp.bfloat16), total))
            for half, cols, exps, total in weighed:
                lanes = slice(half * HEAD_DIM, (half + 1) * HEAD_DIM)
                ot_ref[lanes, cols] = forward_product(values_t[lanes], exps) / total
            at = pl.multiple_of(side * width + pair * LANES, LANES)
            mixed_ref[:, pl.ds(at, LANES)] = ot_ref[...].T.astype(jnp.bfloat16)
            return carry

        lax.fori_loop(0, pairs, one_pair, 0)


def attend_core(qkv_lo, qkv_hi, seq_lengths):
    total, wide = qkv_lo.shape
    seqs = seq_lengths.shape[0]
    rows, width = total // seqs, 2 * wide // 3
    heads = width // HEAD_DIM
    lse_rows = -(-heads // 8) * 8
    side = pl.BlockSpec((rows, wide), lambda seq, lens: (seq, 0))
    return pl.pallas_call(
        attend_kernel,
        out_shape=(
            jax.ShapeDtypeStruct((total, width), jnp.bfloat16),
            jax.ShapeDtypeStruct((seqs, lse_rows, rows), jnp.float32),
        ),
        grid_spec=pltpu.PrefetchScalarGridSpec(
            num_scalar_prefetch=1,
            grid=(seqs,),
            in_specs=[side, side],
            out_specs=[
                pl.BlockSpec((rows, width), lambda seq, lens: (seq, 0)),
                pl.BlockSpec((None, lse_rows, rows), lambda seq, lens: (seq, 0, 0)),
            ],
            scratch_shapes=[pltpu.VMEM((LANES, rows), jnp.float32)],
        ),
        compiler_params=pltpu.CompilerParams(vmem_limit_bytes=32 << 20),
        cost_estimate=LIGHT,
        name="attend",
    )(seq_lengths, qkv_lo, qkv_hi)


def attend_back_kernel(len_ref, qkv_lo, qkv_hi, d_mixed_ref, lse_ref, d_qkv_ref, sums_ref, dqt_ref):
    rows = d_mixed_ref.shape[0]
    width = qkv_lo.shape[1] // 3
    pairs = width // LANES
    scale = 1.0 / math.sqrt(HEAD_DIM)
    real = len_ref[pl.program_id(0)]
    lane = lax.broadcasted_iota(jnp.int32, (rows, LANES), 1)
    place_key = lax.broadcasted_iota(jnp.int32, (rows, LANES), 0)
    bias = jnp.where(place_key < real, 0.0, NEG_FILL)
    for side, qkv_ref in enumerate((qkv_lo, qkv_hi)):

        def one_pair(pair, carry, side=side, qkv_ref=qkv_ref):
            queries = pair_of(qkv_ref, 0, pair) * scale
            keys = pair_of(qkv_ref, 1, pair)
            values = pair_of(qkv_ref, 2, pair)
            at_mixed = pl.multiple_of(side * width + pair * LANES, LANES)
            d_mixed = d_mixed_ref[:, pl.ds(at_mixed, LANES)].astype(jnp.float32)
            keys_t = keys.T.astype(jnp.bfloat16)
            scored = []
            for half in range(2):
                keys_one = key_side(keys, bias, lane, half)
                queries_one = query_side(queries, lane, half)
                values_only = one_head(values, lane, half)
                queries_only = one_head(queries, lane, half)
                d_mixed_only = one_head(d_mixed, lane, half)
                for at in range(0, rows, QUERY_BLOCK):
                    cols = slice(at, at + QUERY_BLOCK)
                    scores = back_product(keys_one, queries_one[cols])
                    d_probs = back_product(values_only, d_mixed_only[cols])
                    scored.append(
                        (half, cols, scores, d_probs, queries_only[cols], d_mixed_only[cols])
                    )
            weighed = []
            for half, cols, scores, d_probs, queries_only, d_mixed_only in scored:
                head = side * 2 * pairs + 2 * pair + half
                probs = jnp.exp(scores - lse_ref[pl.ds(head, 1), cols])
                row_part = jnp.sum(probs * d_probs, axis=0, keepdims=True)
                d_scores = (probs * (d_probs - row_part)).astype(jnp.bfloat16)
                weighed.append(
                    (half, cols, probs.astype(jnp.bfloat16), d_scores, queries_only, d_mixed_only)
                )
            d_keys = d_values = None
            for half, cols, probs, d_scores, queries_only, d_mixed_only in weighed:
                value_part = forward_product(probs, d_mixed_only)
                key_part = forward_product(d_scores, queries_only)
                d_values = value_part if d_values is None else d_values + value_part
                d_keys = key_part if d_keys is None else d_keys + key_part
                lanes = slice(half * HEAD_DIM, (half + 1) * HEAD_DIM)
                dqt_ref[lanes, cols] = forward_product(keys_t[lanes], d_scores)
            for part, value in enumerate((dqt_ref[...].T * scale, d_keys, d_values)):
                at = pl.multiple_of(part * width + pair * LANES, LANES)
                rounded = value.astype(jnp.bfloat16)
                d_qkv_ref[side, :, pl.ds(at, LANES)] = rounded
                if part != 1:
                    sums_ref[side, :, pl.ds(at, LANES)] = jnp.broadcast_to(
                        jnp.sum(rounded.astype(jnp.float32), axis=0, keepdims=True), (8, LANES)
                    )
            return carry

        lax.fori_loop(0, pairs, one_pair, 0)


def attend_core_back(qkv_lo, qkv_hi, d_mixed, lse, seq_lengths):
    total, wide = qkv_lo.shape
    seqs = seq_lengths.shape[0]
    rows, width = total // seqs, 2 * wide // 3
    heads = width // HEAD_DIM
    side = pl.BlockSpec((rows, wide), lambda seq, lens: (seq, 0))
    return pl.pallas_call(
        attend_back_kernel,
        out_shape=(
            jax.ShapeDtypeStruct((2, total, wide), jnp.bfloat16),
            jax.ShapeDtypeStruct((seqs, 2, 8, wide), jnp.float32),
        ),
        grid_spec=pltpu.PrefetchScalarGridSpec(
            num_scalar_prefetch=1,
            grid=(seqs,),
            in_specs=[
                side,
                side,
                pl.BlockSpec((rows, width), lambda seq, lens: (seq, 0)),
                pl.BlockSpec((None, lse.shape[1], rows), lambda seq, lens: (seq, 0, 0)),
            ],
            out_specs=[
                pl.BlockSpec((2, rows, wide), lambda seq, lens: (0, seq, 0)),
                pl.BlockSpec((None, 2, 8, wide), lambda seq, lens: (seq, 0, 0, 0)),
            ],
            scratch_shapes=[pltpu.VMEM((LANES, rows), jnp.float32)],
        ),
        compiler_params=pltpu.CompilerParams(vmem_limit_bytes=40 << 20),
        cost_estimate=LIGHT,
        name="attend_back",
    )(seq_lengths, qkv_lo, qkv_hi, d_mixed, lse)


def half_of(rows, side):
    width = rows.shape[1] // 2
    return lax.dynamic_slice_in_dim(rows, side * width, width, 1)


def project_in(flat_low, in_layer, small_layer):
    third = flat_low.shape[1] // 2
    qkv = []
    for side in range(2):
        cols = slice(side * third, (side + 1) * third)
        bias = jnp.concatenate(
            [small_layer[0, cols], jnp.zeros((third,), jnp.float32), small_layer[1, cols]]
        )
        part = forward_product(flat_low, in_layer[side]) + bias
        qkv.append(part.astype(jnp.bfloat16))
    return qkv


def project_out(flat_rows, mixed_heads, out_layer, small_layer):
    branch = forward_product(mixed_heads, out_layer)
    return norm_forward(flat_rows + branch + small_layer[2], small_layer[3], small_layer[4])


def project_out_back(d_normed, normal_part, inv_std, out_layer, small_layer):
    d_resid, d_gain, d_shift = norm_backward(d_normed, normal_part, inv_std, small_layer[3])
    d_branch = d_resid.astype(jnp.bfloat16)
    d_out_bias = jnp.sum(d_branch.astype(jnp.float32), axis=0, keepdims=True)
    d_mixed = back_product(d_branch, out_layer).astype(jnp.bfloat16)
    return (d_resid, d_branch, d_mixed, (d_out_bias, d_gain, d_shift))


def project_in_back(d_resid, d_qkv, in_layer):
    return d_resid + sum(back_product(d_qkv[side], in_layer[side]) for side in range(2))


def attn_small(sums, sums_out):
    width = sums.shape[-1] // 3
    sums = jnp.sum(sums[:, :, :1], axis=0)
    rows = [
        jnp.concatenate([sums[side, :, start : start + width] for side in range(2)], axis=1)
        for start in (0, 2 * width)
    ]
    return rows + list(sums_out)


def attn_grads_kernel(core, x_ref, mixed_ref, d_qkv_ref, d_branch_ref, *rest):
    small_ref = rest[0] if len(rest) == 5 else None
    far_ref, own_ref, xt_ref, mixed_t_ref = rest[-4:]
    third = d_branch_ref.shape[1]

    @pl.when(pl.program_id(0) == 0)
    def _():
        xt_ref[...] = x_ref[...].T
        mixed_t_ref[...] = mixed_ref[...].T

    def fill(out_ref):
        out_ref[:, : 3 * third] = forward_product(xt_ref[...], d_qkv_ref[...]).astype(jnp.bfloat16)
        out_ref[:, 3 * third : 4 * third] = forward_product(
            mixed_t_ref[...], d_branch_ref[...]
        ).astype(jnp.bfloat16)
        if small_ref is not None:
            out_ref[:, 4 * third :] = small_ref[...].T.astype(jnp.bfloat16)

    @pl.when(pl.program_id(0) == 0)
    def _():
        fill(far_ref)

    @pl.when(pl.program_id(0) == 1)
    def _():
        fill(own_ref)


def attn_grads(core, x_low, mixed_heads, d_qkv, d_branch, small=None):
    total, width = x_low.shape
    third = width // 2
    extra = 0 if small is None else small.shape[1]

    def side(at, core):
        return jnp.where(at == 0, 1 - core[0], core[0])

    specs = [pl.BlockSpec((total, width), lambda at, core: (0, 0))] * 2 + [
        pl.BlockSpec((None, total, 3 * third), lambda at, core: (side(at, core), 0, 0)),
        pl.BlockSpec((total, third), lambda at, core: (0, side(at, core))),
    ]
    given = [x_low, mixed_heads, d_qkv, d_branch]
    if small is not None:
        specs.append(
            pl.BlockSpec((None, extra, width), lambda at, core: (side(at, core), 0, 0))
        )
        given.append(small)
    shape = jax.ShapeDtypeStruct((width, 4 * third + extra), jnp.bfloat16)
    return pl.pallas_call(
        attn_grads_kernel,
        out_shape=(shape, shape),
        grid_spec=pltpu.PrefetchScalarGridSpec(
            num_scalar_prefetch=1,
            grid=(2,),
            in_specs=specs,
            out_specs=[pl.BlockSpec(shape.shape, lambda at, core: (0, 0))] * 2,
            scratch_shapes=[pltpu.VMEM((width, total), jnp.bfloat16)] * 2,
        ),
        compiler_params=pltpu.CompilerParams(vmem_limit_bytes=36 << 20),
        cost_estimate=LIGHT,
        name="attn_grads",
    )(core.reshape(1).astype(jnp.int32), *given)


def feed_up_kernel(rows_ref, up_ref, bias_ref, act_ref, slope_ref):
    low_rows = rows_ref[...]
    for at in range(0, up_ref.shape[1], HIDDEN_BLOCK):
        cols = slice(at, at + HIDDEN_BLOCK)
        pre_act = forward_product(low_rows, up_ref[:, cols]) + bias_ref[:, cols]
        below = 0.5 * (1.0 + lax.erf(pre_act * 0.7071067811865476))
        density = jnp.exp(-0.5 * pre_act * pre_act) * 0.3989422804014327
        act_ref[:, cols] = (pre_act * below).astype(jnp.bfloat16)
        slope_ref[:, cols] = (below + pre_act * density).astype(jnp.bfloat16)


def feed_up(rows_in, up_layer, small_layer):
    rows_low = rows_in.astype(jnp.bfloat16)
    total, width = rows_low.shape
    hidden = up_layer.shape[1]
    block = math.gcd(total, 256)
    bias = small_layer[5:9].reshape(1, hidden)
    shape = jax.ShapeDtypeStruct((total, hidden), jnp.bfloat16)
    act_low, slope = pl.pallas_call(
        feed_up_kernel,
        out_shape=(shape, shape),
        grid=(total // block,),
        in_specs=[
            pl.BlockSpec((block, width), lambda at: (at, 0)),
            pl.BlockSpec((width, hidden), lambda at: (0, 0)),
            pl.BlockSpec((1, hidden), lambda at: (0, 0)),
        ],
        out_specs=[pl.BlockSpec((block, hidden), lambda at: (at, 0))] * 2,
        compiler_params=pltpu.CompilerParams(vmem_limit_bytes=32 << 20),
        cost_estimate=LIGHT,
        name="feed_up",
    )(rows_low, up_layer, bias)
    return (rows_low, act_low, slope)


def feed_down(rows_in, act_low, down_layer, small_layer):
    branch = forward_product(act_low, down_layer) + small_layer[9]
    return norm_forward(rows_in + branch, small_layer[10], small_layer[11])


def feed_down_back(d_normed, normal_part, inv_std, slope, down_layer, small_layer):
    d_resid, d_gain, d_shift = norm_backward(d_normed, normal_part, inv_std, small_layer[10])
    d_branch = d_resid.astype(jnp.bfloat16)
    d_pre = (back_product(d_branch, down_layer) * slope.astype(jnp.float32)).astype(jnp.bfloat16)
    model_width = d_resid.shape[1]
    d_bias = jnp.sum(d_pre.astype(jnp.float32), axis=0, keepdims=True)
    small_rows = [
        d_bias[:, part * model_width : (part + 1) * model_width] for part in range(4)
    ] + [jnp.sum(d_branch.astype(jnp.float32), axis=0, keepdims=True), d_gain, d_shift]
    return (d_resid, d_branch, d_pre, small_rows)


def norm_back_rows(d_out, xhat, inv, gain):
    d_normal = d_out * gain
    d_resid = inv * (
        d_normal
        - jnp.mean(d_normal, axis=-1, keepdims=True)
        - xhat * jnp.mean(d_normal * xhat, axis=-1, keepdims=True)
    )
    return (d_resid, d_resid.astype(jnp.bfloat16))


def add_sums(sums_ref, values):
    width = values[0].shape[1]
    first = pl.program_id(0) == 0
    for number, value in enumerate(values):
        cols = slice(number * width, (number + 1) * width)
        part = jnp.broadcast_to(jnp.sum(value, axis=0, keepdims=True), (8, width))
        sums_ref[:, cols] = jnp.where(first, part, part + sums_ref[:, cols])


def layer_back_kernel(
    d_resid_ref, d_qkv_ref, in_ref, xhat_ref, inv_ref, gain_ref, down_ref, slope_ref, *outs
):
    out_resid_ref, d_branch_ref, d_pre_ref, pre_sums_ref, sums_ref = outs
    d_out = d_resid_ref[...]
    for side in range(2):
        d_out = d_out + back_product(d_qkv_ref[side], in_ref[side])
    xhat = xhat_ref[...]
    d_resid, d_branch = norm_back_rows(d_out, xhat, inv_ref[:, :1], gain_ref[...])
    out_resid_ref[...] = d_resid
    d_branch_ref[...] = d_branch
    add_sums(sums_ref, (d_branch.astype(jnp.float32), d_out * xhat, d_out))
    first = pl.program_id(0) == 0
    for at in range(0, down_ref.shape[0], HIDDEN_BLOCK):
        cols = slice(at, at + HIDDEN_BLOCK)
        d_act = back_product(d_branch, down_ref[cols])
        d_pre = (d_act * slope_ref[:, cols].astype(jnp.float32)).astype(jnp.bfloat16)
        d_pre_ref[:, cols] = d_pre
        part = jnp.broadcast_to(
            jnp.sum(d_pre.astype(jnp.float32), axis=0, keepdims=True), (8, HIDDEN_BLOCK)
        )
        pre_sums_ref[:, cols] = jnp.where(first, part, part + pre_sums_ref[:, cols])


def layer_back(d_resid, d_qkv, in_layer, xhat, inv, small_layer, down_layer, slope):
    total, width = d_resid.shape
    hidden = slope.shape[1]
    wide = d_qkv.shape[2]
    block = math.gcd(total, 256)
    row = pl.BlockSpec((block, width), lambda at: (at, 0))
    hidden_row = pl.BlockSpec((block, hidden), lambda at: (at, 0))
    d_resid, d_branch, d_pre, pre_sums, sums = pl.pallas_call(
        layer_back_kernel,
        out_shape=(
            jax.ShapeDtypeStruct((total, width), jnp.float32),
            jax.ShapeDtypeStruct((total, width), jnp.bfloat16),
            jax.ShapeDtypeStruct((total, hidden), jnp.bfloat16),
            jax.ShapeDtypeStruct((8, hidden), jnp.float32),
            jax.ShapeDtypeStruct((8, 3 * width), jnp.float32),
        ),
        grid=(total // block,),
        in_specs=[
            row,
            pl.BlockSpec((2, block, wide), lambda at: (0, at, 0)),
            pl.BlockSpec((2, width, wide), lambda at: (0, 0, 0), pipeline_mode=pl.Buffered(1)),
            row,
            pl.BlockSpec((block, LANES), lambda at: (at, 0)),
            pl.BlockSpec((1, width), lambda at: (0, 0)),
            pl.BlockSpec((hidden, width), lambda at: (0, 0), pipeline_mode=pl.Buffered(1)),
            hidden_row,
        ],
        out_specs=[
            row,
            row,
            hidden_row,
            pl.BlockSpec((8, hidden), lambda at: (0, 0)),
            pl.BlockSpec((8, 3 * width), lambda at: (0, 0)),
        ],
        compiler_params=pltpu.CompilerParams(vmem_limit_bytes=30 << 20),
        cost_estimate=LIGHT,
        name="layer_back",
    )(d_resid, d_qkv, in_layer, xhat, inv, small_layer[10:11], down_layer, slope)
    small_rows = [pre_sums[:1, part * width : (part + 1) * width] for part in range(4)]
    small_rows += [sums[:1, part * width : (part + 1) * width] for part in range(3)]
    return (d_resid, d_branch, d_pre, small_rows)


def feed_back_kernel(d_resid_ref, d_pre_ref, up_ref, xhat_ref, inv_ref, gain_ref, out_ref, *outs):
    out_resid_ref, d_branch_ref, d_mixed_ref, sums_ref = outs
    d_out = d_resid_ref[...] + back_product(d_pre_ref[...], up_ref[...])
    xhat = xhat_ref[...]
    d_resid, d_branch = norm_back_rows(d_out, xhat, inv_ref[:, :1], gain_ref[...])
    out_resid_ref[...] = d_resid
    d_branch_ref[...] = d_branch
    d_mixed_ref[...] = back_product(d_branch, out_ref[...]).astype(jnp.bfloat16)
    add_sums(sums_ref, (d_branch.astype(jnp.float32), d_out * xhat, d_out))


def feed_back(d_resid, d_pre, up_layer, xhat, inv, small_layer, out_layer):
    total, width = d_resid.shape
    hidden = d_pre.shape[1]
    block = math.gcd(total, 256)
    row = pl.BlockSpec((block, width), lambda at: (at, 0))
    d_resid, d_branch, d_mixed, sums = pl.pallas_call(
        feed_back_kernel,
        out_shape=(
            jax.ShapeDtypeStruct((total, width), jnp.float32),
            jax.ShapeDtypeStruct((total, width), jnp.bfloat16),
            jax.ShapeDtypeStruct((total, width), jnp.bfloat16),
            jax.ShapeDtypeStruct((8, 3 * width), jnp.float32),
        ),
        grid=(total // block,),
        in_specs=[
            row,
            pl.BlockSpec((block, hidden), lambda at: (at, 0)),
            pl.BlockSpec((width, hidden), lambda at: (0, 0), pipeline_mode=pl.Buffered(1)),
            row,
            pl.BlockSpec((block, LANES), lambda at: (at, 0)),
            pl.BlockSpec((1, width), lambda at: (0, 0)),
            pl.BlockSpec((width, width), lambda at: (0, 0), pipeline_mode=pl.Buffered(1)),
        ],
        out_specs=[row, row, row, pl.BlockSpec((8, 3 * width), lambda at: (0, 0))],
        compiler_params=pltpu.CompilerParams(vmem_limit_bytes=24 << 20),
        cost_estimate=LIGHT,
        name="feed_back",
    )(d_resid, d_pre, up_layer, xhat, inv, small_layer[3:4], out_layer)
    sums_out = [sums[:1, part * width : (part + 1) * width] for part in range(3)]
    return (d_resid, d_branch, d_mixed, sums_out)


def order_attn_kernel(core_ref, *refs):
    pairs, out_ref = (refs[:2], refs[2:4]), refs[4]
    third = out_ref.shape[3] // 2
    core = core_ref[0]
    for layer, (own_ref, far_ref) in enumerate(pairs):
        for part in range(4):
            cols = slice(part * third, (part + 1) * third)
            own, far = own_ref[:, cols], far_ref[:, cols]
            for side in range(2):
                out_ref[layer, part, :, side * third : (side + 1) * third] = jnp.where(
                    core == side, own, far
                )


def order_attn(core, one, two, width):
    local = pl.BlockSpec(memory_space=pltpu.VMEM)
    shard = one[0].shape[0]
    return pl.pallas_call(
        order_attn_kernel,
        out_shape=jax.ShapeDtypeStruct((2, 4, shard, width), jnp.bfloat16),
        grid_spec=pltpu.PrefetchScalarGridSpec(
            num_scalar_prefetch=1, grid=(), in_specs=[local] * 4, out_specs=local
        ),
        cost_estimate=LIGHT,
        name="order_attn",
    )(core.reshape(1).astype(jnp.int32), *one, *two)


def feed_grads_kernel(shard, core, low_ref, d_pre_ref, act_ref, d_branch_ref, *rest):
    far_ref, own_ref, low_t_ref, down_ref = rest
    at = pl.program_id(0)
    width = low_ref.shape[1]
    third = width // 2

    @pl.when(at == 0)
    def _():
        low_t_ref[...] = low_ref[...].T

    for step in range(4):

        @pl.when(at == step)
        def _(step=step):
            out_ref = far_ref if step < 2 else own_ref
            cols = slice((step % 2) * width, (step % 2 + 1) * width)
            out_ref[:, cols] = forward_product(low_t_ref[...], d_pre_ref[...]).astype(jnp.bfloat16)

    @pl.when(at >= 4)
    def _():
        down_ref[...] = weight_grad(act_ref[...], d_branch_ref[...])
        blocks = width // (4 * shard)
        for out_ref, side in ((far_ref, 1 - core[0]), (own_ref, core[0])):
            from_cols = pl.ds(pl.multiple_of(side * third, LANES), third)
            for block in range(blocks):
                row = pl.multiple_of(((at - 4) * blocks + block) * shard, 16)
                for part in range(4):
                    start = (block * 4 + part) * shard
                    cols = slice(2 * width + part * third, 2 * width + (part + 1) * third)
                    out_ref[pl.ds(row, shard), cols] = down_ref[
                        start : start + shard, from_cols
                    ].astype(jnp.bfloat16)


def feed_grads_plain(core, rows_low, d_pre, act_low, d_branch, shard):
    sides = []
    width = rows_low.shape[1]
    for side in (1 - core, core):
        d_up = weight_grad(rows_low, half_of(d_pre, side))
        d_down = weight_grad(act_low, half_of(d_branch, side))
        d_down = d_down.reshape(-1, 4, shard, width // 2).transpose(0, 2, 1, 3)
        sides.append(jnp.concatenate([d_up, d_down.reshape(width, -1)], axis=1))
    return [part.astype(jnp.bfloat16) for part in sides]


def feed_grads(core, rows_low, d_pre, act_low, d_branch, shard):
    total, width = rows_low.shape
    hidden = act_low.shape[1]
    if shard % 16 or hidden != 4 * width:
        return feed_grads_plain(core, rows_low, d_pre, act_low, d_branch, shard)

    def pre_at(at, core):
        step = jnp.minimum(at, 3)
        return (0, jnp.where(step < 2, 1 - core[0], core[0]) * 2 + step % 2)

    shape = jax.ShapeDtypeStruct((width, hidden), jnp.bfloat16)
    return pl.pallas_call(
        functools.partial(feed_grads_kernel, shard),
        out_shape=(shape, shape),
        grid_spec=pltpu.PrefetchScalarGridSpec(
            num_scalar_prefetch=1,
            grid=(8,),
            in_specs=[
                pl.BlockSpec((total, width), lambda at, core: (0, 0)),
                pl.BlockSpec((total, width), pre_at),
                pl.BlockSpec((total, width), lambda at, core: (0, jnp.maximum(at - 4, 0))),
                pl.BlockSpec((total, width), lambda at, core: (0, 0)),
            ],
            out_specs=[pl.BlockSpec((width, hidden), lambda at, core: (0, 0))] * 2,
            scratch_shapes=[
                pltpu.VMEM((width, total), jnp.bfloat16),
                pltpu.VMEM((width, width), jnp.float32),
            ],
        ),
        compiler_params=pltpu.CompilerParams(vmem_limit_bytes=40 << 20),
        cost_estimate=LIGHT,
        name="feed_grads",
    )(core.reshape(1).astype(jnp.int32), rows_low, d_pre, act_low, d_branch)


def row_select(token_mask, capacity):
    flat_mask = token_mask.reshape(1, -1)
    row_total = flat_mask.shape[1]
    before = (
        lax.broadcasted_iota(jnp.int32, (row_total, row_total), 0)
        < lax.broadcasted_iota(jnp.int32, (row_total, row_total), 1)
    ).astype(jnp.bfloat16)
    rank = forward_product(flat_mask.astype(jnp.bfloat16), before).astype(jnp.int32)
    slots = lax.broadcasted_iota(jnp.int32, (capacity, row_total), 0)
    return ((slots == rank) & (flat_mask == 1)).astype(jnp.bfloat16)


def split_low(wide, parts):
    pieces = []
    left = wide
    for _ in range(parts - 1):
        piece = lax.reduce_precision(left, 8, 7)
        pieces.append(piece.astype(jnp.bfloat16))
        left = left - piece
    pieces.append(left.astype(jnp.bfloat16))
    return jnp.concatenate(pieces, axis=1)


def join_low(joined, parts):
    width = joined.shape[1] // parts
    total = joined[:, :width]
    for number in range(1, parts):
        total = total + joined[:, number * width : (number + 1) * width]
    return total


def adam_update(
    master, first_moment, second_moment, gradient, clip_scale, step_value, decay_rate, rate_value
):
    clipped = gradient.astype(jnp.float32) * clip_scale
    first_new = BETA_FIRST * first_moment + (1.0 - BETA_FIRST) * clipped
    second_new = BETA_SECOND * second_moment + (1.0 - BETA_SECOND) * clipped * clipped
    first_hat = first_new / (1.0 - jnp.power(BETA_FIRST, step_value))
    second_hat = second_new / (1.0 - jnp.power(BETA_SECOND, step_value))
    master_new = master - rate_value * (
        first_hat / (jnp.sqrt(second_hat) + ADAM_EPS) + decay_rate * master
    )
    return (master_new, first_new, second_new, master_new.astype(jnp.bfloat16))


def routes(peers):
    bits = peers.bit_length() - 1
    deep = min(2, bits)
    rest = bits - deep
    x_bits = [1 << at for at in range(rest - rest // 2)]
    y_bits = [1 << at for at in range(rest - rest // 2, rest)]
    z_bits = [1 << at for at in range(rest, bits)]
    if len(x_bits) == len(y_bits):
        return ((z_bits, y_bits, x_bits), (z_bits, x_bits, y_bits))
    return ((z_bits, y_bits, x_bits), (z_bits, y_bits, x_bits))


def stage_sizes(peers):
    return [1 << len(bits) for bits in routes(peers)[0]]


def mask_of(bits, turn):
    return sum(bit for at, bit in enumerate(bits) if turn >> at & 1)


def shift(value, stage, turn, peers):
    pairs = []
    for core, path in enumerate(routes(peers)):
        mask = mask_of(path[stage], turn)
        pairs += [(core * peers + at, core * peers + (at ^ mask)) for at in range(peers)]
    return lax.ppermute(value, ("dp", "bal"), pairs)


def swap(value):
    return lax.ppermute(value, "dp", [(0, 1), (1, 0)])


def place_table(peers, core):
    masks = [
        [mask_of(sum(path, []), spot) for spot in range(peers)] for path in routes(peers)
    ]
    masks = jnp.asarray(np.array(masks, np.int32))
    mine = lax.axis_index("bal")
    own = jnp.where(core == 0, masks[0], masks[1])
    far = jnp.where(core == 0, masks[1], masks[0])
    return jnp.concatenate([mine ^ own, mine ^ far, core.reshape(1).astype(jnp.int32)])


def place_kernel(plan, count, spots, *refs):
    parts, outs = refs[:count], refs[count:]
    held, rows, _ = parts[0].shape
    core = spots[count * held]

    for number, part in enumerate(parts):
        side = core if number < count // 2 else 1 - core

        def one_block(at, carry, number=number, part=part, side=side):
            spot = spots[number * held + at]
            for (start, width, kind), out in zip(plan, outs):
                cols = pl.ds(pl.multiple_of(side * width, LANES), width)
                if kind == "stack":
                    out[side, spot] = part[at, :, start : start + width]
                elif kind == "wide":
                    out[spot, :, cols] = part[at, :, start : start + width]
                else:
                    for piece in range(4):
                        begin = start + piece * width
                        out[spot, piece * rows : (piece + 1) * rows, cols] = part[
                            at, :, begin : begin + width
                        ]
            return carry

        lax.fori_loop(0, held, one_block, 0)


def place(spots, parts, plan):
    held, rows, whole = parts[0].shape
    peers = len(parts) * held // 2
    kinds = [
        (start, 4 * width, "stack") if kind == "down" and rows % 16 else (start, width, kind)
        for start, width, kind in plan
    ]
    shapes = {
        "stack": lambda width: (2, peers, rows, width),
        "wide": lambda width: (peers, rows, 2 * width),
        "down": lambda width: (peers, 4 * rows, 2 * width),
    }
    local = pl.BlockSpec(memory_space=pltpu.VMEM)
    placed = pl.pallas_call(
        functools.partial(place_kernel, kinds, len(parts)),
        out_shape=[
            jax.ShapeDtypeStruct(shapes[kind](width), parts[0].dtype) for _, width, kind in kinds
        ],
        grid_spec=pltpu.PrefetchScalarGridSpec(
            num_scalar_prefetch=1,
            grid=(),
            in_specs=[local] * len(parts),
            out_specs=[local] * len(kinds),
        ),
        compiler_params=pltpu.CompilerParams(vmem_limit_bytes=40 << 20),
        cost_estimate=LIGHT,
        name="place",
    )(spots, *parts)
    results = []
    for part, (_, width, kind), (_, _, asked) in zip(placed, kinds, plan):
        if kind != asked:
            part = part.reshape(2, peers, rows, 4, width // 4).transpose(1, 3, 2, 0, 4)
            results.append(part.reshape(peers * rows * 4, width // 2))
        elif kind == "stack":
            results.append(part.reshape(2, peers * rows, width))
        else:
            results.append(part.reshape(-1, 2 * width))
    return results


class Gather:
    def __init__(self, mine, spots, peers, plan):
        self.kept, self.moved = [mine[None]], []
        self.spots, self.peers, self.plan = spots, peers, plan
        self.sizes = stage_sizes(peers)
        self.stage, self.turn = 0, 1

    def done(self):
        return self.stage > len(self.sizes)

    def launch(self, count):
        if self.stage == len(self.sizes):
            return [swap(part) for part in self.kept]
        stop = self.sizes[self.stage]
        stop = stop if count is None else min(stop, self.turn + count)
        turns = range(self.turn, stop)
        self.turn = stop
        return [shift(self.kept[0], self.stage, turn, self.peers) for turn in turns]

    def land(self, moved):
        self.moved += moved
        if self.stage < len(self.sizes) and len(self.moved) < self.sizes[self.stage] - 1:
            return
        whole = self.kept + self.moved
        if self.stage < len(self.sizes) - 1:
            whole = [jnp.concatenate(whole, axis=0)]
        self.kept, self.moved = whole, []
        self.stage, self.turn = self.stage + 1, 1

    def result(self):
        return place(self.spots, self.kept, self.plan)


class Scatter:
    def __init__(self, far, own, spots, peers):
        self.kept = [grads.reshape(peers, -1, grads.shape[1]) for grads in (own, far)]
        self.moved = []
        self.spots, self.peers = spots, peers
        self.sizes = stage_sizes(peers)
        self.stage, self.turn = len(self.sizes), 1

    def done(self):
        return self.stage < 0

    def launch(self, count):
        if self.stage == len(self.sizes):
            return [swap(self.kept[1])]
        stop = self.sizes[self.stage]
        stop = stop if count is None else min(stop, self.turn + count)
        turns = range(self.turn, stop)
        self.turn = stop
        return [shift(self.kept[turn], self.stage, turn, self.peers) for turn in turns]

    def land(self, moved):
        self.moved += moved
        if self.stage == len(self.sizes):
            self.kept = list(fold(self.spots, self.kept[0], self.moved[0], self.sizes[-1]))
        else:
            if len(self.moved) < self.sizes[self.stage] - 1:
                return
            pieces = self.sizes[self.stage - 1] if self.stage else 1
            size = self.kept[0].shape[0] // pieces

            def total(at):
                rows = slice(at * size, (at + 1) * size)
                adds = [part[rows].astype(jnp.float32) for part in [self.kept[0]] + self.moved]
                return sum(adds[1:], adds[0]).astype(jnp.bfloat16)

            self.kept = [total(at) for at in range(pieces)]
        self.moved = []
        self.stage, self.turn = self.stage - 1, 1

    def result(self):
        return self.kept[0][0]


class Lanes:
    def __init__(self):
        self.flying = {}

    def launch(self, *moves):
        for move in moves:
            move, count = move if isinstance(move, tuple) else (move, None)
            if not move.done():
                self.flying[move] = self.flying.get(move, []) + move.launch(count)

    def meet(self, work, *landing, ready=()):
        moves = [move for move in landing if move in self.flying]
        flown = [self.flying.pop(move) for move in moves]
        waiting = [move.kept for move in ready]
        work, flown, waiting = lax.optimization_barrier((work, flown, waiting))
        for move, moved in zip(moves, flown):
            move.land(moved)
        for move, kept in zip(ready, waiting):
            move.kept = kept
        return work

    def settle(self, work, *moves):
        return self.meet(work, ready=moves)

    def finish(self, work, *moves):
        work = self.meet(work, *moves)
        while not all(move.done() for move in moves):
            self.launch(*moves)
            work = self.meet(work, *moves)
        return work


def fold_kernel(spots, own, far, *outs):
    held = outs[0].shape[0]

    def one_block(at, carry):
        for number, out in enumerate(outs):
            spot = spots[number * held + at]
            out[at] = (own[spot].astype(jnp.float32) + far[spot].astype(jnp.float32)).astype(
                out.dtype
            )
        return carry

    lax.fori_loop(0, held, one_block, 0)


def fold(spots, own, far, pieces):
    peers, rows, width = own.shape
    shape = jax.ShapeDtypeStruct((peers // pieces, rows, width), own.dtype)
    local = pl.BlockSpec(memory_space=pltpu.VMEM)
    return pl.pallas_call(
        fold_kernel,
        out_shape=[shape] * pieces,
        grid_spec=pltpu.PrefetchScalarGridSpec(
            num_scalar_prefetch=1,
            grid=(),
            in_specs=[local, local],
            out_specs=[local] * pieces,
        ),
        compiler_params=pltpu.CompilerParams(vmem_limit_bytes=32 << 20),
        cost_estimate=LIGHT,
        name="fold",
    )(spots, own, far)


def both_sides(own, other, core):
    return (jnp.where(core == 0, own, other), jnp.where(core == 0, other, own))


def per_device(
    tokens,
    cotangent,
    seq_lengths,
    token_mask,
    step_count,
    attn_master,
    attn_first,
    attn_second,
    up_master,
    up_first,
    up_second,
    down_master,
    down_first,
    down_second,
    small_master,
    small_first,
    small_second,
):
    core = lax.axis_index("dp")
    peers = lax.axis_size("bal")
    seq_count, length, model_width = tokens.shape
    rows_total = seq_count * length
    spots = place_table(peers, core)
    shard = attn_master.shape[2]
    attn_half = lax.dynamic_slice_in_dim(attn_master, core * (model_width // 2), model_width // 2, 3)
    attn_half = attn_half.astype(jnp.bfloat16).transpose(0, 2, 1, 3).reshape(2, shard, -1)
    small_half = lax.dynamic_slice_in_dim(small_master.reshape(24, shard), core * 12, 12, 0)
    small_half = jnp.pad(small_half.astype(jnp.bfloat16).T, ((0, 0), (0, LANES - 12)))
    wide = attn_half.shape[2]
    lanes = Lanes()
    third = model_width // 2
    hidden_half = up_master.shape[2] // 2

    def down_half(layer):
        half = half_of(down_master[layer], core).astype(jnp.bfloat16)
        return [half[part * shard : (part + 1) * shard] for part in range(4)]

    up_half = [half_of(up_master[layer], core).astype(jnp.bfloat16) for layer in range(2)]
    in_one = Gather(
        jnp.concatenate([attn_half[0, :, : 3 * third], small_half], axis=1),
        spots,
        peers,
        [(0, 3 * third, "stack"), (3 * third, LANES, "stack")],
    )
    out_up_one = Gather(
        jnp.concatenate([attn_half[0, :, 3 * third :], up_half[0]], axis=1),
        spots,
        peers,
        [(0, third, "wide"), (third, hidden_half, "wide")],
    )
    down_one = Gather(
        jnp.concatenate(down_half(0), axis=1), spots, peers, [(0, third, "down")]
    )
    attn_two = Gather(
        attn_half[1], spots, peers, [(0, 3 * third, "stack"), (3 * third, third, "wide")]
    )
    up_two = Gather(up_half[1], spots, peers, [(0, hidden_half, "wide")])
    down_two = Gather(
        jnp.concatenate(down_half(1), axis=1), spots, peers, [(0, third, "down")]
    )
    flat_low = tokens.reshape(rows_total, model_width)
    cot_flat = cotangent.reshape(rows_total, model_width)
    select_rows = row_select(token_mask, MCAP)
    flat_mask = token_mask.reshape(-1, 1) == 1

    lanes.launch(in_one)
    lanes.meet((), in_one, ready=(out_up_one,))
    lanes.launch(in_one, (out_up_one, 2))
    lanes.meet((), in_one, out_up_one)
    lanes.launch(in_one, out_up_one)
    lanes.meet((), in_one, out_up_one, ready=(down_one,))
    lanes.launch(in_one, out_up_one, (down_one, 2))
    lanes.finish((), in_one)
    w_in_one, small_rows = in_one.result()
    small_vals = small_rows[:, :, :12].transpose(0, 2, 1).astype(jnp.float32)
    qkv_one = project_in(flat_low, w_in_one, small_vals[0])
    qkv_one = lanes.meet(qkv_one, out_up_one, down_one, ready=(attn_two,))
    lanes.launch(out_up_one, down_one, (attn_two, 2))
    attended = attend_core(qkv_one[0], qkv_one[1], seq_lengths)
    attended = lanes.meet(attended, out_up_one, down_one, attn_two, ready=(up_two,))
    lanes.launch(out_up_one, down_one, attn_two)
    mixed_one, lse_one = lanes.finish(attended, out_up_one)
    w_out_one, w_up_one = out_up_one.result()
    attended_one = project_out(flat_low.astype(jnp.float32), mixed_one, w_out_one, small_vals[0])
    attended_one = lanes.meet(attended_one, down_one, attn_two, ready=(down_two,))
    attended_one, attn_xhat_one, attn_inv_one = attended_one
    lanes.launch(down_one, attn_two, (up_two, 2))
    act_one = feed_up(attended_one, w_up_one, small_vals[0])
    act_one = lanes.meet(act_one, down_one, attn_two, up_two)
    lanes.launch(down_one, attn_two, up_two, (down_two, 1))
    low_one, act_one, slope_one = lanes.finish(act_one, down_one)
    attn_inv_one = jnp.broadcast_to(attn_inv_one, (rows_total, LANES))
    (w_down_one,) = down_one.result()
    layer_one = feed_down(attended_one, act_one, w_down_one, small_vals[0])
    layer_one = lanes.meet(layer_one, attn_two, up_two, down_two)
    lanes.launch(attn_two, up_two, down_two)
    layer_one, feed_xhat_one, feed_inv_one = lanes.finish(layer_one, attn_two)
    w_in_two, w_out_two = attn_two.result()
    feed_inv_one = jnp.broadcast_to(feed_inv_one, (rows_total, LANES))
    w_in_two, w_out_two = lanes.meet((w_in_two, w_out_two), up_two, down_two)
    lanes.launch(up_two, down_two)
    layer_low = layer_one.astype(jnp.bfloat16)
    qkv_two = project_in(layer_low, w_in_two, small_vals[1])
    attended = attend_core(qkv_two[0], qkv_two[1], seq_lengths)
    mixed_two, lse_two = lanes.meet(attended, up_two, down_two)
    lanes.launch(up_two, down_two)
    attended_two = project_out(layer_one, mixed_two, w_out_two, small_vals[1])
    attended_two, attn_xhat_two, attn_inv_two = attended_two
    rows_in = join_low(forward_product(select_rows, split_low(attended_two, 3)), 3)
    d_rows_out = forward_product(select_rows, cot_flat)
    rows_in = lanes.finish(rows_in, up_two)
    rows_in = lanes.meet(rows_in, down_two)
    lanes.launch(down_two)
    (w_up_two,) = up_two.result()
    rows_low, act_two, slope_two = feed_up(rows_in, w_up_two, small_vals[1])
    rows_low, act_two, slope_two = lanes.finish((rows_low, act_two, slope_two), down_two)
    (w_down_two,) = down_two.result()
    out_rows, feed_xhat_two, feed_inv_two = feed_down(rows_in, act_two, w_down_two, small_vals[1])
    d_resid, d_branch, d_pre, feed_small_two = feed_down_back(
        d_rows_out, feed_xhat_two, feed_inv_two, slope_two, w_down_two, small_vals[1]
    )
    grads = feed_grads(core, rows_low, d_pre, act_two, d_branch, shard)
    grads, d_resid, d_pre = lanes.meet((grads, d_resid, d_pre))
    g_feed_two = Scatter(*grads, spots, peers)
    lanes.launch(g_feed_two)
    d_in_rows = d_resid + back_product(d_pre, w_up_two)
    d_attended_two = jnp.where(
        flat_mask,
        join_low(weight_grad(select_rows, split_low(d_in_rows, 2)), 2),
        cot_flat.astype(jnp.float32),
    )
    back = project_out_back(d_attended_two, attn_xhat_two, attn_inv_two, w_out_two, small_vals[1])
    d_resid, d_branch, d_mixed, sums_out = lanes.meet(back, g_feed_two)
    lanes.launch(g_feed_two)
    back = attend_core_back(qkv_two[0], qkv_two[1], d_mixed, lse_two, seq_lengths)
    d_qkv, sums = back
    grads = attn_grads(core, layer_low, mixed_two, d_qkv, d_branch)
    grads, d_resid, d_qkv = lanes.meet((grads, d_resid, d_qkv), g_feed_two)
    attn_small_two = attn_small(sums, sums_out)
    g_attn_two = Scatter(*grads, spots, peers)
    d_resid = lanes.settle(d_resid, g_feed_two)
    lanes.launch(g_feed_two, g_attn_two)
    back = layer_back(
        d_resid,
        d_qkv,
        w_in_two,
        feed_xhat_one,
        feed_inv_one,
        small_vals[0],
        w_down_one,
        slope_one,
    )
    d_resid, d_branch, d_pre, feed_small_one = lanes.meet(back, g_attn_two, g_feed_two)
    d_branch = lanes.settle(d_branch, g_attn_two, g_feed_two)
    lanes.launch(g_attn_two, (g_feed_two, 2))
    grads = feed_grads(core, low_one, d_pre, act_one, d_branch, shard)
    grads, d_resid, d_pre = lanes.meet((grads, d_resid, d_pre), g_attn_two, g_feed_two)
    g_feed_one = Scatter(*grads, spots, peers)
    d_pre = lanes.settle(d_pre, g_attn_two)
    lanes.launch(g_feed_one, g_attn_two)
    back = feed_back(
        d_resid, d_pre, w_up_one, attn_xhat_one, attn_inv_one, small_vals[0], w_out_one
    )
    d_resid, d_branch, d_mixed, sums_out = lanes.meet(back, g_feed_one, g_attn_two)
    d_mixed = lanes.settle(d_mixed, g_feed_one, g_attn_two)
    lanes.launch(g_feed_one, (g_attn_two, 2), g_feed_two)
    back = attend_core_back(qkv_one[0], qkv_one[1], d_mixed, lse_one, seq_lengths)
    d_qkv, sums = lanes.meet(back, g_feed_one, g_attn_two, g_feed_two)
    d_qkv, sums, d_branch = lanes.settle((d_qkv, sums, d_branch), g_feed_one, g_attn_two)
    lanes.launch(g_feed_one, g_attn_two)
    attn_small_one = attn_small(sums, sums_out)
    small_pad = [jnp.zeros((LANES - 12, model_width), jnp.float32)]
    small_grads = jnp.stack(
        [
            jnp.concatenate(attn_small_one + feed_small_one + small_pad, axis=0),
            jnp.concatenate(attn_small_two + feed_small_two + small_pad, axis=0),
        ]
    )
    grads = attn_grads(core, flat_low, mixed_one, d_qkv, d_branch, small_grads)
    grads, d_resid, d_qkv, attended_two, out_rows = lanes.meet(
        (grads, d_resid, d_qkv, attended_two, out_rows), g_feed_one, g_attn_two
    )
    g_attn_one = Scatter(*grads, spots, peers)
    lanes.launch(g_attn_one)
    lanes.meet((), g_attn_one)
    lanes.launch(g_attn_one, (g_feed_one, 2))
    d_tokens = project_in_back(d_resid, d_qkv, w_in_one).astype(jnp.bfloat16)
    d_tokens, attended_two, out_rows = lanes.meet(
        (d_tokens, attended_two, out_rows), g_attn_one, g_feed_one
    )
    lanes.launch(g_attn_one, g_feed_one)
    output_flat = jnp.where(
        flat_mask,
        weight_grad(select_rows, out_rows.astype(jnp.bfloat16)),
        attended_two,
    ).astype(jnp.bfloat16)
    output_flat = lanes.meet(output_flat, g_attn_one, g_feed_one)
    lanes.launch(g_attn_one)
    lanes.finish((), g_feed_one, g_attn_two, g_feed_two, g_attn_one)
    owned = {
        "attn0": g_attn_one.result(),
        "feed0": g_feed_one.result(),
        "attn1": g_attn_two.result(),
        "feed1": g_feed_two.result(),
    }
    partial_squares = sum(jnp.sum(jnp.square(owned[name].astype(jnp.float32))) for name in owned)
    raw = {name: (owned[name], swap(owned[name])) for name in owned}
    both = {name: both_sides(*raw[name], core) for name in raw}

    def joined(name, start, width):
        return jnp.concatenate([part[:, start : start + width] for part in both[name]], axis=1)

    def down_rows(name):
        return jnp.concatenate(
            [joined(name, hidden_half + part * third, third) for part in range(4)], axis=0
        )

    reduced = (
        order_attn(core, raw["attn0"], raw["attn1"], model_width),
        jnp.stack([joined(name, 0, hidden_half) for name in ("feed0", "feed1")]).astype(
            jnp.float32
        ),
        jnp.stack([down_rows(name) for name in ("feed0", "feed1")]),
        jnp.stack([part[:, wide : wide + 12].T for part in both["attn0"]]),
    )
    partial_squares = partial_squares.reshape(1, 1)
    partial_squares = partial_squares + swap(partial_squares)
    hops = [
        (stage, 1 << at)
        for stage, bits in enumerate(routes(peers)[0])
        for at in range(len(bits))
    ]
    for stage, turn in hops[:-1]:
        partial_squares = partial_squares + shift(partial_squares, stage, turn, peers)
    reduced, partial_squares = lax.optimization_barrier((reduced, partial_squares))
    moved = shift(partial_squares, *hops[-1], peers)
    square_total = (partial_squares + moved)[0, 0]
    grad_norm = jnp.sqrt(square_total).reshape(1)
    clip_scale = jnp.minimum(1.0, CLIP_NORM / (grad_norm[0] + 1e-06))
    step_value = step_count[0].astype(jnp.float32)
    attn_new = adam_update(
        attn_master,
        attn_first,
        attn_second,
        reduced[0],
        clip_scale,
        step_value,
        WEIGHT_DECAY,
        LEARN_RATE,
    )
    up_new = adam_update(
        up_master, up_first, up_second, reduced[1], clip_scale, step_value, WEIGHT_DECAY, LEARN_RATE
    )
    down_new = adam_update(
        down_master,
        down_first,
        down_second,
        reduced[2],
        clip_scale,
        step_value,
        WEIGHT_DECAY,
        LEARN_RATE,
    )
    small_new = adam_update(
        small_master, small_first, small_second, reduced[3], clip_scale, step_value, 0.0, SMALL_RATE
    )
    output = output_flat.reshape(seq_count, length, model_width)
    input_grad = d_tokens.reshape(seq_count, length, model_width)
    return (output, input_grad, grad_norm) + attn_new + up_new + down_new + small_new


def solution(mesh):
    return jax.shard_map(
        per_device,
        mesh=mesh,
        in_specs=(
            P(("dp", "bal"), None, None),
            P(("dp", "bal"), None, None),
            P(("dp", "bal")),
            P(("dp", "bal"), None),
            P(),
            P(None, None, "bal", None),
            P(None, None, "bal", None),
            P(None, None, "bal", None),
            P(None, "bal", None),
            P(None, "bal", None),
            P(None, "bal", None),
            P(None, "bal", None),
            P(None, "bal", None),
            P(None, "bal", None),
            P(None, None, "bal"),
            P(None, None, "bal"),
            P(None, None, "bal"),
        ),
        out_specs=(
            P(("dp", "bal"), None, None),
            P(("dp", "bal"), None, None),
            P(),
            P(None, None, "bal", None),
            P(None, None, "bal", None),
            P(None, None, "bal", None),
            P(None, None, "bal", None),
            P(None, "bal", None),
            P(None, "bal", None),
            P(None, "bal", None),
            P(None, "bal", None),
            P(None, "bal", None),
            P(None, "bal", None),
            P(None, "bal", None),
            P(None, "bal", None),
            P(None, None, "bal"),
            P(None, None, "bal"),
            P(None, None, "bal"),
            P(None, None, "bal"),
        ),
        check_vma=False,
    )
```

```python
import functools
import math

import jax
import jax.numpy as jnp
import numpy as np
from jax import lax
from jax.experimental import pallas as pl
from jax.experimental.pallas import tpu as pltpu
from jax.sharding import PartitionSpec as P

HEADS = 12
HEAD_DIM = 64
MCAP = 384
LANES = 128
QUERY_BLOCK = 256
HIDDEN_BLOCK = 512
LIGHT = pl.CostEstimate(flops=3000000000, bytes_accessed=8000000, transcendentals=0)


LN_EPS = 1e-06
NEG_FILL = -1000000000.0
CLIP_NORM = 1.0
LEARN_RATE = 0.05
SMALL_RATE = 0.25
BETA_FIRST = 0.9
BETA_SECOND = 0.999
ADAM_EPS = 1e-08
WEIGHT_DECAY = 0.01


def forward_product(left_side, right_side):
    return jnp.dot(left_side, right_side, preferred_element_type=jnp.float32)


def weight_grad(left_side, right_side):
    return lax.dot_general(
        left_side, right_side, (((0,), (0,)), ((), ())), preferred_element_type=jnp.float32
    )


def back_product(left_side, right_side):
    return lax.dot_general(
        left_side, right_side, (((1,), (1,)), ((), ())), preferred_element_type=jnp.float32
    )


def norm_forward(residual, norm_gain, norm_shift):
    centered = residual - jnp.mean(residual, axis=-1, keepdims=True)
    variance = jnp.mean(centered * centered, axis=-1, keepdims=True)
    inv_std = lax.rsqrt(variance + LN_EPS)
    normal_part = centered * inv_std
    return (normal_part * norm_gain + norm_shift, normal_part, inv_std)


def norm_backward(d_out, normal_part, inv_std, norm_gain):
    d_normal = d_out * norm_gain
    d_resid = inv_std * (
        d_normal
        - jnp.mean(d_normal, axis=-1, keepdims=True)
        - normal_part * jnp.mean(d_normal * normal_part, axis=-1, keepdims=True)
    )
    return (
        d_resid,
        jnp.sum(d_out * normal_part, axis=0, keepdims=True),
        jnp.sum(d_out, axis=0, keepdims=True),
    )


def gelu_slope(pre_act):
    return (
        0.5 * (1.0 + lax.erf(pre_act * 0.7071067811865476))
        + pre_act * jnp.exp(-0.5 * pre_act * pre_act) * 0.3989422804014327
    )


def key_side(keys, bias, lane, half):
    own = (lane < HEAD_DIM) if half == 0 else (lane >= HEAD_DIM)
    spare = HEAD_DIM if half == 0 else 0
    return jnp.where(own, keys, jnp.where(lane == spare, bias, 0.0)).astype(jnp.bfloat16)


def query_side(queries, lane, half):
    own = (lane < HEAD_DIM) if half == 0 else (lane >= HEAD_DIM)
    spare = HEAD_DIM if half == 0 else 0
    return jnp.where(own, queries, jnp.where(lane == spare, 1.0, 0.0)).astype(jnp.bfloat16)


def one_head(rows, lane, half):
    own = (lane < HEAD_DIM) if half == 0 else (lane >= HEAD_DIM)
    return jnp.where(own, rows, 0.0).astype(jnp.bfloat16)


def pair_of(ref, part, pair):
    width = ref.shape[1] // 3
    at = pl.multiple_of(part * width + pair * LANES, LANES)
    return ref[:, pl.ds(at, LANES)].astype(jnp.float32)


def attend_kernel(len_ref, qkv_lo, qkv_hi, mixed_ref, lse_ref, ot_ref):
    rows = mixed_ref.shape[0]
    width = qkv_lo.shape[1] // 3
    pairs = width // LANES
    real = len_ref[pl.program_id(0)]
    lane = lax.broadcasted_iota(jnp.int32, (rows, LANES), 1)
    place_key = lax.broadcasted_iota(jnp.int32, (rows, LANES), 0)
    bias = jnp.where(place_key < real, 0.0, NEG_FILL)
    for side, qkv_ref in enumerate((qkv_lo, qkv_hi)):

        def one_pair(pair, carry, side=side, qkv_ref=qkv_ref):
            queries = pair_of(qkv_ref, 0, pair) * (1.0 / math.sqrt(HEAD_DIM))
            keys = pair_of(qkv_ref, 1, pair)
            values_t = pair_of(qkv_ref, 2, pair).T.astype(jnp.bfloat16)
            scored = []
            for half in range(2):
                keys_one = key_side(keys, bias, lane, half)
                queries_one = query_side(queries, lane, half)
                for at in range(0, rows, QUERY_BLOCK):
                    cols = slice(at, at + QUERY_BLOCK)
                    scored.append((half, cols, back_product(keys_one, queries_one[cols])))
            weighed = []
            for half, cols, scores in scored:
                head = side * 2 * pairs + 2 * pair + half
                top = jnp.max(scores, axis=0, keepdims=True)
                exps = jnp.exp(scores - top)
                total = jnp.sum(exps, axis=0, keepdims=True)
                lse_ref[pl.ds(head, 1), cols] = top + jnp.log(total)
                weighed.append((half, cols, exps.astype(jnp.bfloat16), total))
            for half, cols, exps, total in weighed:
                lanes = slice(half * HEAD_DIM, (half + 1) * HEAD_DIM)
                ot_ref[lanes, cols] = forward_product(values_t[lanes], exps) / total
            at = pl.multiple_of(side * width + pair * LANES, LANES)
            mixed_ref[:, pl.ds(at, LANES)] = ot_ref[...].T.astype(jnp.bfloat16)
            return carry

        lax.fori_loop(0, pairs, one_pair, 0)


def attend_core(qkv_lo, qkv_hi, seq_lengths):
    total, wide = qkv_lo.shape
    seqs = seq_lengths.shape[0]
    rows, width = total // seqs, 2 * wide // 3
    heads = width // HEAD_DIM
    lse_rows = -(-heads // 8) * 8
    side = pl.BlockSpec((rows, wide), lambda seq, lens: (seq, 0))
    return pl.pallas_call(
        attend_kernel,
        out_shape=(
            jax.ShapeDtypeStruct((total, width), jnp.bfloat16),
            jax.ShapeDtypeStruct((seqs, lse_rows, rows), jnp.float32),
        ),
        grid_spec=pltpu.PrefetchScalarGridSpec(
            num_scalar_prefetch=1,
            grid=(seqs,),
            in_specs=[side, side],
            out_specs=[
                pl.BlockSpec((rows, width), lambda seq, lens: (seq, 0)),
                pl.BlockSpec((None, lse_rows, rows), lambda seq, lens: (seq, 0, 0)),
            ],
            scratch_shapes=[pltpu.VMEM((LANES, rows), jnp.float32)],
        ),
        compiler_params=pltpu.CompilerParams(vmem_limit_bytes=32 << 20),
        cost_estimate=LIGHT,
        name="attend",
    )(seq_lengths, qkv_lo, qkv_hi)


def attend_back_kernel(small_rows, len_ref, core_ref, *refs):
    qkv_lo, qkv_hi, d_mixed_ref, lse_ref = refs[:4]
    late = refs[4:7]
    small_ref = refs[7] if small_rows else None
    d_out_ref, sums_ref, far_ref, own_ref, dqt_ref, d_qkv_ref, held_ref, sems = refs[-8:]
    loads = [
        pltpu.make_async_copy(ref, held_ref.at[number], sems.at[number])
        for number, ref in enumerate(late)
    ]
    seq = pl.program_id(0)
    rows = d_mixed_ref.shape[0]
    width = qkv_lo.shape[1] // 3
    pairs = width // LANES
    scale = 1.0 / math.sqrt(HEAD_DIM)
    real = len_ref[seq]
    first_seq = seq == 0

    @pl.when(first_seq)
    def _():
        for load in loads:
            load.start()

    here = pl.ds(pl.multiple_of(seq * rows, LANES), rows)
    lane = lax.broadcasted_iota(jnp.int32, (rows, LANES), 1)
    place_key = lax.broadcasted_iota(jnp.int32, (rows, LANES), 0)
    bias = jnp.where(place_key < real, 0.0, NEG_FILL)
    for side, qkv_ref in enumerate((qkv_lo, qkv_hi)):

        def one_pair(pair, carry, side=side, qkv_ref=qkv_ref):
            queries = pair_of(qkv_ref, 0, pair) * scale
            keys = pair_of(qkv_ref, 1, pair)
            values = pair_of(qkv_ref, 2, pair)
            at_mixed = pl.multiple_of(side * width + pair * LANES, LANES)
            d_mixed = d_mixed_ref[:, pl.ds(at_mixed, LANES)].astype(jnp.float32)
            keys_t = keys.T.astype(jnp.bfloat16)
            scored = []
            for half in range(2):
                keys_one = key_side(keys, bias, lane, half)
                queries_one = query_side(queries, lane, half)
                values_only = one_head(values, lane, half)
                queries_only = one_head(queries, lane, half)
                d_mixed_only = one_head(d_mixed, lane, half)
                for at in range(0, rows, QUERY_BLOCK):
                    cols = slice(at, at + QUERY_BLOCK)
                    scores = back_product(keys_one, queries_one[cols])
                    d_probs = back_product(values_only, d_mixed_only[cols])
                    scored.append(
                        (half, cols, scores, d_probs, queries_only[cols], d_mixed_only[cols])
                    )
            weighed = []
            for half, cols, scores, d_probs, queries_only, d_mixed_only in scored:
                head = side * 2 * pairs + 2 * pair + half
                probs = jnp.exp(scores - lse_ref[pl.ds(head, 1), cols])
                row_part = jnp.sum(probs * d_probs, axis=0, keepdims=True)
                d_scores = (probs * (d_probs - row_part)).astype(jnp.bfloat16)
                weighed.append(
                    (half, cols, probs.astype(jnp.bfloat16), d_scores, queries_only, d_mixed_only)
                )
            d_keys = d_values = None
            for half, cols, probs, d_scores, queries_only, d_mixed_only in weighed:
                value_part = forward_product(probs, d_mixed_only)
                key_part = forward_product(d_scores, queries_only)
                d_values = value_part if d_values is None else d_values + value_part
                d_keys = key_part if d_keys is None else d_keys + key_part
                lanes = slice(half * HEAD_DIM, (half + 1) * HEAD_DIM)
                dqt_ref[lanes, cols] = forward_product(keys_t[lanes], d_scores)
            for part, value in enumerate((dqt_ref[...].T * scale, d_keys, d_values)):
                at = pl.multiple_of(part * width + pair * LANES, LANES)
                rounded = value.astype(jnp.bfloat16)
                d_qkv_ref[side, here, pl.ds(at, LANES)] = rounded
                d_out_ref[side, :, pl.ds(at, LANES)] = rounded
                if part != 1:
                    column = jnp.sum(rounded.astype(jnp.float32), axis=0, keepdims=True)
                    column = jnp.broadcast_to(column, (8, LANES))
                    known = sums_ref[side, :, pl.ds(at, LANES)]
                    sums_ref[side, :, pl.ds(at, LANES)] = jnp.where(
                        first_seq, column, column + known
                    )
            return carry

        lax.fori_loop(0, pairs, one_pair, 0)

    @pl.when(seq == pl.num_programs(0) - 1)
    def _():
        core = core_ref[0]
        for load in loads:
            load.wait()
        d_branch_ref = held_ref.at[2]
        for out_ref, side in ((far_ref, 1 - core), (own_ref, core)):
            out_ref[:, : 3 * width] = weight_grad(held_ref[0], d_qkv_ref[side]).astype(
                jnp.bfloat16
            )
            cols = pl.ds(pl.multiple_of(side * width, LANES), width)
            out_ref[:, 3 * width : 4 * width] = weight_grad(
                held_ref[1], d_branch_ref[:, cols]
            ).astype(jnp.bfloat16)
            if small_ref is not None:
                tile = small_ref[side]
                number = lax.broadcasted_iota(jnp.int32, tile.shape, 0)
                for row, start in ((0, 0), (1, 2 * width)):
                    line = jnp.concatenate(
                        [sums_ref[one, :1, start : start + width] for one in range(2)], axis=1
                    )
                    tile = jnp.where((number == row) & (side == 0), line, tile)
                out_ref[:, 4 * width :] = tile.T.astype(jnp.bfloat16)


def attend_core_back(
    core, qkv, d_mixed, lse, x_low, mixed_heads, d_branch, seq_lengths, small=None
):
    qkv_lo, qkv_hi = qkv
    total, wide = qkv_lo.shape
    seqs = seq_lengths.shape[0]
    rows, width = total // seqs, 2 * wide // 3
    extra = 0 if small is None else small.shape[1]
    once = pl.Buffered(1)
    side = pl.BlockSpec((rows, wide), lambda seq, *_: (seq, 0))
    whole = pl.BlockSpec(memory_space=pl.ANY)
    specs = [
        side,
        side,
        pl.BlockSpec((rows, width), lambda seq, *_: (seq, 0)),
        pl.BlockSpec((None, lse.shape[1], rows), lambda seq, *_: (seq, 0, 0)),
        whole,
        whole,
        whole,
    ]
    given = [qkv_lo, qkv_hi, d_mixed, lse, x_low, mixed_heads, d_branch]
    if small is not None:
        specs.append(pl.BlockSpec(small.shape, lambda seq, *_: (0, 0, 0), pipeline_mode=once))
        given.append(small)
    grad_shape = (width, 2 * width + extra)
    grad_spec = pl.BlockSpec(grad_shape, lambda seq, *_: (0, 0), pipeline_mode=once)
    return pl.pallas_call(
        functools.partial(attend_back_kernel, extra),
        out_shape=(
            jax.ShapeDtypeStruct((2, total, wide), jnp.bfloat16),
            jax.ShapeDtypeStruct((2, 8, wide), jnp.float32),
            jax.ShapeDtypeStruct(grad_shape, jnp.bfloat16),
            jax.ShapeDtypeStruct(grad_shape, jnp.bfloat16),
        ),
        grid_spec=pltpu.PrefetchScalarGridSpec(
            num_scalar_prefetch=2,
            grid=(seqs,),
            in_specs=specs,
            out_specs=[
                pl.BlockSpec((2, rows, wide), lambda seq, *_: (0, seq, 0)),
                pl.BlockSpec((2, 8, wide), lambda seq, *_: (0, 0, 0)),
                grad_spec,
                grad_spec,
            ],
            scratch_shapes=[
                pltpu.VMEM((LANES, rows), jnp.float32),
                pltpu.VMEM((2, total, wide), jnp.bfloat16),
                pltpu.VMEM((3, total, width), jnp.bfloat16),
                pltpu.SemaphoreType.DMA((3,)),
            ],
        ),
        compiler_params=pltpu.CompilerParams(vmem_limit_bytes=60 << 20),
        cost_estimate=LIGHT,
        name="attend_back",
    )(seq_lengths, core.reshape(1).astype(jnp.int32), *given)


def half_of(rows, side):
    width = rows.shape[1] // 2
    return lax.dynamic_slice_in_dim(rows, side * width, width, 1)


def project_in(flat_low, in_layer, small_layer):
    third = flat_low.shape[1] // 2
    qkv = []
    for side in range(2):
        cols = slice(side * third, (side + 1) * third)
        bias = jnp.concatenate(
            [small_layer[0, cols], jnp.zeros((third,), jnp.float32), small_layer[1, cols]]
        )
        part = forward_product(flat_low, in_layer[side]) + bias
        qkv.append(part.astype(jnp.bfloat16))
    return qkv


def project_in_back(d_resid, d_qkv, in_layer):
    return d_resid + sum(back_product(d_qkv[side], in_layer[side]) for side in range(2))


def small_tile_kernel(*refs):
    out_ref = refs[-1]
    width = out_ref.shape[2]
    out_ref[...] = jnp.zeros_like(out_ref)
    third = width // 2

    def put(layer, row, ref, parts):
        for part in range(parts):
            cols = slice(part * width, (part + 1) * width)
            out_ref[layer, row + part : row + part + 1, :] = ref[:1, cols]

    for layer in range(2):
        out_sums, pre_sums, feed_sums = refs[3 * layer : 3 * layer + 3]
        put(layer, 2, out_sums, 3)
        put(layer, 5, pre_sums, 4)
        put(layer, 9, feed_sums, 3)
    attn_sums = refs[6]
    for row, start in ((0, 0), (1, 2 * third)):
        for side in range(2):
            out_ref[1, row : row + 1, side * third : (side + 1) * third] = attn_sums[
                side, :1, start : start + third
            ]


def small_tile(one, two, attn_sums, width):
    return pl.pallas_call(
        small_tile_kernel,
        out_shape=jax.ShapeDtypeStruct((2, LANES, width), jnp.float32),
        cost_estimate=LIGHT,
        name="small_tile",
    )(*one, *two, attn_sums)


def project_norm_kernel(rows_ref, weight_ref, resid_ref, bias_ref, gain_ref, shift_ref, *outs):
    normed_ref, low_ref, xhat_ref, inv_ref = outs
    branch = forward_product(rows_ref[...], weight_ref[...]) + bias_ref[...]
    normed, normal_part, inv_std = norm_forward(
        resid_ref[...].astype(jnp.float32) + branch, gain_ref[...], shift_ref[...]
    )
    normed_ref[...] = normed
    low_ref[...] = normed.astype(jnp.bfloat16)
    xhat_ref[...] = normal_part
    inv_ref[...] = jnp.broadcast_to(inv_std, inv_ref.shape)


def project_norm(rows_low, weight, resid, small_layer, first):
    total, depth = rows_low.shape
    width = resid.shape[1]
    block = math.gcd(total, 256)
    row = pl.BlockSpec((block, width), lambda at: (at, 0))
    line = pl.BlockSpec((1, width), lambda at: (0, 0))
    return pl.pallas_call(
        project_norm_kernel,
        out_shape=(
            jax.ShapeDtypeStruct((total, width), jnp.float32),
            jax.ShapeDtypeStruct((total, width), jnp.bfloat16),
            jax.ShapeDtypeStruct((total, width), jnp.float32),
            jax.ShapeDtypeStruct((total, LANES), jnp.float32),
        ),
        grid=(total // block,),
        in_specs=[
            pl.BlockSpec((block, depth), lambda at: (at, 0)),
            pl.BlockSpec((depth, width), lambda at: (0, 0), pipeline_mode=pl.Buffered(1)),
            row,
            line,
            line,
            line,
        ],
        out_specs=[row, row, row, pl.BlockSpec((block, LANES), lambda at: (at, 0))],
        compiler_params=pltpu.CompilerParams(vmem_limit_bytes=24 << 20),
        cost_estimate=LIGHT,
        name="project_norm",
    )(rows_low, weight, resid, *[small_layer[at : at + 1] for at in range(first, first + 3)])


def served_back_kernel(
    select_ref, d_served_ref, cot_ref, xhat_ref, inv_ref, gain_ref, out_ref, *outs
):
    out_resid_ref, d_branch_ref, d_mixed_ref, sums_ref = outs
    width = cot_ref.shape[1]
    select = select_ref[...]
    both = weight_grad(select, d_served_ref[...])
    hit = weight_grad(select, jnp.ones((select.shape[0], LANES), jnp.bfloat16))[:, :1] > 0.5
    d_out = jnp.where(hit, both[:, :width] + both[:, width:], cot_ref[...].astype(jnp.float32))
    xhat = xhat_ref[...]
    d_resid, d_branch = norm_back_rows(d_out, xhat, inv_ref[:, :1], gain_ref[...])
    out_resid_ref[...] = d_resid
    d_branch_ref[...] = d_branch
    d_mixed_ref[...] = back_product(d_branch, out_ref[...]).astype(jnp.bfloat16)
    add_sums(sums_ref, (d_branch.astype(jnp.float32), d_out * xhat, d_out))


def served_back(select_rows, d_served, cot_flat, xhat, inv, small_layer, out_layer):
    total, width = cot_flat.shape
    slots = select_rows.shape[0]
    block = math.gcd(total, 256)
    row = pl.BlockSpec((block, width), lambda at: (at, 0))
    d_resid, d_branch, d_mixed, sums = pl.pallas_call(
        served_back_kernel,
        out_shape=(
            jax.ShapeDtypeStruct((total, width), jnp.float32),
            jax.ShapeDtypeStruct((total, width), jnp.bfloat16),
            jax.ShapeDtypeStruct((total, width), jnp.bfloat16),
            jax.ShapeDtypeStruct((8, 3 * width), jnp.float32),
        ),
        grid=(total // block,),
        in_specs=[
            pl.BlockSpec((slots, block), lambda at: (0, at)),
            pl.BlockSpec((slots, 2 * width), lambda at: (0, 0)),
            row,
            row,
            pl.BlockSpec((block, LANES), lambda at: (at, 0)),
            pl.BlockSpec((1, width), lambda at: (0, 0)),
            pl.BlockSpec((width, width), lambda at: (0, 0)),
        ],
        out_specs=[row, row, row, pl.BlockSpec((8, 3 * width), lambda at: (0, 0))],
        compiler_params=pltpu.CompilerParams(vmem_limit_bytes=24 << 20),
        cost_estimate=LIGHT,
        name="served_back",
    )(select_rows, d_served, cot_flat, xhat, inv, small_layer[3:4], out_layer)
    return (d_resid, d_branch, d_mixed, sums)


def feed_up_kernel(rows_ref, up_ref, bias_ref, act_ref, slope_ref):
    low_rows = rows_ref[...]
    for at in range(0, up_ref.shape[1], HIDDEN_BLOCK):
        cols = slice(at, at + HIDDEN_BLOCK)
        pre_act = forward_product(low_rows, up_ref[:, cols]) + bias_ref[:, cols]
        below = 0.5 * (1.0 + lax.erf(pre_act * 0.7071067811865476))
        density = jnp.exp(-0.5 * pre_act * pre_act) * 0.3989422804014327
        act_ref[:, cols] = (pre_act * below).astype(jnp.bfloat16)
        slope_ref[:, cols] = (below + pre_act * density).astype(jnp.bfloat16)


def feed_up(rows_low, up_layer, small_layer):
    total, width = rows_low.shape
    hidden = up_layer.shape[1]
    block = math.gcd(total, 256)
    bias = small_layer[5:9].reshape(1, hidden)
    shape = jax.ShapeDtypeStruct((total, hidden), jnp.bfloat16)
    act_low, slope = pl.pallas_call(
        feed_up_kernel,
        out_shape=(shape, shape),
        grid=(total // block,),
        in_specs=[
            pl.BlockSpec((block, width), lambda at: (at, 0)),
            pl.BlockSpec((width, hidden), lambda at: (0, 0)),
            pl.BlockSpec((1, hidden), lambda at: (0, 0)),
        ],
        out_specs=[pl.BlockSpec((block, hidden), lambda at: (at, 0))] * 2,
        compiler_params=pltpu.CompilerParams(vmem_limit_bytes=32 << 20),
        cost_estimate=LIGHT,
        name="feed_up",
    )(rows_low, up_layer, bias)
    return (act_low, slope)


def feed_down(rows_in, act_low, down_layer, small_layer):
    branch = forward_product(act_low, down_layer) + small_layer[9]
    return norm_forward(rows_in + branch, small_layer[10], small_layer[11])


def feed_down_back(d_normed, normal_part, inv_std, slope, down_layer, small_layer):
    d_resid, d_gain, d_shift = norm_backward(d_normed, normal_part, inv_std, small_layer[10])
    d_branch = d_resid.astype(jnp.bfloat16)
    d_pre = (back_product(d_branch, down_layer) * slope.astype(jnp.float32)).astype(jnp.bfloat16)
    d_bias = jnp.sum(d_pre.astype(jnp.float32), axis=0, keepdims=True)
    d_shared = jnp.sum(d_branch.astype(jnp.float32), axis=0, keepdims=True)
    small_rows = (d_bias, jnp.concatenate([d_shared, d_gain, d_shift], axis=1))
    return (d_resid, d_branch, d_pre, small_rows)


def norm_back_rows(d_out, xhat, inv, gain):
    d_normal = d_out * gain
    d_resid = inv * (
        d_normal
        - jnp.mean(d_normal, axis=-1, keepdims=True)
        - xhat * jnp.mean(d_normal * xhat, axis=-1, keepdims=True)
    )
    return (d_resid, d_resid.astype(jnp.bfloat16))


def add_sums(sums_ref, values):
    width = values[0].shape[1]
    first = pl.program_id(0) == 0
    for number, value in enumerate(values):
        cols = slice(number * width, (number + 1) * width)
        part = jnp.broadcast_to(jnp.sum(value, axis=0, keepdims=True), (8, width))
        sums_ref[:, cols] = jnp.where(first, part, part + sums_ref[:, cols])


def layer_back_kernel(
    d_resid_ref, d_qkv_ref, in_ref, xhat_ref, inv_ref, gain_ref, down_ref, slope_ref, *outs
):
    out_resid_ref, d_branch_ref, d_pre_ref, pre_sums_ref, sums_ref = outs
    d_out = d_resid_ref[...]
    for side in range(2):
        d_out = d_out + back_product(d_qkv_ref[side], in_ref[side])
    xhat = xhat_ref[...]
    d_resid, d_branch = norm_back_rows(d_out, xhat, inv_ref[:, :1], gain_ref[...])
    out_resid_ref[...] = d_resid
    d_branch_ref[...] = d_branch
    add_sums(sums_ref, (d_branch.astype(jnp.float32), d_out * xhat, d_out))
    first = pl.program_id(0) == 0
    for at in range(0, down_ref.shape[0], HIDDEN_BLOCK):
        cols = slice(at, at + HIDDEN_BLOCK)
        d_act = back_product(d_branch, down_ref[cols])
        d_pre = (d_act * slope_ref[:, cols].astype(jnp.float32)).astype(jnp.bfloat16)
        d_pre_ref[:, cols] = d_pre
        part = jnp.broadcast_to(
            jnp.sum(d_pre.astype(jnp.float32), axis=0, keepdims=True), (8, HIDDEN_BLOCK)
        )
        pre_sums_ref[:, cols] = jnp.where(first, part, part + pre_sums_ref[:, cols])


def layer_back(d_resid, d_qkv, in_layer, xhat, inv, small_layer, down_layer, slope):
    total, width = d_resid.shape
    hidden = slope.shape[1]
    wide = d_qkv.shape[2]
    block = math.gcd(total, 256)
    row = pl.BlockSpec((block, width), lambda at: (at, 0))
    hidden_row = pl.BlockSpec((block, hidden), lambda at: (at, 0))
    d_resid, d_branch, d_pre, pre_sums, sums = pl.pallas_call(
        layer_back_kernel,
        out_shape=(
            jax.ShapeDtypeStruct((total, width), jnp.float32),
            jax.ShapeDtypeStruct((total, width), jnp.bfloat16),
            jax.ShapeDtypeStruct((total, hidden), jnp.bfloat16),
            jax.ShapeDtypeStruct((8, hidden), jnp.float32),
            jax.ShapeDtypeStruct((8, 3 * width), jnp.float32),
        ),
        grid=(total // block,),
        in_specs=[
            row,
            pl.BlockSpec((2, block, wide), lambda at: (0, at, 0)),
            pl.BlockSpec((2, width, wide), lambda at: (0, 0, 0), pipeline_mode=pl.Buffered(1)),
            row,
            pl.BlockSpec((block, LANES), lambda at: (at, 0)),
            pl.BlockSpec((1, width), lambda at: (0, 0)),
            pl.BlockSpec((hidden, width), lambda at: (0, 0), pipeline_mode=pl.Buffered(1)),
            hidden_row,
        ],
        out_specs=[
            row,
            row,
            hidden_row,
            pl.BlockSpec((8, hidden), lambda at: (0, 0)),
            pl.BlockSpec((8, 3 * width), lambda at: (0, 0)),
        ],
        compiler_params=pltpu.CompilerParams(vmem_limit_bytes=60 << 20),
        cost_estimate=LIGHT,
        name="layer_back",
    )(d_resid, d_qkv, in_layer, xhat, inv, small_layer[10:11], down_layer, slope)
    return (d_resid, d_branch, d_pre, (pre_sums, sums))


def feed_back_kernel(d_resid_ref, d_pre_ref, up_ref, xhat_ref, inv_ref, gain_ref, out_ref, *outs):
    out_resid_ref, d_branch_ref, d_mixed_ref, sums_ref = outs
    d_out = d_resid_ref[...] + back_product(d_pre_ref[...], up_ref[...])
    xhat = xhat_ref[...]
    d_resid, d_branch = norm_back_rows(d_out, xhat, inv_ref[:, :1], gain_ref[...])
    out_resid_ref[...] = d_resid
    d_branch_ref[...] = d_branch
    d_mixed_ref[...] = back_product(d_branch, out_ref[...]).astype(jnp.bfloat16)
    add_sums(sums_ref, (d_branch.astype(jnp.float32), d_out * xhat, d_out))


def feed_back(d_resid, d_pre, up_layer, xhat, inv, small_layer, out_layer):
    total, width = d_resid.shape
    hidden = d_pre.shape[1]
    block = math.gcd(total, 256)
    row = pl.BlockSpec((block, width), lambda at: (at, 0))
    d_resid, d_branch, d_mixed, sums = pl.pallas_call(
        feed_back_kernel,
        out_shape=(
            jax.ShapeDtypeStruct((total, width), jnp.float32),
            jax.ShapeDtypeStruct((total, width), jnp.bfloat16),
            jax.ShapeDtypeStruct((total, width), jnp.bfloat16),
            jax.ShapeDtypeStruct((8, 3 * width), jnp.float32),
        ),
        grid=(total // block,),
        in_specs=[
            row,
            pl.BlockSpec((block, hidden), lambda at: (at, 0)),
            pl.BlockSpec((width, hidden), lambda at: (0, 0), pipeline_mode=pl.Buffered(1)),
            row,
            pl.BlockSpec((block, LANES), lambda at: (at, 0)),
            pl.BlockSpec((1, width), lambda at: (0, 0)),
            pl.BlockSpec((width, width), lambda at: (0, 0), pipeline_mode=pl.Buffered(1)),
        ],
        out_specs=[row, row, row, pl.BlockSpec((8, 3 * width), lambda at: (0, 0))],
        compiler_params=pltpu.CompilerParams(vmem_limit_bytes=60 << 20),
        cost_estimate=LIGHT,
        name="feed_back",
    )(d_resid, d_pre, up_layer, xhat, inv, small_layer[3:4], out_layer)
    return (d_resid, d_branch, d_mixed, sums)


def order_attn_kernel(core_ref, *refs):
    pairs, out_ref = (refs[:2], refs[2:4]), refs[4]
    third = out_ref.shape[3] // 2
    core = core_ref[0]
    for layer, (own_ref, far_ref) in enumerate(pairs):
        for part in range(4):
            cols = slice(part * third, (part + 1) * third)
            own, far = own_ref[:, cols], far_ref[:, cols]
            for side in range(2):
                out_ref[layer, part, :, side * third : (side + 1) * third] = jnp.where(
                    core == side, own, far
                )


def order_attn(core, one, two, width):
    local = pl.BlockSpec(memory_space=pltpu.VMEM)
    shard = one[0].shape[0]
    return pl.pallas_call(
        order_attn_kernel,
        out_shape=jax.ShapeDtypeStruct((2, 4, shard, width), jnp.bfloat16),
        grid_spec=pltpu.PrefetchScalarGridSpec(
            num_scalar_prefetch=1, grid=(), in_specs=[local] * 4, out_specs=local
        ),
        cost_estimate=LIGHT,
        name="order_attn",
    )(core.reshape(1).astype(jnp.int32), *one, *two)


def feed_grads_kernel(shard, core, low_ref, d_pre_ref, act_ref, d_branch_ref, *rest):
    far_ref, own_ref, low_t_ref, down_ref = rest
    at = pl.program_id(0)
    width = low_ref.shape[1]
    third = width // 2

    @pl.when(at == 0)
    def _():
        low_t_ref[...] = low_ref[...].T

    for step in range(4):

        @pl.when(at == step)
        def _(step=step):
            out_ref = far_ref if step < 2 else own_ref
            cols = slice((step % 2) * width, (step % 2 + 1) * width)
            out_ref[:, cols] = forward_product(low_t_ref[...], d_pre_ref[...]).astype(jnp.bfloat16)

    @pl.when(at >= 4)
    def _():
        down_ref[...] = weight_grad(act_ref[...], d_branch_ref[...])
        blocks = width // (4 * shard)
        for out_ref, side in ((far_ref, 1 - core[0]), (own_ref, core[0])):
            from_cols = pl.ds(pl.multiple_of(side * third, LANES), third)
            for block in range(blocks):
                row = pl.multiple_of(((at - 4) * blocks + block) * shard, 16)
                for part in range(4):
                    start = (block * 4 + part) * shard
                    cols = slice(2 * width + part * third, 2 * width + (part + 1) * third)
                    out_ref[pl.ds(row, shard), cols] = down_ref[
                        start : start + shard, from_cols
                    ].astype(jnp.bfloat16)


def feed_grads_plain(core, rows_low, d_pre, act_low, d_branch, shard):
    sides = []
    width = rows_low.shape[1]
    for side in (1 - core, core):
        d_up = weight_grad(rows_low, half_of(d_pre, side))
        d_down = weight_grad(act_low, half_of(d_branch, side))
        d_down = d_down.reshape(-1, 4, shard, width // 2).transpose(0, 2, 1, 3)
        sides.append(jnp.concatenate([d_up, d_down.reshape(width, -1)], axis=1))
    return [part.astype(jnp.bfloat16) for part in sides]


def feed_grads(core, rows_low, d_pre, act_low, d_branch, shard):
    total, width = rows_low.shape
    hidden = act_low.shape[1]
    if shard % 16 or hidden != 4 * width:
        return feed_grads_plain(core, rows_low, d_pre, act_low, d_branch, shard)

    def pre_at(at, core):
        step = jnp.minimum(at, 3)
        return (0, jnp.where(step < 2, 1 - core[0], core[0]) * 2 + step % 2)

    shape = jax.ShapeDtypeStruct((width, hidden), jnp.bfloat16)
    return pl.pallas_call(
        functools.partial(feed_grads_kernel, shard),
        out_shape=(shape, shape),
        grid_spec=pltpu.PrefetchScalarGridSpec(
            num_scalar_prefetch=1,
            grid=(8,),
            in_specs=[
                pl.BlockSpec((total, width), lambda at, core: (0, 0)),
                pl.BlockSpec((total, width), pre_at),
                pl.BlockSpec((total, width), lambda at, core: (0, jnp.maximum(at - 4, 0))),
                pl.BlockSpec((total, width), lambda at, core: (0, 0)),
            ],
            out_specs=[pl.BlockSpec((width, hidden), lambda at, core: (0, 0))] * 2,
            scratch_shapes=[
                pltpu.VMEM((width, total), jnp.bfloat16),
                pltpu.VMEM((width, width), jnp.float32),
            ],
        ),
        compiler_params=pltpu.CompilerParams(vmem_limit_bytes=40 << 20),
        cost_estimate=LIGHT,
        name="feed_grads",
    )(core.reshape(1).astype(jnp.int32), rows_low, d_pre, act_low, d_branch)


def row_select(token_mask, capacity):
    flat_mask = token_mask.reshape(1, -1)
    row_total = flat_mask.shape[1]
    before = (
        lax.broadcasted_iota(jnp.int32, (row_total, row_total), 0)
        < lax.broadcasted_iota(jnp.int32, (row_total, row_total), 1)
    ).astype(jnp.bfloat16)
    rank = forward_product(flat_mask.astype(jnp.bfloat16), before).astype(jnp.int32)
    slots = lax.broadcasted_iota(jnp.int32, (capacity, row_total), 0)
    return ((slots == rank) & (flat_mask == 1)).astype(jnp.bfloat16)


def split_low(wide, parts):
    pieces = []
    left = wide
    for _ in range(parts - 1):
        piece = lax.reduce_precision(left, 8, 7)
        pieces.append(piece.astype(jnp.bfloat16))
        left = left - piece
    pieces.append(left.astype(jnp.bfloat16))
    return jnp.concatenate(pieces, axis=1)


def join_low(joined, parts):
    width = joined.shape[1] // parts
    total = joined[:, :width]
    for number in range(1, parts):
        total = total + joined[:, number * width : (number + 1) * width]
    return total


def adam_update(
    master, first_moment, second_moment, gradient, clip_scale, step_value, decay_rate, rate_value
):
    clipped = gradient.astype(jnp.float32) * clip_scale
    first_new = BETA_FIRST * first_moment + (1.0 - BETA_FIRST) * clipped
    second_new = BETA_SECOND * second_moment + (1.0 - BETA_SECOND) * clipped * clipped
    first_hat = first_new / (1.0 - jnp.power(BETA_FIRST, step_value))
    second_hat = second_new / (1.0 - jnp.power(BETA_SECOND, step_value))
    master_new = master - rate_value * (
        first_hat / (jnp.sqrt(second_hat) + ADAM_EPS) + decay_rate * master
    )
    return (master_new, first_new, second_new, master_new.astype(jnp.bfloat16))


def routes(peers):
    bits = peers.bit_length() - 1
    deep = min(2, bits)
    rest = bits - deep
    x_bits = [1 << at for at in range(rest - rest // 2)]
    y_bits = [1 << at for at in range(rest - rest // 2, rest)]
    z_bits = [1 << at for at in range(rest, bits)]
    if len(x_bits) == len(y_bits):
        return ((z_bits, y_bits, x_bits), (z_bits, x_bits, y_bits))
    return ((z_bits, y_bits, x_bits), (z_bits, y_bits, x_bits))


def stage_sizes(peers):
    return [1 << len(bits) for bits in routes(peers)[0]]


def mask_of(bits, turn):
    return sum(bit for at, bit in enumerate(bits) if turn >> at & 1)


def shift(value, stage, turn, peers):
    pairs = []
    for core, path in enumerate(routes(peers)):
        mask = mask_of(path[stage], turn)
        pairs += [(core * peers + at, core * peers + (at ^ mask)) for at in range(peers)]
    return lax.ppermute(value, ("dp", "bal"), pairs)


def swap(value):
    return lax.ppermute(value, "dp", [(0, 1), (1, 0)])


def place_table(peers, core):
    masks = [
        [mask_of(sum(path, []), spot) for spot in range(peers)] for path in routes(peers)
    ]
    masks = jnp.asarray(np.array(masks, np.int32))
    mine = lax.axis_index("bal")
    own = jnp.where(core == 0, masks[0], masks[1])
    far = jnp.where(core == 0, masks[1], masks[0])
    return jnp.concatenate([mine ^ own, mine ^ far, core.reshape(1).astype(jnp.int32)])


def place_kernel(plan, count, spots, *refs):
    parts, outs = refs[:count], refs[count:]
    held, rows, _ = parts[0].shape
    core = spots[count * held]

    for number, part in enumerate(parts):
        side = core if number < count // 2 else 1 - core

        def one_block(at, carry, number=number, part=part, side=side):
            spot = spots[number * held + at]
            for (start, width, kind), out in zip(plan, outs):
                cols = pl.ds(pl.multiple_of(side * width, LANES), width)
                if kind == "stack":
                    out[side, spot] = part[at, :, start : start + width]
                elif kind == "wide":
                    out[spot, :, cols] = part[at, :, start : start + width]
                else:
                    for piece in range(4):
                        begin = start + piece * width
                        out[spot, piece * rows : (piece + 1) * rows, cols] = part[
                            at, :, begin : begin + width
                        ]
            return carry

        lax.fori_loop(0, held, one_block, 0)


def place(spots, parts, plan):
    held, rows, whole = parts[0].shape
    peers = len(parts) * held // 2
    kinds = [
        (start, 4 * width, "stack") if kind == "down" and rows % 16 else (start, width, kind)
        for start, width, kind in plan
    ]
    shapes = {
        "stack": lambda width: (2, peers, rows, width),
        "wide": lambda width: (peers, rows, 2 * width),
        "down": lambda width: (peers, 4 * rows, 2 * width),
    }
    local = pl.BlockSpec(memory_space=pltpu.VMEM)
    placed = pl.pallas_call(
        functools.partial(place_kernel, kinds, len(parts)),
        out_shape=[
            jax.ShapeDtypeStruct(shapes[kind](width), parts[0].dtype) for _, width, kind in kinds
        ],
        grid_spec=pltpu.PrefetchScalarGridSpec(
            num_scalar_prefetch=1,
            grid=(),
            in_specs=[local] * len(parts),
            out_specs=[local] * len(kinds),
        ),
        compiler_params=pltpu.CompilerParams(vmem_limit_bytes=40 << 20),
        cost_estimate=LIGHT,
        name="place",
    )(spots, *parts)
    results = []
    for part, (_, width, kind), (_, _, asked) in zip(placed, kinds, plan):
        if kind != asked:
            part = part.reshape(2, peers, rows, 4, width // 4).transpose(1, 3, 2, 0, 4)
            results.append(part.reshape(peers * rows * 4, width // 2))
        elif kind == "stack":
            results.append(part.reshape(2, peers * rows, width))
        else:
            results.append(part.reshape(-1, 2 * width))
    return results


class Gather:
    def __init__(self, mine, spots, peers, plan):
        self.kept, self.moved = [mine[None]], []
        self.spots, self.peers, self.plan = spots, peers, plan
        self.sizes = stage_sizes(peers)
        self.stage, self.turn = 0, 1

    def done(self):
        return self.stage > len(self.sizes)

    def launch(self, count):
        if self.stage == len(self.sizes):
            return [swap(part) for part in self.kept]
        stop = self.sizes[self.stage]
        stop = stop if count is None else min(stop, self.turn + count)
        turns = range(self.turn, stop)
        self.turn = stop
        return [shift(self.kept[0], self.stage, turn, self.peers) for turn in turns]

    def land(self, moved):
        self.moved += moved
        if self.stage < len(self.sizes) and len(self.moved) < self.sizes[self.stage] - 1:
            return
        whole = self.kept + self.moved
        if self.stage < len(self.sizes) - 1:
            whole = [jnp.concatenate(whole, axis=0)]
        self.kept, self.moved = whole, []
        self.stage, self.turn = self.stage + 1, 1

    def result(self):
        return place(self.spots, self.kept, self.plan)


class Scatter:
    def __init__(self, far, own, spots, peers):
        self.kept = [grads.reshape(peers, -1, grads.shape[1]) for grads in (own, far)]
        self.moved = []
        self.spots, self.peers = spots, peers
        self.sizes = stage_sizes(peers)
        self.stage, self.turn = len(self.sizes), 1

    def done(self):
        return self.stage < 0

    def launch(self, count):
        if self.stage == len(self.sizes):
            return [swap(self.kept[1])]
        stop = self.sizes[self.stage]
        stop = stop if count is None else min(stop, self.turn + count)
        turns = range(self.turn, stop)
        self.turn = stop
        return [shift(self.kept[turn], self.stage, turn, self.peers) for turn in turns]

    def land(self, moved):
        self.moved += moved
        if self.stage == len(self.sizes):
            self.kept = list(fold(self.spots, self.kept[0], self.moved[0], self.sizes[-1]))
        else:
            if len(self.moved) < self.sizes[self.stage] - 1:
                return
            pieces = self.sizes[self.stage - 1] if self.stage else 1
            size = self.kept[0].shape[0] // pieces

            def total(at):
                rows = slice(at * size, (at + 1) * size)
                adds = [part[rows].astype(jnp.float32) for part in [self.kept[0]] + self.moved]
                return sum(adds[1:], adds[0]).astype(jnp.bfloat16)

            self.kept = [total(at) for at in range(pieces)]
        self.moved = []
        self.stage, self.turn = self.stage - 1, 1

    def result(self):
        return self.kept[0][0]


class Lanes:
    def __init__(self):
        self.flying = {}

    def launch(self, *moves):
        for move in moves:
            move, count = move if isinstance(move, tuple) else (move, None)
            if not move.done():
                self.flying[move] = self.flying.get(move, []) + move.launch(count)

    def meet(self, work, *landing, ready=()):
        moves = [move for move in landing if move in self.flying]
        flown = [self.flying.pop(move) for move in moves]
        waiting = [move.kept for move in ready]
        work, flown, waiting = lax.optimization_barrier((work, flown, waiting))
        for move, moved in zip(moves, flown):
            move.land(moved)
        for move, kept in zip(ready, waiting):
            move.kept = kept
        return work

    def settle(self, work, *moves):
        return self.meet(work, ready=moves)

    def finish(self, work, *moves):
        work = self.meet(work, *moves)
        while not all(move.done() for move in moves):
            self.launch(*moves)
            work = self.meet(work, *moves)
        return work


def fold_kernel(spots, own, far, *outs):
    held = outs[0].shape[0]

    def one_block(at, carry):
        for number, out in enumerate(outs):
            spot = spots[number * held + at]
            out[at] = (own[spot].astype(jnp.float32) + far[spot].astype(jnp.float32)).astype(
                out.dtype
            )
        return carry

    lax.fori_loop(0, held, one_block, 0)


def fold(spots, own, far, pieces):
    peers, rows, width = own.shape
    shape = jax.ShapeDtypeStruct((peers // pieces, rows, width), own.dtype)
    local = pl.BlockSpec(memory_space=pltpu.VMEM)
    return pl.pallas_call(
        fold_kernel,
        out_shape=[shape] * pieces,
        grid_spec=pltpu.PrefetchScalarGridSpec(
            num_scalar_prefetch=1,
            grid=(),
            in_specs=[local, local],
            out_specs=[local] * pieces,
        ),
        compiler_params=pltpu.CompilerParams(vmem_limit_bytes=32 << 20),
        cost_estimate=LIGHT,
        name="fold",
    )(spots, own, far)


def both_sides(own, other, core):
    return (jnp.where(core == 0, own, other), jnp.where(core == 0, other, own))


def per_device(
    tokens,
    cotangent,
    seq_lengths,
    token_mask,
    step_count,
    attn_master,
    attn_first,
    attn_second,
    up_master,
    up_first,
    up_second,
    down_master,
    down_first,
    down_second,
    small_master,
    small_first,
    small_second,
):
    core = lax.axis_index("dp")
    peers = lax.axis_size("bal")
    seq_count, length, model_width = tokens.shape
    rows_total = seq_count * length
    spots = place_table(peers, core)
    shard = attn_master.shape[2]
    attn_half = lax.dynamic_slice_in_dim(attn_master, core * (model_width // 2), model_width // 2, 3)
    attn_half = attn_half.astype(jnp.bfloat16).transpose(0, 2, 1, 3).reshape(2, shard, -1)
    small_half = lax.dynamic_slice_in_dim(small_master.reshape(24, shard), core * 12, 12, 0)
    small_half = jnp.pad(small_half.astype(jnp.bfloat16).T, ((0, 0), (0, LANES - 12)))
    wide = attn_half.shape[2]
    lanes = Lanes()
    third = model_width // 2
    hidden_half = up_master.shape[2] // 2

    def down_half(layer):
        half = half_of(down_master[layer], core).astype(jnp.bfloat16)
        return [half[part * shard : (part + 1) * shard] for part in range(4)]

    up_half = [half_of(up_master[layer], core).astype(jnp.bfloat16) for layer in range(2)]
    in_one = Gather(
        jnp.concatenate([attn_half[0, :, : 3 * third], small_half], axis=1),
        spots,
        peers,
        [(0, 3 * third, "stack"), (3 * third, LANES, "stack")],
    )
    out_up_one = Gather(
        jnp.concatenate([attn_half[0, :, 3 * third :], up_half[0]], axis=1),
        spots,
        peers,
        [(0, third, "wide"), (third, hidden_half, "wide")],
    )
    down_one = Gather(
        jnp.concatenate(down_half(0), axis=1), spots, peers, [(0, third, "down")]
    )
    attn_two = Gather(
        attn_half[1], spots, peers, [(0, 3 * third, "stack"), (3 * third, third, "wide")]
    )
    up_two = Gather(up_half[1], spots, peers, [(0, hidden_half, "wide")])
    down_two = Gather(
        jnp.concatenate(down_half(1), axis=1), spots, peers, [(0, third, "down")]
    )
    flat_low = tokens.reshape(rows_total, model_width)
    cot_flat = cotangent.reshape(rows_total, model_width)
    select_rows = row_select(token_mask, MCAP)
    flat_mask = token_mask.reshape(-1, 1) == 1

    lanes.launch(in_one)
    lanes.meet((), in_one, ready=(out_up_one,))
    lanes.launch(in_one, (out_up_one, 2))
    lanes.meet((), in_one, out_up_one)
    lanes.launch(in_one, out_up_one)
    lanes.meet((), in_one, out_up_one, ready=(down_one,))
    lanes.launch(in_one, out_up_one, (down_one, 2))
    lanes.finish((), in_one)
    w_in_one, small_rows = in_one.result()
    small_vals = small_rows[:, :, :12].transpose(0, 2, 1).astype(jnp.float32)
    qkv_one = project_in(flat_low, w_in_one, small_vals[0])
    qkv_one = lanes.meet(qkv_one, out_up_one, down_one, ready=(attn_two,))
    lanes.launch(out_up_one, down_one, (attn_two, 2))
    attended = attend_core(qkv_one[0], qkv_one[1], seq_lengths)
    attended = lanes.meet(attended, out_up_one, down_one, attn_two, ready=(up_two,))
    lanes.launch(out_up_one, down_one, attn_two)
    mixed_one, lse_one = lanes.finish(attended, out_up_one)
    w_out_one, w_up_one = out_up_one.result()
    attended_one = project_norm(mixed_one, w_out_one, flat_low, small_vals[0], 2)
    attended_one = lanes.meet(attended_one, down_one, attn_two, ready=(down_two,))
    attended_one, low_one, attn_xhat_one, attn_inv_one = attended_one
    lanes.launch(down_one, attn_two, (up_two, 2))
    act_one = feed_up(low_one, w_up_one, small_vals[0])
    act_one = lanes.meet(act_one, down_one, attn_two, up_two)
    lanes.launch(down_one, attn_two, up_two, (down_two, 1))
    act_one, slope_one = lanes.finish(act_one, down_one)
    (w_down_one,) = down_one.result()
    layer_one = project_norm(act_one, w_down_one, attended_one, small_vals[0], 9)
    layer_one = lanes.meet(layer_one, attn_two, up_two, down_two)
    lanes.launch(attn_two, up_two, down_two)
    layer_one, layer_low, feed_xhat_one, feed_inv_one = lanes.finish(layer_one, attn_two)
    w_in_two, w_out_two = attn_two.result()
    w_in_two, w_out_two = lanes.meet((w_in_two, w_out_two), up_two, down_two)
    lanes.launch(up_two, down_two)
    qkv_two = project_in(layer_low, w_in_two, small_vals[1])
    attended = attend_core(qkv_two[0], qkv_two[1], seq_lengths)
    mixed_two, lse_two = lanes.meet(attended, up_two, down_two)
    lanes.launch(up_two, down_two)
    attended_two, _, attn_xhat_two, attn_inv_two = project_norm(
        mixed_two, w_out_two, layer_one, small_vals[1], 2
    )
    rows_in = join_low(forward_product(select_rows, split_low(attended_two, 3)), 3)
    d_rows_out = forward_product(select_rows, cot_flat)
    rows_in = lanes.finish(rows_in, up_two)
    rows_in = lanes.meet(rows_in, down_two)
    lanes.launch(down_two)
    (w_up_two,) = up_two.result()
    rows_low = rows_in.astype(jnp.bfloat16)
    act_two, slope_two = feed_up(rows_low, w_up_two, small_vals[1])
    act_two, slope_two = lanes.finish((act_two, slope_two), down_two)
    (w_down_two,) = down_two.result()
    out_rows, feed_xhat_two, feed_inv_two = feed_down(rows_in, act_two, w_down_two, small_vals[1])
    d_resid, d_branch, d_pre, feed_small_two = feed_down_back(
        d_rows_out, feed_xhat_two, feed_inv_two, slope_two, w_down_two, small_vals[1]
    )
    grads = feed_grads(core, rows_low, d_pre, act_two, d_branch, shard)
    grads, d_resid, d_pre = lanes.meet((grads, d_resid, d_pre))
    g_feed_two = Scatter(*grads, spots, peers)
    lanes.launch(g_feed_two)
    d_in_rows = d_resid + back_product(d_pre, w_up_two)
    back = served_back(
        select_rows,
        split_low(d_in_rows, 2),
        cot_flat,
        attn_xhat_two,
        attn_inv_two,
        small_vals[1],
        w_out_two,
    )
    d_resid, d_branch, d_mixed, sums_out = lanes.meet(back, g_feed_two)
    d_mixed = lanes.settle(d_mixed, g_feed_two)
    lanes.launch(g_feed_two)
    back = attend_core_back(
        core, qkv_two, d_mixed, lse_two, layer_low, mixed_two, d_branch, seq_lengths
    )
    (d_qkv, sums, *grads), d_resid = lanes.meet((back, d_resid), g_feed_two)
    attn_sums_two, out_sums_two = sums, sums_out
    g_attn_two = Scatter(*grads, spots, peers)
    d_resid = lanes.settle(d_resid, g_feed_two)
    lanes.launch(g_feed_two, g_attn_two)
    back = layer_back(
        d_resid,
        d_qkv,
        w_in_two,
        feed_xhat_one,
        feed_inv_one,
        small_vals[0],
        w_down_one,
        slope_one,
    )
    d_resid, d_branch, d_pre, feed_small_one = lanes.meet(back, g_attn_two, g_feed_two)
    d_branch = lanes.settle(d_branch, g_attn_two, g_feed_two)
    lanes.launch(g_attn_two, (g_feed_two, 2))
    grads = feed_grads(core, low_one, d_pre, act_one, d_branch, shard)
    grads, d_resid, d_pre = lanes.meet((grads, d_resid, d_pre), g_attn_two, g_feed_two)
    g_feed_one = Scatter(*grads, spots, peers)
    d_pre = lanes.settle(d_pre, g_attn_two)
    lanes.launch(g_feed_one, g_attn_two)
    back = feed_back(
        d_resid, d_pre, w_up_one, attn_xhat_one, attn_inv_one, small_vals[0], w_out_one
    )
    d_resid, d_branch, d_mixed, sums_out = lanes.meet(back, g_feed_one, g_attn_two)
    d_mixed = lanes.settle(d_mixed, g_feed_one, g_attn_two)
    lanes.launch(g_feed_one, (g_attn_two, 2), g_feed_two)
    small_grads = small_tile(
        (sums_out,) + feed_small_one,
        (out_sums_two,) + feed_small_two,
        attn_sums_two,
        model_width,
    )
    back = attend_core_back(
        core, qkv_one, d_mixed, lse_one, flat_low, mixed_one, d_branch, seq_lengths, small_grads
    )
    back = lanes.meet(
        (back, d_resid, attended_two, out_rows), g_feed_one, g_attn_two, g_feed_two
    )
    (d_qkv, sums, *grads), d_resid, attended_two, out_rows = back
    grads = lanes.settle(grads, g_feed_one, g_attn_two)
    g_attn_one = Scatter(*grads, spots, peers)
    lanes.launch(g_attn_one, g_feed_one, g_attn_two)
    d_tokens = project_in_back(d_resid, d_qkv, w_in_one).astype(jnp.bfloat16)
    d_tokens = lanes.meet(d_tokens, g_attn_one)
    lanes.launch(g_attn_one)
    lanes.meet((), g_feed_one, g_attn_two)
    lanes.launch((g_feed_one, 2))
    attended_two, out_rows = lanes.meet((attended_two, out_rows), g_attn_one, g_feed_one)
    lanes.launch(g_attn_one, g_feed_one)
    output_flat = jnp.where(
        flat_mask,
        weight_grad(select_rows, out_rows.astype(jnp.bfloat16)),
        attended_two,
    ).astype(jnp.bfloat16)
    output_flat = lanes.meet(output_flat, g_attn_one, g_feed_one)
    lanes.launch(g_attn_one)
    lanes.finish((), g_feed_one, g_attn_two, g_feed_two, g_attn_one)
    owned = {
        "attn0": g_attn_one.result(),
        "feed0": g_feed_one.result(),
        "attn1": g_attn_two.result(),
        "feed1": g_feed_two.result(),
    }
    partial_squares = sum(jnp.sum(jnp.square(owned[name].astype(jnp.float32))) for name in owned)
    raw = {name: (owned[name], swap(owned[name])) for name in owned}
    both = {name: both_sides(*raw[name], core) for name in raw}

    def joined(name, start, width):
        return jnp.concatenate([part[:, start : start + width] for part in both[name]], axis=1)

    def down_rows(name):
        return jnp.concatenate(
            [joined(name, hidden_half + part * third, third) for part in range(4)], axis=0
        )

    reduced = (
        order_attn(core, raw["attn0"], raw["attn1"], model_width),
        jnp.stack([joined(name, 0, hidden_half) for name in ("feed0", "feed1")]).astype(
            jnp.float32
        ),
        jnp.stack([down_rows(name) for name in ("feed0", "feed1")]),
        jnp.stack([part[:, wide : wide + 12].T for part in both["attn0"]]),
    )
    partial_squares = partial_squares.reshape(1, 1)
    partial_squares = partial_squares + swap(partial_squares)
    hops = [
        (stage, 1 << at)
        for stage, bits in enumerate(routes(peers)[0])
        for at in range(len(bits))
    ]
    for stage, turn in hops[:-1]:
        partial_squares = partial_squares + shift(partial_squares, stage, turn, peers)
    reduced, partial_squares = lax.optimization_barrier((reduced, partial_squares))
    moved = shift(partial_squares, *hops[-1], peers)
    square_total = (partial_squares + moved)[0, 0]
    grad_norm = jnp.sqrt(square_total).reshape(1)
    clip_scale = jnp.minimum(1.0, CLIP_NORM / (grad_norm[0] + 1e-06))
    step_value = step_count[0].astype(jnp.float32)
    attn_new = adam_update(
        attn_master,
        attn_first,
        attn_second,
        reduced[0],
        clip_scale,
        step_value,
        WEIGHT_DECAY,
        LEARN_RATE,
    )
    up_new = adam_update(
        up_master, up_first, up_second, reduced[1], clip_scale, step_value, WEIGHT_DECAY, LEARN_RATE
    )
    down_new = adam_update(
        down_master,
        down_first,
        down_second,
        reduced[2],
        clip_scale,
        step_value,
        WEIGHT_DECAY,
        LEARN_RATE,
    )
    small_new = adam_update(
        small_master, small_first, small_second, reduced[3], clip_scale, step_value, 0.0, SMALL_RATE
    )
    output = output_flat.reshape(seq_count, length, model_width)
    input_grad = d_tokens.reshape(seq_count, length, model_width)
    return (output, input_grad, grad_norm) + attn_new + up_new + down_new + small_new


def solution(mesh):
    return jax.shard_map(
        per_device,
        mesh=mesh,
        in_specs=(
            P(("dp", "bal"), None, None),
            P(("dp", "bal"), None, None),
            P(("dp", "bal")),
            P(("dp", "bal"), None),
            P(),
            P(None, None, "bal", None),
            P(None, None, "bal", None),
            P(None, None, "bal", None),
            P(None, "bal", None),
            P(None, "bal", None),
            P(None, "bal", None),
            P(None, "bal", None),
            P(None, "bal", None),
            P(None, "bal", None),
            P(None, None, "bal"),
            P(None, None, "bal"),
            P(None, None, "bal"),
        ),
        out_specs=(
            P(("dp", "bal"), None, None),
            P(("dp", "bal"), None, None),
            P(),
            P(None, None, "bal", None),
            P(None, None, "bal", None),
            P(None, None, "bal", None),
            P(None, None, "bal", None),
            P(None, "bal", None),
            P(None, "bal", None),
            P(None, "bal", None),
            P(None, "bal", None),
            P(None, "bal", None),
            P(None, "bal", None),
            P(None, "bal", None),
            P(None, "bal", None),
            P(None, None, "bal"),
            P(None, None, "bal"),
            P(None, None, "bal"),
            P(None, None, "bal"),
        ),
        check_vma=False,
    )
```

```python
import functools
import math

import jax
import jax.numpy as jnp
import numpy as np
from jax import lax
from jax.experimental import pallas as pl
from jax.experimental.pallas import tpu as pltpu
from jax.sharding import PartitionSpec as P

HEADS = 12
HEAD_DIM = 64
MCAP = 384
LANES = 128
QUERY_BLOCK = 256
HIDDEN_BLOCK = 512
LIGHT = pl.CostEstimate(flops=3000000000, bytes_accessed=8000000, transcendentals=0)


LN_EPS = 1e-06
NEG_FILL = -1000000000.0
CLIP_NORM = 1.0
LEARN_RATE = 0.05
SMALL_RATE = 0.25
BETA_FIRST = 0.9
BETA_SECOND = 0.999
ADAM_EPS = 1e-08
WEIGHT_DECAY = 0.01


def forward_product(left_side, right_side):
    return jnp.dot(left_side, right_side, preferred_element_type=jnp.float32)


def weight_grad(left_side, right_side):
    return lax.dot_general(
        left_side, right_side, (((0,), (0,)), ((), ())), preferred_element_type=jnp.float32
    )


def back_product(left_side, right_side):
    return lax.dot_general(
        left_side, right_side, (((1,), (1,)), ((), ())), preferred_element_type=jnp.float32
    )


def norm_forward(residual, norm_gain, norm_shift):
    centered = residual - jnp.mean(residual, axis=-1, keepdims=True)
    variance = jnp.mean(centered * centered, axis=-1, keepdims=True)
    inv_std = lax.rsqrt(variance + LN_EPS)
    normal_part = centered * inv_std
    return (normal_part * norm_gain + norm_shift, normal_part, inv_std)


def norm_backward(d_out, normal_part, inv_std, norm_gain):
    d_normal = d_out * norm_gain
    d_resid = inv_std * (
        d_normal
        - jnp.mean(d_normal, axis=-1, keepdims=True)
        - normal_part * jnp.mean(d_normal * normal_part, axis=-1, keepdims=True)
    )
    return (
        d_resid,
        jnp.sum(d_out * normal_part, axis=0, keepdims=True),
        jnp.sum(d_out, axis=0, keepdims=True),
    )


def gelu_slope(pre_act):
    return (
        0.5 * (1.0 + lax.erf(pre_act * 0.7071067811865476))
        + pre_act * jnp.exp(-0.5 * pre_act * pre_act) * 0.3989422804014327
    )


def key_side(keys, bias, lane, half):
    own = (lane < HEAD_DIM) if half == 0 else (lane >= HEAD_DIM)
    spare = HEAD_DIM if half == 0 else 0
    return jnp.where(own, keys, jnp.where(lane == spare, bias, 0.0)).astype(jnp.bfloat16)


def query_side(queries, lane, half):
    own = (lane < HEAD_DIM) if half == 0 else (lane >= HEAD_DIM)
    spare = HEAD_DIM if half == 0 else 0
    return jnp.where(own, queries, jnp.where(lane == spare, 1.0, 0.0)).astype(jnp.bfloat16)


def one_head(rows, lane, half):
    own = (lane < HEAD_DIM) if half == 0 else (lane >= HEAD_DIM)
    return jnp.where(own, rows, 0.0).astype(jnp.bfloat16)


def pair_of(ref, part, pair):
    width = ref.shape[1] // 3
    at = pl.multiple_of(part * width + pair * LANES, LANES)
    return ref[:, pl.ds(at, LANES)].astype(jnp.float32)


def attend_kernel(len_ref, qkv_lo, qkv_hi, mixed_ref, lse_ref, ot_ref):
    rows = mixed_ref.shape[0]
    width = qkv_lo.shape[1] // 3
    pairs = width // LANES
    real = len_ref[pl.program_id(0)]
    lane = lax.broadcasted_iota(jnp.int32, (rows, LANES), 1)
    place_key = lax.broadcasted_iota(jnp.int32, (rows, LANES), 0)
    bias = jnp.where(place_key < real, 0.0, NEG_FILL)
    for side, qkv_ref in enumerate((qkv_lo, qkv_hi)):

        def one_pair(pair, carry, side=side, qkv_ref=qkv_ref):
            queries = pair_of(qkv_ref, 0, pair) * (1.0 / math.sqrt(HEAD_DIM))
            keys = pair_of(qkv_ref, 1, pair)
            values_t = pair_of(qkv_ref, 2, pair).T.astype(jnp.bfloat16)
            scored = []
            for half in range(2):
                keys_one = key_side(keys, bias, lane, half)
                queries_one = query_side(queries, lane, half)
                for at in range(0, rows, QUERY_BLOCK):
                    cols = slice(at, at + QUERY_BLOCK)
                    scored.append((half, cols, back_product(keys_one, queries_one[cols])))
            weighed = []
            for half, cols, scores in scored:
                head = side * 2 * pairs + 2 * pair + half
                top = jnp.max(scores, axis=0, keepdims=True)
                exps = jnp.exp(scores - top)
                total = jnp.sum(exps, axis=0, keepdims=True)
                lse_ref[pl.ds(head, 1), cols] = top + jnp.log(total)
                weighed.append((half, cols, exps.astype(jnp.bfloat16), total))
            for half, cols, exps, total in weighed:
                lanes = slice(half * HEAD_DIM, (half + 1) * HEAD_DIM)
                ot_ref[lanes, cols] = forward_product(values_t[lanes], exps) / total
            at = pl.multiple_of(side * width + pair * LANES, LANES)
            mixed_ref[:, pl.ds(at, LANES)] = ot_ref[...].T.astype(jnp.bfloat16)
            return carry

        lax.fori_loop(0, pairs, one_pair, 0)


def attend_core(qkv_lo, qkv_hi, seq_lengths):
    total, wide = qkv_lo.shape
    seqs = seq_lengths.shape[0]
    rows, width = total // seqs, 2 * wide // 3
    heads = width // HEAD_DIM
    lse_rows = -(-heads // 8) * 8
    side = pl.BlockSpec((rows, wide), lambda seq, lens: (seq, 0))
    return pl.pallas_call(
        attend_kernel,
        out_shape=(
            jax.ShapeDtypeStruct((total, width), jnp.bfloat16),
            jax.ShapeDtypeStruct((seqs, lse_rows, rows), jnp.float32),
        ),
        grid_spec=pltpu.PrefetchScalarGridSpec(
            num_scalar_prefetch=1,
            grid=(seqs,),
            in_specs=[side, side],
            out_specs=[
                pl.BlockSpec((rows, width), lambda seq, lens: (seq, 0)),
                pl.BlockSpec((None, lse_rows, rows), lambda seq, lens: (seq, 0, 0)),
            ],
            scratch_shapes=[pltpu.VMEM((LANES, rows), jnp.float32)],
        ),
        compiler_params=pltpu.CompilerParams(vmem_limit_bytes=32 << 20),
        cost_estimate=LIGHT,
        name="attend",
    )(seq_lengths, qkv_lo, qkv_hi)


def attend_back_kernel(small_rows, len_ref, core_ref, *refs):
    qkv_lo, qkv_hi, d_mixed_ref, lse_ref = refs[:4]
    late = refs[4:7]
    small_ref = refs[7] if small_rows else None
    d_out_ref, sums_ref, far_ref, own_ref, dqt_ref, d_qkv_ref, held_ref, sems = refs[-8:]
    loads = [
        pltpu.make_async_copy(ref, held_ref.at[number], sems.at[number])
        for number, ref in enumerate(late)
    ]
    seq = pl.program_id(0)
    rows = d_mixed_ref.shape[0]
    width = qkv_lo.shape[1] // 3
    pairs = width // LANES
    scale = 1.0 / math.sqrt(HEAD_DIM)
    real = len_ref[seq]
    first_seq = seq == 0

    @pl.when(first_seq)
    def _():
        for load in loads:
            load.start()

    here = pl.ds(pl.multiple_of(seq * rows, LANES), rows)
    lane = lax.broadcasted_iota(jnp.int32, (rows, LANES), 1)
    place_key = lax.broadcasted_iota(jnp.int32, (rows, LANES), 0)
    bias = jnp.where(place_key < real, 0.0, NEG_FILL)
    for side, qkv_ref in enumerate((qkv_lo, qkv_hi)):

        def one_pair(pair, carry, side=side, qkv_ref=qkv_ref):
            queries = pair_of(qkv_ref, 0, pair) * scale
            keys = pair_of(qkv_ref, 1, pair)
            values = pair_of(qkv_ref, 2, pair)
            at_mixed = pl.multiple_of(side * width + pair * LANES, LANES)
            d_mixed = d_mixed_ref[:, pl.ds(at_mixed, LANES)].astype(jnp.float32)
            keys_t = keys.T.astype(jnp.bfloat16)
            scored = []
            for half in range(2):
                keys_one = key_side(keys, bias, lane, half)
                queries_one = query_side(queries, lane, half)
                values_only = one_head(values, lane, half)
                queries_only = one_head(queries, lane, half)
                d_mixed_only = one_head(d_mixed, lane, half)
                for at in range(0, rows, QUERY_BLOCK):
                    cols = slice(at, at + QUERY_BLOCK)
                    scores = back_product(keys_one, queries_one[cols])
                    d_probs = back_product(values_only, d_mixed_only[cols])
                    scored.append(
                        (half, cols, scores, d_probs, queries_only[cols], d_mixed_only[cols])
                    )
            weighed = []
            for half, cols, scores, d_probs, queries_only, d_mixed_only in scored:
                head = side * 2 * pairs + 2 * pair + half
                probs = jnp.exp(scores - lse_ref[pl.ds(head, 1), cols])
                row_part = jnp.sum(probs * d_probs, axis=0, keepdims=True)
                d_scores = (probs * (d_probs - row_part)).astype(jnp.bfloat16)
                weighed.append(
                    (half, cols, probs.astype(jnp.bfloat16), d_scores, queries_only, d_mixed_only)
                )
            d_keys = d_values = None
            for half, cols, probs, d_scores, queries_only, d_mixed_only in weighed:
                value_part = forward_product(probs, d_mixed_only)
                key_part = forward_product(d_scores, queries_only)
                d_values = value_part if d_values is None else d_values + value_part
                d_keys = key_part if d_keys is None else d_keys + key_part
                lanes = slice(half * HEAD_DIM, (half + 1) * HEAD_DIM)
                dqt_ref[lanes, cols] = forward_product(keys_t[lanes], d_scores)
            for part, value in enumerate((dqt_ref[...].T * scale, d_keys, d_values)):
                at = pl.multiple_of(part * width + pair * LANES, LANES)
                rounded = value.astype(jnp.bfloat16)
                d_qkv_ref[side, here, pl.ds(at, LANES)] = rounded
                d_out_ref[side, :, pl.ds(at, LANES)] = rounded
                if part != 1:
                    column = jnp.sum(rounded.astype(jnp.float32), axis=0, keepdims=True)
                    column = jnp.broadcast_to(column, (8, LANES))
                    known = sums_ref[side, :, pl.ds(at, LANES)]
                    sums_ref[side, :, pl.ds(at, LANES)] = jnp.where(
                        first_seq, column, column + known
                    )
            return carry

        lax.fori_loop(0, pairs, one_pair, 0)

    @pl.when(seq == pl.num_programs(0) - 1)
    def _():
        core = core_ref[0]
        for load in loads:
            load.wait()
        d_branch_ref = held_ref.at[2]
        for out_ref, side in ((far_ref, 1 - core), (own_ref, core)):
            out_ref[:, : 3 * width] = weight_grad(held_ref[0], d_qkv_ref[side]).astype(
                jnp.bfloat16
            )
            cols = pl.ds(pl.multiple_of(side * width, LANES), width)
            out_ref[:, 3 * width : 4 * width] = weight_grad(
                held_ref[1], d_branch_ref[:, cols]
            ).astype(jnp.bfloat16)
            if small_ref is not None:
                tile = small_ref[side]
                number = lax.broadcasted_iota(jnp.int32, tile.shape, 0)
                for row, start in ((0, 0), (1, 2 * width)):
                    line = jnp.concatenate(
                        [sums_ref[one, :1, start : start + width] for one in range(2)], axis=1
                    )
                    tile = jnp.where((number == row) & (side == 0), line, tile)
                out_ref[:, 4 * width :] = tile.T.astype(jnp.bfloat16)


def attend_core_back(
    core, qkv, d_mixed, lse, x_low, mixed_heads, d_branch, seq_lengths, small=None
):
    qkv_lo, qkv_hi = qkv
    total, wide = qkv_lo.shape
    seqs = seq_lengths.shape[0]
    rows, width = total // seqs, 2 * wide // 3
    extra = 0 if small is None else small.shape[1]
    once = pl.Buffered(1)
    side = pl.BlockSpec((rows, wide), lambda seq, *_: (seq, 0))
    whole = pl.BlockSpec(memory_space=pl.ANY)
    specs = [
        side,
        side,
        pl.BlockSpec((rows, width), lambda seq, *_: (seq, 0)),
        pl.BlockSpec((None, lse.shape[1], rows), lambda seq, *_: (seq, 0, 0)),
        whole,
        whole,
        whole,
    ]
    given = [qkv_lo, qkv_hi, d_mixed, lse, x_low, mixed_heads, d_branch]
    if small is not None:
        specs.append(pl.BlockSpec(small.shape, lambda seq, *_: (0, 0, 0), pipeline_mode=once))
        given.append(small)
    grad_shape = (width, 2 * width + extra)
    grad_spec = pl.BlockSpec(grad_shape, lambda seq, *_: (0, 0), pipeline_mode=once)
    return pl.pallas_call(
        functools.partial(attend_back_kernel, extra),
        out_shape=(
            jax.ShapeDtypeStruct((2, total, wide), jnp.bfloat16),
            jax.ShapeDtypeStruct((2, 8, wide), jnp.float32),
            jax.ShapeDtypeStruct(grad_shape, jnp.bfloat16),
            jax.ShapeDtypeStruct(grad_shape, jnp.bfloat16),
        ),
        grid_spec=pltpu.PrefetchScalarGridSpec(
            num_scalar_prefetch=2,
            grid=(seqs,),
            in_specs=specs,
            out_specs=[
                pl.BlockSpec((2, rows, wide), lambda seq, *_: (0, seq, 0)),
                pl.BlockSpec((2, 8, wide), lambda seq, *_: (0, 0, 0)),
                grad_spec,
                grad_spec,
            ],
            scratch_shapes=[
                pltpu.VMEM((LANES, rows), jnp.float32),
                pltpu.VMEM((2, total, wide), jnp.bfloat16),
                pltpu.VMEM((3, total, width), jnp.bfloat16),
                pltpu.SemaphoreType.DMA((3,)),
            ],
        ),
        compiler_params=pltpu.CompilerParams(vmem_limit_bytes=60 << 20),
        cost_estimate=LIGHT,
        name="attend_back",
    )(seq_lengths, core.reshape(1).astype(jnp.int32), *given)


def half_of(rows, side):
    width = rows.shape[1] // 2
    return lax.dynamic_slice_in_dim(rows, side * width, width, 1)


def project_in(flat_low, in_layer, small_layer):
    third = flat_low.shape[1] // 2
    qkv = []
    for side in range(2):
        cols = slice(side * third, (side + 1) * third)
        bias = jnp.concatenate(
            [small_layer[0, cols], jnp.zeros((third,), jnp.float32), small_layer[1, cols]]
        )
        part = forward_product(flat_low, in_layer[side]) + bias
        qkv.append(part.astype(jnp.bfloat16))
    return qkv


def project_in_back(d_resid, d_qkv, in_layer):
    return d_resid + sum(back_product(d_qkv[side], in_layer[side]) for side in range(2))


def small_tile_kernel(*refs):
    out_ref = refs[-1]
    width = out_ref.shape[2]
    out_ref[...] = jnp.zeros_like(out_ref)
    third = width // 2

    def put(layer, row, ref, parts):
        for part in range(parts):
            cols = slice(part * width, (part + 1) * width)
            out_ref[layer, row + part : row + part + 1, :] = ref[:1, cols]

    for layer in range(2):
        out_sums, pre_sums, feed_sums = refs[3 * layer : 3 * layer + 3]
        put(layer, 2, out_sums, 3)
        put(layer, 5, pre_sums, 4)
        put(layer, 9, feed_sums, 3)
    attn_sums = refs[6]
    for row, start in ((0, 0), (1, 2 * third)):
        for side in range(2):
            out_ref[1, row : row + 1, side * third : (side + 1) * third] = attn_sums[
                side, :1, start : start + third
            ]


def small_tile(one, two, attn_sums, width):
    return pl.pallas_call(
        small_tile_kernel,
        out_shape=jax.ShapeDtypeStruct((2, LANES, width), jnp.float32),
        cost_estimate=LIGHT,
        name="small_tile",
    )(*one, *two, attn_sums)


def project_norm_kernel(rows_ref, weight_ref, resid_ref, bias_ref, gain_ref, shift_ref, *outs):
    normed_ref, low_ref, xhat_ref, inv_ref = outs
    branch = forward_product(rows_ref[...], weight_ref[...]) + bias_ref[...]
    normed, normal_part, inv_std = norm_forward(
        resid_ref[...].astype(jnp.float32) + branch, gain_ref[...], shift_ref[...]
    )
    normed_ref[...] = normed
    low_ref[...] = normed.astype(jnp.bfloat16)
    xhat_ref[...] = normal_part
    inv_ref[...] = jnp.broadcast_to(inv_std, inv_ref.shape)


def project_norm(rows_low, weight, resid, small_layer, first):
    total, depth = rows_low.shape
    width = resid.shape[1]
    block = math.gcd(total, 256)
    row = pl.BlockSpec((block, width), lambda at: (at, 0))
    line = pl.BlockSpec((1, width), lambda at: (0, 0))
    return pl.pallas_call(
        project_norm_kernel,
        out_shape=(
            jax.ShapeDtypeStruct((total, width), jnp.float32),
            jax.ShapeDtypeStruct((total, width), jnp.bfloat16),
            jax.ShapeDtypeStruct((total, width), jnp.float32),
            jax.ShapeDtypeStruct((total, LANES), jnp.float32),
        ),
        grid=(total // block,),
        in_specs=[
            pl.BlockSpec((block, depth), lambda at: (at, 0)),
            pl.BlockSpec((depth, width), lambda at: (0, 0), pipeline_mode=pl.Buffered(1)),
            row,
            line,
            line,
            line,
        ],
        out_specs=[row, row, row, pl.BlockSpec((block, LANES), lambda at: (at, 0))],
        compiler_params=pltpu.CompilerParams(vmem_limit_bytes=24 << 20),
        cost_estimate=LIGHT,
        name="project_norm",
    )(rows_low, weight, resid, *[small_layer[at : at + 1] for at in range(first, first + 3)])


def served_back_kernel(
    select_ref, d_served_ref, cot_ref, xhat_ref, inv_ref, gain_ref, out_ref, *outs
):
    out_resid_ref, d_branch_ref, d_mixed_ref, sums_ref = outs
    width = cot_ref.shape[1]
    select = select_ref[...]
    both = weight_grad(select, d_served_ref[...])
    hit = weight_grad(select, jnp.ones((select.shape[0], LANES), jnp.bfloat16))[:, :1] > 0.5
    d_out = jnp.where(hit, both[:, :width] + both[:, width:], cot_ref[...].astype(jnp.float32))
    xhat = xhat_ref[...]
    d_resid, d_branch = norm_back_rows(d_out, xhat, inv_ref[:, :1], gain_ref[...])
    out_resid_ref[...] = d_resid
    d_branch_ref[...] = d_branch
    d_mixed_ref[...] = back_product(d_branch, out_ref[...]).astype(jnp.bfloat16)
    add_sums(sums_ref, (d_branch.astype(jnp.float32), d_out * xhat, d_out))


def served_back(select_rows, d_served, cot_flat, xhat, inv, small_layer, out_layer):
    total, width = cot_flat.shape
    slots = select_rows.shape[0]
    block = math.gcd(total, 256)
    row = pl.BlockSpec((block, width), lambda at: (at, 0))
    d_resid, d_branch, d_mixed, sums = pl.pallas_call(
        served_back_kernel,
        out_shape=(
            jax.ShapeDtypeStruct((total, width), jnp.float32),
            jax.ShapeDtypeStruct((total, width), jnp.bfloat16),
            jax.ShapeDtypeStruct((total, width), jnp.bfloat16),
            jax.ShapeDtypeStruct((8, 3 * width), jnp.float32),
        ),
        grid=(total // block,),
        in_specs=[
            pl.BlockSpec((slots, block), lambda at: (0, at)),
            pl.BlockSpec((slots, 2 * width), lambda at: (0, 0)),
            row,
            row,
            pl.BlockSpec((block, LANES), lambda at: (at, 0)),
            pl.BlockSpec((1, width), lambda at: (0, 0)),
            pl.BlockSpec((width, width), lambda at: (0, 0)),
        ],
        out_specs=[row, row, row, pl.BlockSpec((8, 3 * width), lambda at: (0, 0))],
        compiler_params=pltpu.CompilerParams(vmem_limit_bytes=24 << 20),
        cost_estimate=LIGHT,
        name="served_back",
    )(select_rows, d_served, cot_flat, xhat, inv, small_layer[3:4], out_layer)
    return (d_resid, d_branch, d_mixed, sums)


def feed_up_kernel(rows_ref, up_ref, bias_ref, act_ref, slope_ref):
    low_rows = rows_ref[...]
    for at in range(0, up_ref.shape[1], HIDDEN_BLOCK):
        cols = slice(at, at + HIDDEN_BLOCK)
        pre_act = forward_product(low_rows, up_ref[:, cols]) + bias_ref[:, cols]
        below = 0.5 * (1.0 + lax.erf(pre_act * 0.7071067811865476))
        density = jnp.exp(-0.5 * pre_act * pre_act) * 0.3989422804014327
        act_ref[:, cols] = (pre_act * below).astype(jnp.bfloat16)
        slope_ref[:, cols] = (below + pre_act * density).astype(jnp.bfloat16)


def feed_up(rows_low, up_layer, small_layer):
    total, width = rows_low.shape
    hidden = up_layer.shape[1]
    block = math.gcd(total, 256)
    bias = small_layer[5:9].reshape(1, hidden)
    shape = jax.ShapeDtypeStruct((total, hidden), jnp.bfloat16)
    act_low, slope = pl.pallas_call(
        feed_up_kernel,
        out_shape=(shape, shape),
        grid=(total // block,),
        in_specs=[
            pl.BlockSpec((block, width), lambda at: (at, 0)),
            pl.BlockSpec((width, hidden), lambda at: (0, 0)),
            pl.BlockSpec((1, hidden), lambda at: (0, 0)),
        ],
        out_specs=[pl.BlockSpec((block, hidden), lambda at: (at, 0))] * 2,
        compiler_params=pltpu.CompilerParams(vmem_limit_bytes=32 << 20),
        cost_estimate=LIGHT,
        name="feed_up",
    )(rows_low, up_layer, bias)
    return (act_low, slope)


def feed_down(rows_in, act_low, down_layer, small_layer):
    branch = forward_product(act_low, down_layer) + small_layer[9]
    return norm_forward(rows_in + branch, small_layer[10], small_layer[11])


def feed_down_back(d_normed, normal_part, inv_std, slope, down_layer, small_layer):
    d_resid, d_gain, d_shift = norm_backward(d_normed, normal_part, inv_std, small_layer[10])
    d_branch = d_resid.astype(jnp.bfloat16)
    d_pre = (back_product(d_branch, down_layer) * slope.astype(jnp.float32)).astype(jnp.bfloat16)
    d_bias = jnp.sum(d_pre.astype(jnp.float32), axis=0, keepdims=True)
    d_shared = jnp.sum(d_branch.astype(jnp.float32), axis=0, keepdims=True)
    small_rows = (d_bias, jnp.concatenate([d_shared, d_gain, d_shift], axis=1))
    return (d_resid, d_branch, d_pre, small_rows)


def norm_back_rows(d_out, xhat, inv, gain):
    d_normal = d_out * gain
    d_resid = inv * (
        d_normal
        - jnp.mean(d_normal, axis=-1, keepdims=True)
        - xhat * jnp.mean(d_normal * xhat, axis=-1, keepdims=True)
    )
    return (d_resid, d_resid.astype(jnp.bfloat16))


def add_sums(sums_ref, values):
    width = values[0].shape[1]
    first = pl.program_id(0) == 0
    for number, value in enumerate(values):
        cols = slice(number * width, (number + 1) * width)
        part = jnp.broadcast_to(jnp.sum(value, axis=0, keepdims=True), (8, width))
        sums_ref[:, cols] = jnp.where(first, part, part + sums_ref[:, cols])


def layer_back_kernel(
    d_resid_ref, d_qkv_ref, in_ref, xhat_ref, inv_ref, gain_ref, down_ref, slope_ref, *outs
):
    out_resid_ref, d_branch_ref, d_pre_ref, pre_sums_ref, sums_ref = outs
    d_out = d_resid_ref[...]
    for side in range(2):
        d_out = d_out + back_product(d_qkv_ref[side], in_ref[side])
    xhat = xhat_ref[...]
    d_resid, d_branch = norm_back_rows(d_out, xhat, inv_ref[:, :1], gain_ref[...])
    out_resid_ref[...] = d_resid
    d_branch_ref[...] = d_branch
    add_sums(sums_ref, (d_branch.astype(jnp.float32), d_out * xhat, d_out))
    first = pl.program_id(0) == 0
    for at in range(0, down_ref.shape[0], HIDDEN_BLOCK):
        cols = slice(at, at + HIDDEN_BLOCK)
        d_act = back_product(d_branch, down_ref[cols])
        d_pre = (d_act * slope_ref[:, cols].astype(jnp.float32)).astype(jnp.bfloat16)
        d_pre_ref[:, cols] = d_pre
        part = jnp.broadcast_to(
            jnp.sum(d_pre.astype(jnp.float32), axis=0, keepdims=True), (8, HIDDEN_BLOCK)
        )
        pre_sums_ref[:, cols] = jnp.where(first, part, part + pre_sums_ref[:, cols])


def layer_back(d_resid, d_qkv, in_layer, xhat, inv, small_layer, down_layer, slope):
    total, width = d_resid.shape
    hidden = slope.shape[1]
    wide = d_qkv.shape[2]
    block = math.gcd(total, 256)
    row = pl.BlockSpec((block, width), lambda at: (at, 0))
    hidden_row = pl.BlockSpec((block, hidden), lambda at: (at, 0))
    d_resid, d_branch, d_pre, pre_sums, sums = pl.pallas_call(
        layer_back_kernel,
        out_shape=(
            jax.ShapeDtypeStruct((total, width), jnp.float32),
            jax.ShapeDtypeStruct((total, width), jnp.bfloat16),
            jax.ShapeDtypeStruct((total, hidden), jnp.bfloat16),
            jax.ShapeDtypeStruct((8, hidden), jnp.float32),
            jax.ShapeDtypeStruct((8, 3 * width), jnp.float32),
        ),
        grid=(total // block,),
        in_specs=[
            row,
            pl.BlockSpec((2, block, wide), lambda at: (0, at, 0)),
            pl.BlockSpec((2, width, wide), lambda at: (0, 0, 0), pipeline_mode=pl.Buffered(1)),
            row,
            pl.BlockSpec((block, LANES), lambda at: (at, 0)),
            pl.BlockSpec((1, width), lambda at: (0, 0)),
            pl.BlockSpec((hidden, width), lambda at: (0, 0), pipeline_mode=pl.Buffered(1)),
            hidden_row,
        ],
        out_specs=[
            row,
            row,
            hidden_row,
            pl.BlockSpec((8, hidden), lambda at: (0, 0)),
            pl.BlockSpec((8, 3 * width), lambda at: (0, 0)),
        ],
        compiler_params=pltpu.CompilerParams(vmem_limit_bytes=46 << 20),
        cost_estimate=LIGHT,
        name="layer_back",
    )(d_resid, d_qkv, in_layer, xhat, inv, small_layer[10:11], down_layer, slope)
    return (d_resid, d_branch, d_pre, (pre_sums, sums))


def feed_back_kernel(d_resid_ref, d_pre_ref, up_ref, xhat_ref, inv_ref, gain_ref, out_ref, *outs):
    out_resid_ref, d_branch_ref, d_mixed_ref, sums_ref = outs
    d_out = d_resid_ref[...] + back_product(d_pre_ref[...], up_ref[...])
    xhat = xhat_ref[...]
    d_resid, d_branch = norm_back_rows(d_out, xhat, inv_ref[:, :1], gain_ref[...])
    out_resid_ref[...] = d_resid
    d_branch_ref[...] = d_branch
    d_mixed_ref[...] = back_product(d_branch, out_ref[...]).astype(jnp.bfloat16)
    add_sums(sums_ref, (d_branch.astype(jnp.float32), d_out * xhat, d_out))


def feed_back(d_resid, d_pre, up_layer, xhat, inv, small_layer, out_layer):
    total, width = d_resid.shape
    hidden = d_pre.shape[1]
    block = math.gcd(total, 256)
    row = pl.BlockSpec((block, width), lambda at: (at, 0))
    d_resid, d_branch, d_mixed, sums = pl.pallas_call(
        feed_back_kernel,
        out_shape=(
            jax.ShapeDtypeStruct((total, width), jnp.float32),
            jax.ShapeDtypeStruct((total, width), jnp.bfloat16),
            jax.ShapeDtypeStruct((total, width), jnp.bfloat16),
            jax.ShapeDtypeStruct((8, 3 * width), jnp.float32),
        ),
        grid=(total // block,),
        in_specs=[
            row,
            pl.BlockSpec((block, hidden), lambda at: (at, 0)),
            pl.BlockSpec((width, hidden), lambda at: (0, 0), pipeline_mode=pl.Buffered(1)),
            row,
            pl.BlockSpec((block, LANES), lambda at: (at, 0)),
            pl.BlockSpec((1, width), lambda at: (0, 0)),
            pl.BlockSpec((width, width), lambda at: (0, 0), pipeline_mode=pl.Buffered(1)),
        ],
        out_specs=[row, row, row, pl.BlockSpec((8, 3 * width), lambda at: (0, 0))],
        compiler_params=pltpu.CompilerParams(vmem_limit_bytes=40 << 20),
        cost_estimate=LIGHT,
        name="feed_back",
    )(d_resid, d_pre, up_layer, xhat, inv, small_layer[3:4], out_layer)
    return (d_resid, d_branch, d_mixed, sums)


def order_attn_kernel(core_ref, *refs):
    pairs, out_ref = (refs[:2], refs[2:4]), refs[4]
    third = out_ref.shape[3] // 2
    core = core_ref[0]
    for layer, (own_ref, far_ref) in enumerate(pairs):
        for part in range(4):
            cols = slice(part * third, (part + 1) * third)
            own, far = own_ref[:, cols], far_ref[:, cols]
            for side in range(2):
                out_ref[layer, part, :, side * third : (side + 1) * third] = jnp.where(
                    core == side, own, far
                )


def order_attn(core, one, two, width):
    local = pl.BlockSpec(memory_space=pltpu.VMEM)
    shard = one[0].shape[0]
    return pl.pallas_call(
        order_attn_kernel,
        out_shape=jax.ShapeDtypeStruct((2, 4, shard, width), jnp.bfloat16),
        grid_spec=pltpu.PrefetchScalarGridSpec(
            num_scalar_prefetch=1, grid=(), in_specs=[local] * 4, out_specs=local
        ),
        cost_estimate=LIGHT,
        name="order_attn",
    )(core.reshape(1).astype(jnp.int32), *one, *two)


def feed_grads_kernel(shard, core, low_ref, d_pre_ref, act_ref, d_branch_ref, *rest):
    far_ref, own_ref, low_t_ref, down_ref = rest
    at = pl.program_id(0)
    width = low_ref.shape[1]
    third = width // 2

    @pl.when(at == 0)
    def _():
        low_t_ref[...] = low_ref[...].T

    for step in range(4):

        @pl.when(at == step)
        def _(step=step):
            out_ref = far_ref if step < 2 else own_ref
            cols = slice((step % 2) * width, (step % 2 + 1) * width)
            out_ref[:, cols] = forward_product(low_t_ref[...], d_pre_ref[...]).astype(jnp.bfloat16)

    @pl.when(at >= 4)
    def _():
        down_ref[...] = weight_grad(act_ref[...], d_branch_ref[...])
        blocks = width // (4 * shard)
        for out_ref, side in ((far_ref, 1 - core[0]), (own_ref, core[0])):
            from_cols = pl.ds(pl.multiple_of(side * third, LANES), third)
            for block in range(blocks):
                row = pl.multiple_of(((at - 4) * blocks + block) * shard, 16)
                for part in range(4):
                    start = (block * 4 + part) * shard
                    cols = slice(2 * width + part * third, 2 * width + (part + 1) * third)
                    out_ref[pl.ds(row, shard), cols] = down_ref[
                        start : start + shard, from_cols
                    ].astype(jnp.bfloat16)


def feed_grads_plain(core, rows_low, d_pre, act_low, d_branch, shard):
    sides = []
    width = rows_low.shape[1]
    for side in (1 - core, core):
        d_up = weight_grad(rows_low, half_of(d_pre, side))
        d_down = weight_grad(act_low, half_of(d_branch, side))
        d_down = d_down.reshape(-1, 4, shard, width // 2).transpose(0, 2, 1, 3)
        sides.append(jnp.concatenate([d_up, d_down.reshape(width, -1)], axis=1))
    return [part.astype(jnp.bfloat16) for part in sides]


def feed_grads(core, rows_low, d_pre, act_low, d_branch, shard):
    total, width = rows_low.shape
    hidden = act_low.shape[1]
    if shard % 16 or hidden != 4 * width:
        return feed_grads_plain(core, rows_low, d_pre, act_low, d_branch, shard)

    def pre_at(at, core):
        step = jnp.minimum(at, 3)
        return (0, jnp.where(step < 2, 1 - core[0], core[0]) * 2 + step % 2)

    shape = jax.ShapeDtypeStruct((width, hidden), jnp.bfloat16)
    return pl.pallas_call(
        functools.partial(feed_grads_kernel, shard),
        out_shape=(shape, shape),
        grid_spec=pltpu.PrefetchScalarGridSpec(
            num_scalar_prefetch=1,
            grid=(8,),
            in_specs=[
                pl.BlockSpec((total, width), lambda at, core: (0, 0)),
                pl.BlockSpec((total, width), pre_at),
                pl.BlockSpec((total, width), lambda at, core: (0, jnp.maximum(at - 4, 0))),
                pl.BlockSpec((total, width), lambda at, core: (0, 0)),
            ],
            out_specs=[pl.BlockSpec((width, hidden), lambda at, core: (0, 0))] * 2,
            scratch_shapes=[
                pltpu.VMEM((width, total), jnp.bfloat16),
                pltpu.VMEM((width, width), jnp.float32),
            ],
        ),
        compiler_params=pltpu.CompilerParams(vmem_limit_bytes=40 << 20),
        cost_estimate=LIGHT,
        name="feed_grads",
    )(core.reshape(1).astype(jnp.int32), rows_low, d_pre, act_low, d_branch)


def row_select(token_mask, capacity):
    flat_mask = token_mask.reshape(1, -1)
    row_total = flat_mask.shape[1]
    before = (
        lax.broadcasted_iota(jnp.int32, (row_total, row_total), 0)
        < lax.broadcasted_iota(jnp.int32, (row_total, row_total), 1)
    ).astype(jnp.bfloat16)
    rank = forward_product(flat_mask.astype(jnp.bfloat16), before).astype(jnp.int32)
    slots = lax.broadcasted_iota(jnp.int32, (capacity, row_total), 0)
    return ((slots == rank) & (flat_mask == 1)).astype(jnp.bfloat16)


def split_low(wide, parts):
    pieces = []
    left = wide
    for _ in range(parts - 1):
        piece = lax.reduce_precision(left, 8, 7)
        pieces.append(piece.astype(jnp.bfloat16))
        left = left - piece
    pieces.append(left.astype(jnp.bfloat16))
    return jnp.concatenate(pieces, axis=1)


def join_low(joined, parts):
    width = joined.shape[1] // parts
    total = joined[:, :width]
    for number in range(1, parts):
        total = total + joined[:, number * width : (number + 1) * width]
    return total


def adam_update(
    master, first_moment, second_moment, gradient, clip_scale, step_value, decay_rate, rate_value
):
    clipped = gradient.astype(jnp.float32) * clip_scale
    first_new = BETA_FIRST * first_moment + (1.0 - BETA_FIRST) * clipped
    second_new = BETA_SECOND * second_moment + (1.0 - BETA_SECOND) * clipped * clipped
    first_hat = first_new / (1.0 - jnp.power(BETA_FIRST, step_value))
    second_hat = second_new / (1.0 - jnp.power(BETA_SECOND, step_value))
    master_new = master - rate_value * (
        first_hat / (jnp.sqrt(second_hat) + ADAM_EPS) + decay_rate * master
    )
    return (master_new, first_new, second_new, master_new.astype(jnp.bfloat16))


def routes(peers):
    bits = peers.bit_length() - 1
    deep = min(2, bits)
    rest = bits - deep
    x_bits = [1 << at for at in range(rest - rest // 2)]
    y_bits = [1 << at for at in range(rest - rest // 2, rest)]
    z_bits = [1 << at for at in range(rest, bits)]
    if len(x_bits) == len(y_bits):
        return ((z_bits, y_bits, x_bits), (z_bits, x_bits, y_bits))
    return ((z_bits, y_bits, x_bits), (z_bits, y_bits, x_bits))


def stage_sizes(peers):
    return [1 << len(bits) for bits in routes(peers)[0]]


def mask_of(bits, turn):
    return sum(bit for at, bit in enumerate(bits) if turn >> at & 1)


def shift(value, stage, turn, peers):
    pairs = []
    for core, path in enumerate(routes(peers)):
        mask = mask_of(path[stage], turn)
        pairs += [(core * peers + at, core * peers + (at ^ mask)) for at in range(peers)]
    return lax.ppermute(value, ("dp", "bal"), pairs)


def swap(value):
    return lax.ppermute(value, "dp", [(0, 1), (1, 0)])


def place_table(peers, core):
    masks = [
        [mask_of(sum(path, []), spot) for spot in range(peers)] for path in routes(peers)
    ]
    masks = jnp.asarray(np.array(masks, np.int32))
    mine = lax.axis_index("bal")
    own = jnp.where(core == 0, masks[0], masks[1])
    far = jnp.where(core == 0, masks[1], masks[0])
    return jnp.concatenate([mine ^ own, mine ^ far, core.reshape(1).astype(jnp.int32)])


def place_kernel(plan, count, spots, *refs):
    parts, outs = refs[:count], refs[count:]
    held, rows, _ = parts[0].shape
    core = spots[count * held]

    for number, part in enumerate(parts):
        side = core if number < count // 2 else 1 - core

        def one_block(at, carry, number=number, part=part, side=side):
            spot = spots[number * held + at]
            for (start, width, kind), out in zip(plan, outs):
                cols = pl.ds(pl.multiple_of(side * width, LANES), width)
                if kind == "stack":
                    out[side, spot] = part[at, :, start : start + width]
                elif kind == "wide":
                    out[spot, :, cols] = part[at, :, start : start + width]
                else:
                    for piece in range(4):
                        begin = start + piece * width
                        out[spot, piece * rows : (piece + 1) * rows, cols] = part[
                            at, :, begin : begin + width
                        ]
            return carry

        lax.fori_loop(0, held, one_block, 0)


def place(spots, parts, plan):
    held, rows, whole = parts[0].shape
    peers = len(parts) * held // 2
    kinds = [
        (start, 4 * width, "stack") if kind == "down" and rows % 16 else (start, width, kind)
        for start, width, kind in plan
    ]
    shapes = {
        "stack": lambda width: (2, peers, rows, width),
        "wide": lambda width: (peers, rows, 2 * width),
        "down": lambda width: (peers, 4 * rows, 2 * width),
    }
    local = pl.BlockSpec(memory_space=pltpu.VMEM)
    placed = pl.pallas_call(
        functools.partial(place_kernel, kinds, len(parts)),
        out_shape=[
            jax.ShapeDtypeStruct(shapes[kind](width), parts[0].dtype) for _, width, kind in kinds
        ],
        grid_spec=pltpu.PrefetchScalarGridSpec(
            num_scalar_prefetch=1,
            grid=(),
            in_specs=[local] * len(parts),
            out_specs=[local] * len(kinds),
        ),
        compiler_params=pltpu.CompilerParams(vmem_limit_bytes=40 << 20),
        cost_estimate=LIGHT,
        name="place",
    )(spots, *parts)
    results = []
    for part, (_, width, kind), (_, _, asked) in zip(placed, kinds, plan):
        if kind != asked:
            part = part.reshape(2, peers, rows, 4, width // 4).transpose(1, 3, 2, 0, 4)
            results.append(part.reshape(peers * rows * 4, width // 2))
        elif kind == "stack":
            results.append(part.reshape(2, peers * rows, width))
        else:
            results.append(part.reshape(-1, 2 * width))
    return results


class Gather:
    def __init__(self, mine, spots, peers, plan):
        self.kept, self.moved = [mine[None]], []
        self.spots, self.peers, self.plan = spots, peers, plan
        self.sizes = stage_sizes(peers)
        self.stage, self.turn = 0, 1

    def done(self):
        return self.stage > len(self.sizes)

    def launch(self, count):
        if self.stage == len(self.sizes):
            return [swap(part) for part in self.kept]
        stop = self.sizes[self.stage]
        stop = stop if count is None else min(stop, self.turn + count)
        turns = range(self.turn, stop)
        self.turn = stop
        return [shift(self.kept[0], self.stage, turn, self.peers) for turn in turns]

    def land(self, moved):
        self.moved += moved
        if self.stage < len(self.sizes) and len(self.moved) < self.sizes[self.stage] - 1:
            return
        whole = self.kept + self.moved
        if self.stage < len(self.sizes) - 1:
            whole = [jnp.concatenate(whole, axis=0)]
        self.kept, self.moved = whole, []
        self.stage, self.turn = self.stage + 1, 1

    def result(self):
        return place(self.spots, self.kept, self.plan)


class Scatter:
    def __init__(self, far, own, spots, peers):
        self.kept = [grads.reshape(peers, -1, grads.shape[1]) for grads in (own, far)]
        self.moved = []
        self.spots, self.peers = spots, peers
        self.sizes = stage_sizes(peers)
        self.stage, self.turn = len(self.sizes), 1

    def done(self):
        return self.stage < 0

    def launch(self, count):
        if self.stage == len(self.sizes):
            return [swap(self.kept[1])]
        stop = self.sizes[self.stage]
        stop = stop if count is None else min(stop, self.turn + count)
        turns = range(self.turn, stop)
        self.turn = stop
        return [shift(self.kept[turn], self.stage, turn, self.peers) for turn in turns]

    def land(self, moved):
        self.moved += moved
        if self.stage == len(self.sizes):
            self.kept = list(fold(self.spots, self.kept[0], self.moved[0], self.sizes[-1]))
        else:
            if len(self.moved) < self.sizes[self.stage] - 1:
                return
            pieces = self.sizes[self.stage - 1] if self.stage else 1
            size = self.kept[0].shape[0] // pieces

            def total(at):
                rows = slice(at * size, (at + 1) * size)
                adds = [part[rows].astype(jnp.float32) for part in [self.kept[0]] + self.moved]
                return sum(adds[1:], adds[0]).astype(jnp.bfloat16)

            self.kept = [total(at) for at in range(pieces)]
        self.moved = []
        self.stage, self.turn = self.stage - 1, 1

    def result(self):
        return self.kept[0][0]


class Lanes:
    def __init__(self):
        self.flying = {}

    def launch(self, *moves):
        for move in moves:
            move, count = move if isinstance(move, tuple) else (move, None)
            if not move.done():
                self.flying[move] = self.flying.get(move, []) + move.launch(count)

    def meet(self, work, *landing, ready=()):
        moves = [move for move in landing if move in self.flying]
        flown = [self.flying.pop(move) for move in moves]
        waiting = [move.kept for move in ready]
        work, flown, waiting = lax.optimization_barrier((work, flown, waiting))
        for move, moved in zip(moves, flown):
            move.land(moved)
        for move, kept in zip(ready, waiting):
            move.kept = kept
        return work

    def settle(self, work, *moves):
        return self.meet(work, ready=moves)

    def finish(self, work, *moves):
        work = self.meet(work, *moves)
        while not all(move.done() for move in moves):
            self.launch(*moves)
            work = self.meet(work, *moves)
        return work


def fold_kernel(spots, own, far, *outs):
    held = outs[0].shape[0]

    def one_block(at, carry):
        for number, out in enumerate(outs):
            spot = spots[number * held + at]
            out[at] = (own[spot].astype(jnp.float32) + far[spot].astype(jnp.float32)).astype(
                out.dtype
            )
        return carry

    lax.fori_loop(0, held, one_block, 0)


def fold(spots, own, far, pieces):
    peers, rows, width = own.shape
    shape = jax.ShapeDtypeStruct((peers // pieces, rows, width), own.dtype)
    local = pl.BlockSpec(memory_space=pltpu.VMEM)
    return pl.pallas_call(
        fold_kernel,
        out_shape=[shape] * pieces,
        grid_spec=pltpu.PrefetchScalarGridSpec(
            num_scalar_prefetch=1,
            grid=(),
            in_specs=[local, local],
            out_specs=[local] * pieces,
        ),
        compiler_params=pltpu.CompilerParams(vmem_limit_bytes=32 << 20),
        cost_estimate=LIGHT,
        name="fold",
    )(spots, own, far)


def both_sides(own, other, core):
    return (jnp.where(core == 0, own, other), jnp.where(core == 0, other, own))


def per_device(
    tokens,
    cotangent,
    seq_lengths,
    token_mask,
    step_count,
    attn_master,
    attn_first,
    attn_second,
    up_master,
    up_first,
    up_second,
    down_master,
    down_first,
    down_second,
    small_master,
    small_first,
    small_second,
):
    core = lax.axis_index("dp")
    peers = lax.axis_size("bal")
    seq_count, length, model_width = tokens.shape
    rows_total = seq_count * length
    spots = place_table(peers, core)
    shard = attn_master.shape[2]
    attn_half = lax.dynamic_slice_in_dim(attn_master, core * (model_width // 2), model_width // 2, 3)
    attn_half = attn_half.astype(jnp.bfloat16).transpose(0, 2, 1, 3).reshape(2, shard, -1)
    small_half = lax.dynamic_slice_in_dim(small_master.reshape(24, shard), core * 12, 12, 0)
    small_half = jnp.pad(small_half.astype(jnp.bfloat16).T, ((0, 0), (0, LANES - 12)))
    wide = attn_half.shape[2]
    lanes = Lanes()
    third = model_width // 2
    hidden_half = up_master.shape[2] // 2

    def down_half(layer):
        half = half_of(down_master[layer], core).astype(jnp.bfloat16)
        return [half[part * shard : (part + 1) * shard] for part in range(4)]

    up_half = [half_of(up_master[layer], core).astype(jnp.bfloat16) for layer in range(2)]
    in_one = Gather(
        jnp.concatenate([attn_half[0, :, : 3 * third], small_half], axis=1),
        spots,
        peers,
        [(0, 3 * third, "stack"), (3 * third, LANES, "stack")],
    )
    out_up_one = Gather(
        jnp.concatenate([attn_half[0, :, 3 * third :], up_half[0]], axis=1),
        spots,
        peers,
        [(0, third, "wide"), (third, hidden_half, "wide")],
    )
    down_one = Gather(
        jnp.concatenate(down_half(0), axis=1), spots, peers, [(0, third, "down")]
    )
    attn_two = Gather(
        attn_half[1], spots, peers, [(0, 3 * third, "stack"), (3 * third, third, "wide")]
    )
    up_two = Gather(up_half[1], spots, peers, [(0, hidden_half, "wide")])
    down_two = Gather(
        jnp.concatenate(down_half(1), axis=1), spots, peers, [(0, third, "down")]
    )
    flat_low = tokens.reshape(rows_total, model_width)
    cot_flat = cotangent.reshape(rows_total, model_width)
    select_rows = row_select(token_mask, MCAP)
    flat_mask = token_mask.reshape(-1, 1) == 1

    lanes.launch(in_one)
    lanes.meet((), in_one, ready=(out_up_one,))
    lanes.launch(in_one, (out_up_one, 2))
    lanes.meet((), in_one, out_up_one)
    lanes.launch(in_one, out_up_one)
    lanes.meet((), in_one, out_up_one, ready=(down_one,))
    lanes.launch(in_one, out_up_one, (down_one, 2))
    lanes.finish((), in_one)
    w_in_one, small_rows = in_one.result()
    small_vals = small_rows[:, :, :12].transpose(0, 2, 1).astype(jnp.float32)
    qkv_one = project_in(flat_low, w_in_one, small_vals[0])
    qkv_one = lanes.meet(qkv_one, out_up_one, down_one, ready=(attn_two,))
    lanes.launch(out_up_one, down_one, (attn_two, 2))
    attended = attend_core(qkv_one[0], qkv_one[1], seq_lengths)
    attended = lanes.meet(attended, out_up_one, down_one, attn_two, ready=(up_two,))
    lanes.launch(out_up_one, down_one, attn_two)
    mixed_one, lse_one = lanes.finish(attended, out_up_one)
    w_out_one, w_up_one = out_up_one.result()
    attended_one = project_norm(mixed_one, w_out_one, flat_low, small_vals[0], 2)
    attended_one = lanes.meet(attended_one, down_one, attn_two, ready=(down_two,))
    attended_one, low_one, attn_xhat_one, attn_inv_one = attended_one
    lanes.launch(down_one, attn_two, (up_two, 2))
    act_one = feed_up(low_one, w_up_one, small_vals[0])
    act_one = lanes.meet(act_one, down_one, attn_two, up_two)
    lanes.launch(down_one, attn_two, up_two, (down_two, 1))
    act_one, slope_one = lanes.finish(act_one, down_one)
    (w_down_one,) = down_one.result()
    layer_one = project_norm(act_one, w_down_one, attended_one, small_vals[0], 9)
    layer_one = lanes.meet(layer_one, attn_two, up_two, down_two)
    lanes.launch(attn_two, up_two, down_two)
    layer_one, layer_low, feed_xhat_one, feed_inv_one = lanes.finish(layer_one, attn_two)
    w_in_two, w_out_two = attn_two.result()
    w_in_two, w_out_two = lanes.meet((w_in_two, w_out_two), up_two, down_two)
    lanes.launch(up_two, down_two)
    qkv_two = project_in(layer_low, w_in_two, small_vals[1])
    attended = attend_core(qkv_two[0], qkv_two[1], seq_lengths)
    mixed_two, lse_two = lanes.meet(attended, up_two, down_two)
    lanes.launch(up_two, down_two)
    attended_two, _, attn_xhat_two, attn_inv_two = project_norm(
        mixed_two, w_out_two, layer_one, small_vals[1], 2
    )
    rows_in = join_low(forward_product(select_rows, split_low(attended_two, 3)), 3)
    d_rows_out = forward_product(select_rows, cot_flat)
    rows_in = lanes.finish(rows_in, up_two)
    rows_in = lanes.meet(rows_in, down_two)
    lanes.launch(down_two)
    (w_up_two,) = up_two.result()
    rows_low = rows_in.astype(jnp.bfloat16)
    act_two, slope_two = feed_up(rows_low, w_up_two, small_vals[1])
    act_two, slope_two = lanes.finish((act_two, slope_two), down_two)
    (w_down_two,) = down_two.result()
    out_rows, feed_xhat_two, feed_inv_two = feed_down(rows_in, act_two, w_down_two, small_vals[1])
    d_resid, d_branch, d_pre, feed_small_two = feed_down_back(
        d_rows_out, feed_xhat_two, feed_inv_two, slope_two, w_down_two, small_vals[1]
    )
    grads = feed_grads(core, rows_low, d_pre, act_two, d_branch, shard)
    grads, d_resid, d_pre = lanes.meet((grads, d_resid, d_pre))
    g_feed_two = Scatter(*grads, spots, peers)
    lanes.launch(g_feed_two)
    d_in_rows = d_resid + back_product(d_pre, w_up_two)
    back = served_back(
        select_rows,
        split_low(d_in_rows, 2),
        cot_flat,
        attn_xhat_two,
        attn_inv_two,
        small_vals[1],
        w_out_two,
    )
    d_resid, d_branch, d_mixed, sums_out = lanes.meet(back, g_feed_two)
    d_mixed = lanes.settle(d_mixed, g_feed_two)
    lanes.launch(g_feed_two)
    back = attend_core_back(
        core, qkv_two, d_mixed, lse_two, layer_low, mixed_two, d_branch, seq_lengths
    )
    (d_qkv, sums, *grads), d_resid = lanes.meet((back, d_resid), g_feed_two)
    attn_sums_two, out_sums_two = sums, sums_out
    g_attn_two = Scatter(*grads, spots, peers)
    d_resid = lanes.settle(d_resid, g_feed_two)
    lanes.launch(g_feed_two, g_attn_two)
    back = layer_back(
        d_resid,
        d_qkv,
        w_in_two,
        feed_xhat_one,
        feed_inv_one,
        small_vals[0],
        w_down_one,
        slope_one,
    )
    d_resid, d_branch, d_pre, feed_small_one = lanes.meet(back, g_attn_two, g_feed_two)
    d_branch = lanes.settle(d_branch, g_attn_two, g_feed_two)
    lanes.launch(g_attn_two, (g_feed_two, 2))
    grads = feed_grads(core, low_one, d_pre, act_one, d_branch, shard)
    grads, d_resid, d_pre = lanes.meet((grads, d_resid, d_pre), g_attn_two, g_feed_two)
    g_feed_one = Scatter(*grads, spots, peers)
    d_pre = lanes.settle(d_pre, g_attn_two)
    lanes.launch(g_feed_one, g_attn_two)
    back = feed_back(
        d_resid, d_pre, w_up_one, attn_xhat_one, attn_inv_one, small_vals[0], w_out_one
    )
    d_resid, d_branch, d_mixed, sums_out = lanes.meet(back, g_feed_one, g_attn_two)
    d_mixed = lanes.settle(d_mixed, g_feed_one, g_attn_two)
    lanes.launch(g_feed_one, (g_attn_two, 2), g_feed_two)
    small_grads = small_tile(
        (sums_out,) + feed_small_one,
        (out_sums_two,) + feed_small_two,
        attn_sums_two,
        model_width,
    )
    back = attend_core_back(
        core, qkv_one, d_mixed, lse_one, flat_low, mixed_one, d_branch, seq_lengths, small_grads
    )
    back = lanes.meet(
        (back, d_resid, attended_two, out_rows), g_feed_one, g_attn_two, g_feed_two
    )
    (d_qkv, sums, *grads), d_resid, attended_two, out_rows = back
    grads = lanes.settle(grads, g_feed_one, g_attn_two)
    g_attn_one = Scatter(*grads, spots, peers)
    lanes.launch(g_attn_one, g_feed_one, g_attn_two)
    d_tokens = project_in_back(d_resid, d_qkv, w_in_one).astype(jnp.bfloat16)
    d_tokens = lanes.meet(d_tokens, g_attn_one)
    lanes.launch(g_attn_one)
    lanes.meet((), g_feed_one, g_attn_two)
    lanes.launch((g_feed_one, 2))
    attended_two, out_rows = lanes.meet((attended_two, out_rows), g_attn_one, g_feed_one)
    lanes.launch(g_attn_one, g_feed_one)
    output_flat = jnp.where(
        flat_mask,
        weight_grad(select_rows, out_rows.astype(jnp.bfloat16)),
        attended_two,
    ).astype(jnp.bfloat16)
    output_flat = lanes.meet(output_flat, g_attn_one, g_feed_one)
    lanes.launch(g_attn_one)
    lanes.finish((), g_feed_one, g_attn_two, g_feed_two, g_attn_one)
    owned = {
        "attn0": g_attn_one.result(),
        "feed0": g_feed_one.result(),
        "attn1": g_attn_two.result(),
        "feed1": g_feed_two.result(),
    }
    partial_squares = sum(jnp.sum(jnp.square(owned[name].astype(jnp.float32))) for name in owned)
    raw = {name: (owned[name], swap(owned[name])) for name in owned}
    both = {name: both_sides(*raw[name], core) for name in raw}

    def joined(name, start, width):
        return jnp.concatenate([part[:, start : start + width] for part in both[name]], axis=1)

    def down_rows(name):
        return jnp.concatenate(
            [joined(name, hidden_half + part * third, third) for part in range(4)], axis=0
        )

    reduced = (
        order_attn(core, raw["attn0"], raw["attn1"], model_width),
        jnp.stack([joined(name, 0, hidden_half) for name in ("feed0", "feed1")]).astype(
            jnp.float32
        ),
        jnp.stack([down_rows(name) for name in ("feed0", "feed1")]),
        jnp.stack([part[:, wide : wide + 12].T for part in both["attn0"]]),
    )
    partial_squares = partial_squares.reshape(1, 1)
    partial_squares = partial_squares + swap(partial_squares)
    hops = [
        (stage, 1 << at)
        for stage, bits in enumerate(routes(peers)[0])
        for at in range(len(bits))
    ]
    for stage, turn in hops[:-1]:
        partial_squares = partial_squares + shift(partial_squares, stage, turn, peers)
    reduced, partial_squares = lax.optimization_barrier((reduced, partial_squares))
    moved = shift(partial_squares, *hops[-1], peers)
    square_total = (partial_squares + moved)[0, 0]
    grad_norm = jnp.sqrt(square_total).reshape(1)
    clip_scale = jnp.minimum(1.0, CLIP_NORM / (grad_norm[0] + 1e-06))
    step_value = step_count[0].astype(jnp.float32)
    attn_new = adam_update(
        attn_master,
        attn_first,
        attn_second,
        reduced[0],
        clip_scale,
        step_value,
        WEIGHT_DECAY,
        LEARN_RATE,
    )
    up_new = adam_update(
        up_master, up_first, up_second, reduced[1], clip_scale, step_value, WEIGHT_DECAY, LEARN_RATE
    )
    down_new = adam_update(
        down_master,
        down_first,
        down_second,
        reduced[2],
        clip_scale,
        step_value,
        WEIGHT_DECAY,
        LEARN_RATE,
    )
    small_new = adam_update(
        small_master, small_first, small_second, reduced[3], clip_scale, step_value, 0.0, SMALL_RATE
    )
    output = output_flat.reshape(seq_count, length, model_width)
    input_grad = d_tokens.reshape(seq_count, length, model_width)
    return (output, input_grad, grad_norm) + attn_new + up_new + down_new + small_new


def solution(mesh):
    return jax.shard_map(
        per_device,
        mesh=mesh,
        in_specs=(
            P(("dp", "bal"), None, None),
            P(("dp", "bal"), None, None),
            P(("dp", "bal")),
            P(("dp", "bal"), None),
            P(),
            P(None, None, "bal", None),
            P(None, None, "bal", None),
            P(None, None, "bal", None),
            P(None, "bal", None),
            P(None, "bal", None),
            P(None, "bal", None),
            P(None, "bal", None),
            P(None, "bal", None),
            P(None, "bal", None),
            P(None, None, "bal"),
            P(None, None, "bal"),
            P(None, None, "bal"),
        ),
        out_specs=(
            P(("dp", "bal"), None, None),
            P(("dp", "bal"), None, None),
            P(),
            P(None, None, "bal", None),
            P(None, None, "bal", None),
            P(None, None, "bal", None),
            P(None, None, "bal", None),
            P(None, "bal", None),
            P(None, "bal", None),
            P(None, "bal", None),
            P(None, "bal", None),
            P(None, "bal", None),
            P(None, "bal", None),
            P(None, "bal", None),
            P(None, "bal", None),
            P(None, None, "bal"),
            P(None, None, "bal"),
            P(None, None, "bal"),
            P(None, None, "bal"),
        ),
        check_vma=False,
    )
```

```python
import functools
import math

import jax
import jax.numpy as jnp
import numpy as np
from jax import lax
from jax.experimental import pallas as pl
from jax.experimental.pallas import tpu as pltpu
from jax.sharding import PartitionSpec as P

HEADS = 12
HEAD_DIM = 64
MCAP = 384
LANES = 128
QUERY_BLOCK = 256
HIDDEN_BLOCK = 512
LIGHT = pl.CostEstimate(flops=3000000000, bytes_accessed=8000000, transcendentals=0)


LN_EPS = 1e-06
NEG_FILL = -1000000000.0
CLIP_NORM = 1.0
LEARN_RATE = 0.05
SMALL_RATE = 0.25
BETA_FIRST = 0.9
BETA_SECOND = 0.999
ADAM_EPS = 1e-08
WEIGHT_DECAY = 0.01


def forward_product(left_side, right_side):
    return jnp.dot(left_side, right_side, preferred_element_type=jnp.float32)


def weight_grad(left_side, right_side):
    return lax.dot_general(
        left_side, right_side, (((0,), (0,)), ((), ())), preferred_element_type=jnp.float32
    )


def back_product(left_side, right_side):
    return lax.dot_general(
        left_side, right_side, (((1,), (1,)), ((), ())), preferred_element_type=jnp.float32
    )


def norm_forward(residual, norm_gain, norm_shift):
    centered = residual - jnp.mean(residual, axis=-1, keepdims=True)
    variance = jnp.mean(centered * centered, axis=-1, keepdims=True)
    inv_std = lax.rsqrt(variance + LN_EPS)
    normal_part = centered * inv_std
    return (normal_part * norm_gain + norm_shift, normal_part, inv_std)


def norm_backward(d_out, normal_part, inv_std, norm_gain):
    d_normal = d_out * norm_gain
    d_resid = inv_std * (
        d_normal
        - jnp.mean(d_normal, axis=-1, keepdims=True)
        - normal_part * jnp.mean(d_normal * normal_part, axis=-1, keepdims=True)
    )
    return (
        d_resid,
        jnp.sum(d_out * normal_part, axis=0, keepdims=True),
        jnp.sum(d_out, axis=0, keepdims=True),
    )


def gelu_slope(pre_act):
    return (
        0.5 * (1.0 + lax.erf(pre_act * 0.7071067811865476))
        + pre_act * jnp.exp(-0.5 * pre_act * pre_act) * 0.3989422804014327
    )


def key_side(keys, bias, lane, half):
    own = (lane < HEAD_DIM) if half == 0 else (lane >= HEAD_DIM)
    spare = HEAD_DIM if half == 0 else 0
    return jnp.where(own, keys, jnp.where(lane == spare, bias, 0.0)).astype(jnp.bfloat16)


def query_side(queries, lane, half):
    own = (lane < HEAD_DIM) if half == 0 else (lane >= HEAD_DIM)
    spare = HEAD_DIM if half == 0 else 0
    return jnp.where(own, queries, jnp.where(lane == spare, 1.0, 0.0)).astype(jnp.bfloat16)


def one_head(rows, lane, half):
    own = (lane < HEAD_DIM) if half == 0 else (lane >= HEAD_DIM)
    return jnp.where(own, rows, 0.0).astype(jnp.bfloat16)


def pair_of(ref, part, pair):
    width = ref.shape[1] // 3
    at = pl.multiple_of(part * width + pair * LANES, LANES)
    return ref[:, pl.ds(at, LANES)].astype(jnp.float32)


def attend_kernel(len_ref, qkv_lo, qkv_hi, mixed_ref, lse_ref, ot_ref):
    rows = mixed_ref.shape[0]
    width = qkv_lo.shape[1] // 3
    pairs = width // LANES
    real = len_ref[pl.program_id(0)]
    lane = lax.broadcasted_iota(jnp.int32, (rows, LANES), 1)
    place_key = lax.broadcasted_iota(jnp.int32, (rows, LANES), 0)
    bias = jnp.where(place_key < real, 0.0, NEG_FILL)
    for side, qkv_ref in enumerate((qkv_lo, qkv_hi)):

        def one_pair(pair, carry, side=side, qkv_ref=qkv_ref):
            queries = pair_of(qkv_ref, 0, pair) * (1.0 / math.sqrt(HEAD_DIM))
            keys = pair_of(qkv_ref, 1, pair)
            values_t = pair_of(qkv_ref, 2, pair).T.astype(jnp.bfloat16)
            scored = []
            for half in range(2):
                keys_one = key_side(keys, bias, lane, half)
                queries_one = query_side(queries, lane, half)
                for at in range(0, rows, QUERY_BLOCK):
                    cols = slice(at, at + QUERY_BLOCK)
                    scored.append((half, cols, back_product(keys_one, queries_one[cols])))
            weighed = []
            for half, cols, scores in scored:
                head = side * 2 * pairs + 2 * pair + half
                top = jnp.max(scores, axis=0, keepdims=True)
                exps = jnp.exp(scores - top)
                total = jnp.sum(exps, axis=0, keepdims=True)
                lse_ref[pl.ds(head, 1), cols] = top + jnp.log(total)
                weighed.append((half, cols, exps.astype(jnp.bfloat16), total))
            for half, cols, exps, total in weighed:
                lanes = slice(half * HEAD_DIM, (half + 1) * HEAD_DIM)
                ot_ref[lanes, cols] = forward_product(values_t[lanes], exps) / total
            at = pl.multiple_of(side * width + pair * LANES, LANES)
            mixed_ref[:, pl.ds(at, LANES)] = ot_ref[...].T.astype(jnp.bfloat16)
            return carry

        lax.fori_loop(0, pairs, one_pair, 0, unroll=True)


def attend_core(qkv_lo, qkv_hi, seq_lengths):
    total, wide = qkv_lo.shape
    seqs = seq_lengths.shape[0]
    rows, width = total // seqs, 2 * wide // 3
    heads = width // HEAD_DIM
    lse_rows = -(-heads // 8) * 8
    side = pl.BlockSpec((rows, wide), lambda seq, lens: (seq, 0))
    return pl.pallas_call(
        attend_kernel,
        out_shape=(
            jax.ShapeDtypeStruct((total, width), jnp.bfloat16),
            jax.ShapeDtypeStruct((seqs, lse_rows, rows), jnp.float32),
        ),
        grid_spec=pltpu.PrefetchScalarGridSpec(
            num_scalar_prefetch=1,
            grid=(seqs,),
            in_specs=[side, side],
            out_specs=[
                pl.BlockSpec((rows, width), lambda seq, lens: (seq, 0)),
                pl.BlockSpec((None, lse_rows, rows), lambda seq, lens: (seq, 0, 0)),
            ],
            scratch_shapes=[pltpu.VMEM((LANES, rows), jnp.float32)],
        ),
        compiler_params=pltpu.CompilerParams(vmem_limit_bytes=32 << 20),
        cost_estimate=LIGHT,
        name="attend",
    )(seq_lengths, qkv_lo, qkv_hi)


def attend_back_kernel(small_rows, len_ref, core_ref, *refs):
    qkv_lo, qkv_hi, d_mixed_ref, lse_ref = refs[:4]
    late = refs[4:7]
    small_ref = refs[7] if small_rows else None
    d_out_ref, sums_ref, far_ref, own_ref, dqt_ref, d_qkv_ref, held_ref, sems = refs[-8:]
    loads = [
        pltpu.make_async_copy(ref, held_ref.at[number], sems.at[number])
        for number, ref in enumerate(late)
    ]
    seq = pl.program_id(0)
    rows = d_mixed_ref.shape[0]
    width = qkv_lo.shape[1] // 3
    pairs = width // LANES
    scale = 1.0 / math.sqrt(HEAD_DIM)
    real = len_ref[seq]
    first_seq = seq == 0

    @pl.when(first_seq)
    def _():
        for load in loads:
            load.start()

    here = pl.ds(pl.multiple_of(seq * rows, LANES), rows)
    lane = lax.broadcasted_iota(jnp.int32, (rows, LANES), 1)
    place_key = lax.broadcasted_iota(jnp.int32, (rows, LANES), 0)
    bias = jnp.where(place_key < real, 0.0, NEG_FILL)
    for side, qkv_ref in enumerate((qkv_lo, qkv_hi)):

        def one_pair(pair, carry, side=side, qkv_ref=qkv_ref):
            queries = pair_of(qkv_ref, 0, pair) * scale
            keys = pair_of(qkv_ref, 1, pair)
            values = pair_of(qkv_ref, 2, pair)
            at_mixed = pl.multiple_of(side * width + pair * LANES, LANES)
            d_mixed = d_mixed_ref[:, pl.ds(at_mixed, LANES)].astype(jnp.float32)
            keys_t = keys.T.astype(jnp.bfloat16)
            scored = []
            for half in range(2):
                keys_one = key_side(keys, bias, lane, half)
                queries_one = query_side(queries, lane, half)
                values_only = one_head(values, lane, half)
                queries_only = one_head(queries, lane, half)
                d_mixed_only = one_head(d_mixed, lane, half)
                for at in range(0, rows, QUERY_BLOCK):
                    cols = slice(at, at + QUERY_BLOCK)
                    scores = back_product(keys_one, queries_one[cols])
                    d_probs = back_product(values_only, d_mixed_only[cols])
                    scored.append(
                        (half, cols, scores, d_probs, queries_only[cols], d_mixed_only[cols])
                    )
            weighed = []
            for half, cols, scores, d_probs, queries_only, d_mixed_only in scored:
                head = side * 2 * pairs + 2 * pair + half
                probs = jnp.exp(scores - lse_ref[pl.ds(head, 1), cols])
                row_part = jnp.sum(probs * d_probs, axis=0, keepdims=True)
                d_scores = (probs * (d_probs - row_part)).astype(jnp.bfloat16)
                weighed.append(
                    (half, cols, probs.astype(jnp.bfloat16), d_scores, queries_only, d_mixed_only)
                )
            d_keys = d_values = None
            for half, cols, probs, d_scores, queries_only, d_mixed_only in weighed:
                value_part = forward_product(probs, d_mixed_only)
                key_part = forward_product(d_scores, queries_only)
                d_values = value_part if d_values is None else d_values + value_part
                d_keys = key_part if d_keys is None else d_keys + key_part
                lanes = slice(half * HEAD_DIM, (half + 1) * HEAD_DIM)
                dqt_ref[lanes, cols] = forward_product(keys_t[lanes], d_scores)
            for part, value in enumerate((dqt_ref[...].T * scale, d_keys, d_values)):
                at = pl.multiple_of(part * width + pair * LANES, LANES)
                rounded = value.astype(jnp.bfloat16)
                d_qkv_ref[side, here, pl.ds(at, LANES)] = rounded
                d_out_ref[side, :, pl.ds(at, LANES)] = rounded
                if part != 1:
                    column = jnp.sum(rounded.astype(jnp.float32), axis=0, keepdims=True)
                    column = jnp.broadcast_to(column, (8, LANES))
                    known = sums_ref[side, :, pl.ds(at, LANES)]
                    sums_ref[side, :, pl.ds(at, LANES)] = jnp.where(
                        first_seq, column, column + known
                    )
            return carry

        lax.fori_loop(0, pairs, one_pair, 0, unroll=True)

    @pl.when(seq == pl.num_programs(0) - 1)
    def _():
        core = core_ref[0]
        for load in loads:
            load.wait()
        d_branch_ref = held_ref.at[2]
        for out_ref, side in ((far_ref, 1 - core), (own_ref, core)):
            out_ref[:, : 3 * width] = weight_grad(held_ref[0], d_qkv_ref[side]).astype(
                jnp.bfloat16
            )
            cols = pl.ds(pl.multiple_of(side * width, LANES), width)
            out_ref[:, 3 * width : 4 * width] = weight_grad(
                held_ref[1], d_branch_ref[:, cols]
            ).astype(jnp.bfloat16)
            if small_ref is not None:
                tile = small_ref[side]
                number = lax.broadcasted_iota(jnp.int32, tile.shape, 0)
                for row, start in ((0, 0), (1, 2 * width)):
                    line = jnp.concatenate(
                        [sums_ref[one, :1, start : start + width] for one in range(2)], axis=1
                    )
                    tile = jnp.where((number == row) & (side == 0), line, tile)
                out_ref[:, 4 * width :] = tile.T.astype(jnp.bfloat16)


def attend_core_back(
    core, qkv, d_mixed, lse, x_low, mixed_heads, d_branch, seq_lengths, small=None
):
    qkv_lo, qkv_hi = qkv
    total, wide = qkv_lo.shape
    seqs = seq_lengths.shape[0]
    rows, width = total // seqs, 2 * wide // 3
    extra = 0 if small is None else small.shape[1]
    once = pl.Buffered(1)
    side = pl.BlockSpec((rows, wide), lambda seq, *_: (seq, 0))
    whole = pl.BlockSpec(memory_space=pl.ANY)
    specs = [
        side,
        side,
        pl.BlockSpec((rows, width), lambda seq, *_: (seq, 0)),
        pl.BlockSpec((None, lse.shape[1], rows), lambda seq, *_: (seq, 0, 0)),
        whole,
        whole,
        whole,
    ]
    given = [qkv_lo, qkv_hi, d_mixed, lse, x_low, mixed_heads, d_branch]
    if small is not None:
        specs.append(pl.BlockSpec(small.shape, lambda seq, *_: (0, 0, 0), pipeline_mode=once))
        given.append(small)
    grad_shape = (width, 2 * width + extra)
    grad_spec = pl.BlockSpec(grad_shape, lambda seq, *_: (0, 0), pipeline_mode=once)
    return pl.pallas_call(
        functools.partial(attend_back_kernel, extra),
        out_shape=(
            jax.ShapeDtypeStruct((2, total, wide), jnp.bfloat16),
            jax.ShapeDtypeStruct((2, 8, wide), jnp.float32),
            jax.ShapeDtypeStruct(grad_shape, jnp.bfloat16),
            jax.ShapeDtypeStruct(grad_shape, jnp.bfloat16),
        ),
        grid_spec=pltpu.PrefetchScalarGridSpec(
            num_scalar_prefetch=2,
            grid=(seqs,),
            in_specs=specs,
            out_specs=[
                pl.BlockSpec((2, rows, wide), lambda seq, *_: (0, seq, 0)),
                pl.BlockSpec((2, 8, wide), lambda seq, *_: (0, 0, 0)),
                grad_spec,
                grad_spec,
            ],
            scratch_shapes=[
                pltpu.VMEM((LANES, rows), jnp.float32),
                pltpu.VMEM((2, total, wide), jnp.bfloat16),
                pltpu.VMEM((3, total, width), jnp.bfloat16),
                pltpu.SemaphoreType.DMA((3,)),
            ],
        ),
        compiler_params=pltpu.CompilerParams(vmem_limit_bytes=60 << 20),
        cost_estimate=LIGHT,
        name="attend_back",
    )(seq_lengths, core.reshape(1).astype(jnp.int32), *given)


def half_of(rows, side):
    width = rows.shape[1] // 2
    return lax.dynamic_slice_in_dim(rows, side * width, width, 1)


def project_in(flat_low, in_layer, small_layer):
    third = flat_low.shape[1] // 2
    qkv = []
    for side in range(2):
        cols = slice(side * third, (side + 1) * third)
        bias = jnp.concatenate(
            [small_layer[0, cols], jnp.zeros((third,), jnp.float32), small_layer[1, cols]]
        )
        part = forward_product(flat_low, in_layer[side]) + bias
        qkv.append(part.astype(jnp.bfloat16))
    return qkv


def project_in_back(d_resid, d_qkv, in_layer):
    return d_resid + sum(back_product(d_qkv[side], in_layer[side]) for side in range(2))


def small_tile_kernel(*refs):
    out_ref = refs[-1]
    width = out_ref.shape[2]
    out_ref[...] = jnp.zeros_like(out_ref)
    third = width // 2

    def put(layer, row, ref, parts):
        for part in range(parts):
            cols = slice(part * width, (part + 1) * width)
            out_ref[layer, row + part : row + part + 1, :] = ref[:1, cols]

    for layer in range(2):
        out_sums, pre_sums, feed_sums = refs[3 * layer : 3 * layer + 3]
        put(layer, 2, out_sums, 3)
        put(layer, 5, pre_sums, 4)
        put(layer, 9, feed_sums, 3)
    attn_sums = refs[6]
    for row, start in ((0, 0), (1, 2 * third)):
        for side in range(2):
            out_ref[1, row : row + 1, side * third : (side + 1) * third] = attn_sums[
                side, :1, start : start + third
            ]


def small_tile(one, two, attn_sums, width):
    return pl.pallas_call(
        small_tile_kernel,
        out_shape=jax.ShapeDtypeStruct((2, LANES, width), jnp.float32),
        cost_estimate=LIGHT,
        name="small_tile",
    )(*one, *two, attn_sums)


def project_norm_kernel(rows_ref, weight_ref, resid_ref, bias_ref, gain_ref, shift_ref, *outs):
    normed_ref, low_ref, xhat_ref, inv_ref = outs
    branch = forward_product(rows_ref[...], weight_ref[...]) + bias_ref[...]
    normed, normal_part, inv_std = norm_forward(
        resid_ref[...].astype(jnp.float32) + branch, gain_ref[...], shift_ref[...]
    )
    normed_ref[...] = normed
    low_ref[...] = normed.astype(jnp.bfloat16)
    xhat_ref[...] = normal_part
    inv_ref[...] = jnp.broadcast_to(inv_std, inv_ref.shape)


def project_norm(rows_low, weight, resid, small_layer, first):
    total, depth = rows_low.shape
    width = resid.shape[1]
    block = math.gcd(total, 256)
    row = pl.BlockSpec((block, width), lambda at: (at, 0))
    line = pl.BlockSpec((1, width), lambda at: (0, 0))
    return pl.pallas_call(
        project_norm_kernel,
        out_shape=(
            jax.ShapeDtypeStruct((total, width), jnp.float32),
            jax.ShapeDtypeStruct((total, width), jnp.bfloat16),
            jax.ShapeDtypeStruct((total, width), jnp.float32),
            jax.ShapeDtypeStruct((total, LANES), jnp.float32),
        ),
        grid=(total // block,),
        in_specs=[
            pl.BlockSpec((block, depth), lambda at: (at, 0)),
            pl.BlockSpec((depth, width), lambda at: (0, 0), pipeline_mode=pl.Buffered(1)),
            row,
            line,
            line,
            line,
        ],
        out_specs=[row, row, row, pl.BlockSpec((block, LANES), lambda at: (at, 0))],
        compiler_params=pltpu.CompilerParams(vmem_limit_bytes=24 << 20),
        cost_estimate=LIGHT,
        name="project_norm",
    )(rows_low, weight, resid, *[small_layer[at : at + 1] for at in range(first, first + 3)])


def served_back_kernel(
    select_ref, d_served_ref, cot_ref, xhat_ref, inv_ref, gain_ref, out_ref, *outs
):
    out_resid_ref, d_branch_ref, d_mixed_ref, sums_ref = outs
    width = cot_ref.shape[1]
    select = select_ref[...]
    both = weight_grad(select, d_served_ref[...])
    hit = weight_grad(select, jnp.ones((select.shape[0], LANES), jnp.bfloat16))[:, :1] > 0.5
    d_out = jnp.where(hit, both[:, :width] + both[:, width:], cot_ref[...].astype(jnp.float32))
    xhat = xhat_ref[...]
    d_resid, d_branch = norm_back_rows(d_out, xhat, inv_ref[:, :1], gain_ref[...])
    out_resid_ref[...] = d_resid
    d_branch_ref[...] = d_branch
    d_mixed_ref[...] = back_product(d_branch, out_ref[...]).astype(jnp.bfloat16)
    add_sums(sums_ref, (d_branch.astype(jnp.float32), d_out * xhat, d_out))


def served_back(select_rows, d_served, cot_flat, xhat, inv, small_layer, out_layer):
    total, width = cot_flat.shape
    slots = select_rows.shape[0]
    block = math.gcd(total, 256)
    row = pl.BlockSpec((block, width), lambda at: (at, 0))
    d_resid, d_branch, d_mixed, sums = pl.pallas_call(
        served_back_kernel,
        out_shape=(
            jax.ShapeDtypeStruct((total, width), jnp.float32),
            jax.ShapeDtypeStruct((total, width), jnp.bfloat16),
            jax.ShapeDtypeStruct((total, width), jnp.bfloat16),
            jax.ShapeDtypeStruct((8, 3 * width), jnp.float32),
        ),
        grid=(total // block,),
        in_specs=[
            pl.BlockSpec((slots, block), lambda at: (0, at)),
            pl.BlockSpec((slots, 2 * width), lambda at: (0, 0)),
            row,
            row,
            pl.BlockSpec((block, LANES), lambda at: (at, 0)),
            pl.BlockSpec((1, width), lambda at: (0, 0)),
            pl.BlockSpec((width, width), lambda at: (0, 0)),
        ],
        out_specs=[row, row, row, pl.BlockSpec((8, 3 * width), lambda at: (0, 0))],
        compiler_params=pltpu.CompilerParams(vmem_limit_bytes=24 << 20),
        cost_estimate=LIGHT,
        name="served_back",
    )(select_rows, d_served, cot_flat, xhat, inv, small_layer[3:4], out_layer)
    return (d_resid, d_branch, d_mixed, sums)


def feed_up_kernel(rows_ref, up_ref, bias_ref, act_ref, slope_ref):
    low_rows = rows_ref[...]
    for at in range(0, up_ref.shape[1], HIDDEN_BLOCK):
        cols = slice(at, at + HIDDEN_BLOCK)
        pre_act = forward_product(low_rows, up_ref[:, cols]) + bias_ref[:, cols]
        below = 0.5 * (1.0 + lax.erf(pre_act * 0.7071067811865476))
        density = jnp.exp(-0.5 * pre_act * pre_act) * 0.3989422804014327
        act_ref[:, cols] = (pre_act * below).astype(jnp.bfloat16)
        slope_ref[:, cols] = (below + pre_act * density).astype(jnp.bfloat16)


def feed_up(rows_low, up_layer, small_layer):
    total, width = rows_low.shape
    hidden = up_layer.shape[1]
    block = math.gcd(total, 256)
    bias = small_layer[5:9].reshape(1, hidden)
    shape = jax.ShapeDtypeStruct((total, hidden), jnp.bfloat16)
    act_low, slope = pl.pallas_call(
        feed_up_kernel,
        out_shape=(shape, shape),
        grid=(total // block,),
        in_specs=[
            pl.BlockSpec((block, width), lambda at: (at, 0)),
            pl.BlockSpec((width, hidden), lambda at: (0, 0)),
            pl.BlockSpec((1, hidden), lambda at: (0, 0)),
        ],
        out_specs=[pl.BlockSpec((block, hidden), lambda at: (at, 0))] * 2,
        compiler_params=pltpu.CompilerParams(vmem_limit_bytes=32 << 20),
        cost_estimate=LIGHT,
        name="feed_up",
    )(rows_low, up_layer, bias)
    return (act_low, slope)


def feed_down(rows_in, act_low, down_layer, small_layer):
    branch = forward_product(act_low, down_layer) + small_layer[9]
    return norm_forward(rows_in + branch, small_layer[10], small_layer[11])


def feed_down_back(d_normed, normal_part, inv_std, slope, down_layer, small_layer):
    d_resid, d_gain, d_shift = norm_backward(d_normed, normal_part, inv_std, small_layer[10])
    d_branch = d_resid.astype(jnp.bfloat16)
    d_pre = (back_product(d_branch, down_layer) * slope.astype(jnp.float32)).astype(jnp.bfloat16)
    d_bias = jnp.sum(d_pre.astype(jnp.float32), axis=0, keepdims=True)
    d_shared = jnp.sum(d_branch.astype(jnp.float32), axis=0, keepdims=True)
    small_rows = (d_bias, jnp.concatenate([d_shared, d_gain, d_shift], axis=1))
    return (d_resid, d_branch, d_pre, small_rows)


def norm_back_rows(d_out, xhat, inv, gain):
    d_normal = d_out * gain
    d_resid = inv * (
        d_normal
        - jnp.mean(d_normal, axis=-1, keepdims=True)
        - xhat * jnp.mean(d_normal * xhat, axis=-1, keepdims=True)
    )
    return (d_resid, d_resid.astype(jnp.bfloat16))


def add_sums(sums_ref, values):
    width = values[0].shape[1]
    first = pl.program_id(0) == 0
    for number, value in enumerate(values):
        cols = slice(number * width, (number + 1) * width)
        part = jnp.broadcast_to(jnp.sum(value, axis=0, keepdims=True), (8, width))
        sums_ref[:, cols] = jnp.where(first, part, part + sums_ref[:, cols])


def layer_back_kernel(
    d_resid_ref, d_qkv_ref, in_ref, xhat_ref, inv_ref, gain_ref, down_ref, slope_ref, *outs
):
    out_resid_ref, d_branch_ref, d_pre_ref, pre_sums_ref, sums_ref = outs
    d_out = d_resid_ref[...]
    for side in range(2):
        d_out = d_out + back_product(d_qkv_ref[side], in_ref[side])
    xhat = xhat_ref[...]
    d_resid, d_branch = norm_back_rows(d_out, xhat, inv_ref[:, :1], gain_ref[...])
    out_resid_ref[...] = d_resid
    d_branch_ref[...] = d_branch
    add_sums(sums_ref, (d_branch.astype(jnp.float32), d_out * xhat, d_out))
    first = pl.program_id(0) == 0
    for at in range(0, down_ref.shape[0], HIDDEN_BLOCK):
        cols = slice(at, at + HIDDEN_BLOCK)
        d_act = back_product(d_branch, down_ref[cols])
        d_pre = (d_act * slope_ref[:, cols].astype(jnp.float32)).astype(jnp.bfloat16)
        d_pre_ref[:, cols] = d_pre
        part = jnp.broadcast_to(
            jnp.sum(d_pre.astype(jnp.float32), axis=0, keepdims=True), (8, HIDDEN_BLOCK)
        )
        pre_sums_ref[:, cols] = jnp.where(first, part, part + pre_sums_ref[:, cols])


def layer_back(d_resid, d_qkv, in_layer, xhat, inv, small_layer, down_layer, slope):
    total, width = d_resid.shape
    hidden = slope.shape[1]
    wide = d_qkv.shape[2]
    block = math.gcd(total, 256)
    row = pl.BlockSpec((block, width), lambda at: (at, 0))
    hidden_row = pl.BlockSpec((block, hidden), lambda at: (at, 0))
    d_resid, d_branch, d_pre, pre_sums, sums = pl.pallas_call(
        layer_back_kernel,
        out_shape=(
            jax.ShapeDtypeStruct((total, width), jnp.float32),
            jax.ShapeDtypeStruct((total, width), jnp.bfloat16),
            jax.ShapeDtypeStruct((total, hidden), jnp.bfloat16),
            jax.ShapeDtypeStruct((8, hidden), jnp.float32),
            jax.ShapeDtypeStruct((8, 3 * width), jnp.float32),
        ),
        grid=(total // block,),
        in_specs=[
            row,
            pl.BlockSpec((2, block, wide), lambda at: (0, at, 0)),
            pl.BlockSpec((2, width, wide), lambda at: (0, 0, 0), pipeline_mode=pl.Buffered(1)),
            row,
            pl.BlockSpec((block, LANES), lambda at: (at, 0)),
            pl.BlockSpec((1, width), lambda at: (0, 0)),
            pl.BlockSpec((hidden, width), lambda at: (0, 0), pipeline_mode=pl.Buffered(1)),
            hidden_row,
        ],
        out_specs=[
            row,
            row,
            hidden_row,
            pl.BlockSpec((8, hidden), lambda at: (0, 0)),
            pl.BlockSpec((8, 3 * width), lambda at: (0, 0)),
        ],
        compiler_params=pltpu.CompilerParams(vmem_limit_bytes=46 << 20),
        cost_estimate=LIGHT,
        name="layer_back",
    )(d_resid, d_qkv, in_layer, xhat, inv, small_layer[10:11], down_layer, slope)
    return (d_resid, d_branch, d_pre, (pre_sums, sums))


def feed_back_kernel(d_resid_ref, d_pre_ref, up_ref, xhat_ref, inv_ref, gain_ref, out_ref, *outs):
    out_resid_ref, d_branch_ref, d_mixed_ref, sums_ref = outs
    d_out = d_resid_ref[...] + back_product(d_pre_ref[...], up_ref[...])
    xhat = xhat_ref[...]
    d_resid, d_branch = norm_back_rows(d_out, xhat, inv_ref[:, :1], gain_ref[...])
    out_resid_ref[...] = d_resid
    d_branch_ref[...] = d_branch
    d_mixed_ref[...] = back_product(d_branch, out_ref[...]).astype(jnp.bfloat16)
    add_sums(sums_ref, (d_branch.astype(jnp.float32), d_out * xhat, d_out))


def feed_back(d_resid, d_pre, up_layer, xhat, inv, small_layer, out_layer):
    total, width = d_resid.shape
    hidden = d_pre.shape[1]
    block = math.gcd(total, 256)
    row = pl.BlockSpec((block, width), lambda at: (at, 0))
    d_resid, d_branch, d_mixed, sums = pl.pallas_call(
        feed_back_kernel,
        out_shape=(
            jax.ShapeDtypeStruct((total, width), jnp.float32),
            jax.ShapeDtypeStruct((total, width), jnp.bfloat16),
            jax.ShapeDtypeStruct((total, width), jnp.bfloat16),
            jax.ShapeDtypeStruct((8, 3 * width), jnp.float32),
        ),
        grid=(total // block,),
        in_specs=[
            row,
            pl.BlockSpec((block, hidden), lambda at: (at, 0)),
            pl.BlockSpec((width, hidden), lambda at: (0, 0), pipeline_mode=pl.Buffered(1)),
            row,
            pl.BlockSpec((block, LANES), lambda at: (at, 0)),
            pl.BlockSpec((1, width), lambda at: (0, 0)),
            pl.BlockSpec((width, width), lambda at: (0, 0), pipeline_mode=pl.Buffered(1)),
        ],
        out_specs=[row, row, row, pl.BlockSpec((8, 3 * width), lambda at: (0, 0))],
        compiler_params=pltpu.CompilerParams(vmem_limit_bytes=40 << 20),
        cost_estimate=LIGHT,
        name="feed_back",
    )(d_resid, d_pre, up_layer, xhat, inv, small_layer[3:4], out_layer)
    return (d_resid, d_branch, d_mixed, sums)


def order_attn_kernel(core_ref, *refs):
    pairs, out_ref = (refs[:2], refs[2:4]), refs[4]
    third = out_ref.shape[3] // 2
    core = core_ref[0]
    for layer, (own_ref, far_ref) in enumerate(pairs):
        for part in range(4):
            cols = slice(part * third, (part + 1) * third)
            own, far = own_ref[:, cols], far_ref[:, cols]
            for side in range(2):
                out_ref[layer, part, :, side * third : (side + 1) * third] = jnp.where(
                    core == side, own, far
                )


def order_attn(core, one, two, width):
    local = pl.BlockSpec(memory_space=pltpu.VMEM)
    shard = one[0].shape[0]
    return pl.pallas_call(
        order_attn_kernel,
        out_shape=jax.ShapeDtypeStruct((2, 4, shard, width), jnp.bfloat16),
        grid_spec=pltpu.PrefetchScalarGridSpec(
            num_scalar_prefetch=1, grid=(), in_specs=[local] * 4, out_specs=local
        ),
        cost_estimate=LIGHT,
        name="order_attn",
    )(core.reshape(1).astype(jnp.int32), *one, *two)


def feed_grads_kernel(shard, core, low_ref, d_pre_ref, act_ref, d_branch_ref, *rest):
    far_ref, own_ref, low_t_ref, down_ref = rest
    at = pl.program_id(0)
    width = low_ref.shape[1]
    third = width // 2

    @pl.when(at == 0)
    def _():
        low_t_ref[...] = low_ref[...].T

    for step in range(4):

        @pl.when(at == step)
        def _(step=step):
            out_ref = far_ref if step < 2 else own_ref
            cols = slice((step % 2) * width, (step % 2 + 1) * width)
            out_ref[:, cols] = forward_product(low_t_ref[...], d_pre_ref[...]).astype(jnp.bfloat16)

    @pl.when(at >= 4)
    def _():
        down_ref[...] = weight_grad(act_ref[...], d_branch_ref[...])
        blocks = width // (4 * shard)
        for out_ref, side in ((far_ref, 1 - core[0]), (own_ref, core[0])):
            from_cols = pl.ds(pl.multiple_of(side * third, LANES), third)
            for block in range(blocks):
                row = pl.multiple_of(((at - 4) * blocks + block) * shard, 16)
                for part in range(4):
                    start = (block * 4 + part) * shard
                    cols = slice(2 * width + part * third, 2 * width + (part + 1) * third)
                    out_ref[pl.ds(row, shard), cols] = down_ref[
                        start : start + shard, from_cols
                    ].astype(jnp.bfloat16)


def feed_grads_plain(core, rows_low, d_pre, act_low, d_branch, shard):
    sides = []
    width = rows_low.shape[1]
    for side in (1 - core, core):
        d_up = weight_grad(rows_low, half_of(d_pre, side))
        d_down = weight_grad(act_low, half_of(d_branch, side))
        d_down = d_down.reshape(-1, 4, shard, width // 2).transpose(0, 2, 1, 3)
        sides.append(jnp.concatenate([d_up, d_down.reshape(width, -1)], axis=1))
    return [part.astype(jnp.bfloat16) for part in sides]


def feed_grads(core, rows_low, d_pre, act_low, d_branch, shard):
    total, width = rows_low.shape
    hidden = act_low.shape[1]
    if shard % 16 or hidden != 4 * width:
        return feed_grads_plain(core, rows_low, d_pre, act_low, d_branch, shard)

    def pre_at(at, core):
        step = jnp.minimum(at, 3)
        return (0, jnp.where(step < 2, 1 - core[0], core[0]) * 2 + step % 2)

    shape = jax.ShapeDtypeStruct((width, hidden), jnp.bfloat16)
    return pl.pallas_call(
        functools.partial(feed_grads_kernel, shard),
        out_shape=(shape, shape),
        grid_spec=pltpu.PrefetchScalarGridSpec(
            num_scalar_prefetch=1,
            grid=(8,),
            in_specs=[
                pl.BlockSpec((total, width), lambda at, core: (0, 0)),
                pl.BlockSpec((total, width), pre_at),
                pl.BlockSpec((total, width), lambda at, core: (0, jnp.maximum(at - 4, 0))),
                pl.BlockSpec((total, width), lambda at, core: (0, 0)),
            ],
            out_specs=[pl.BlockSpec((width, hidden), lambda at, core: (0, 0))] * 2,
            scratch_shapes=[
                pltpu.VMEM((width, total), jnp.bfloat16),
                pltpu.VMEM((width, width), jnp.float32),
            ],
        ),
        compiler_params=pltpu.CompilerParams(vmem_limit_bytes=40 << 20),
        cost_estimate=LIGHT,
        name="feed_grads",
    )(core.reshape(1).astype(jnp.int32), rows_low, d_pre, act_low, d_branch)


def row_select(token_mask, capacity):
    flat_mask = token_mask.reshape(1, -1)
    row_total = flat_mask.shape[1]
    before = (
        lax.broadcasted_iota(jnp.int32, (row_total, row_total), 0)
        < lax.broadcasted_iota(jnp.int32, (row_total, row_total), 1)
    ).astype(jnp.bfloat16)
    rank = forward_product(flat_mask.astype(jnp.bfloat16), before).astype(jnp.int32)
    slots = lax.broadcasted_iota(jnp.int32, (capacity, row_total), 0)
    return ((slots == rank) & (flat_mask == 1)).astype(jnp.bfloat16)


def split_low(wide, parts):
    pieces = []
    left = wide
    for _ in range(parts - 1):
        piece = lax.reduce_precision(left, 8, 7)
        pieces.append(piece.astype(jnp.bfloat16))
        left = left - piece
    pieces.append(left.astype(jnp.bfloat16))
    return jnp.concatenate(pieces, axis=1)


def join_low(joined, parts):
    width = joined.shape[1] // parts
    total = joined[:, :width]
    for number in range(1, parts):
        total = total + joined[:, number * width : (number + 1) * width]
    return total


def adam_update(
    master, first_moment, second_moment, gradient, clip_scale, step_value, decay_rate, rate_value
):
    clipped = gradient.astype(jnp.float32) * clip_scale
    first_new = BETA_FIRST * first_moment + (1.0 - BETA_FIRST) * clipped
    second_new = BETA_SECOND * second_moment + (1.0 - BETA_SECOND) * clipped * clipped
    first_hat = first_new / (1.0 - jnp.power(BETA_FIRST, step_value))
    second_hat = second_new / (1.0 - jnp.power(BETA_SECOND, step_value))
    master_new = master - rate_value * (
        first_hat / (jnp.sqrt(second_hat) + ADAM_EPS) + decay_rate * master
    )
    return (master_new, first_new, second_new, master_new.astype(jnp.bfloat16))


def routes(peers):
    bits = peers.bit_length() - 1
    deep = min(2, bits)
    rest = bits - deep
    x_bits = [1 << at for at in range(rest - rest // 2)]
    y_bits = [1 << at for at in range(rest - rest // 2, rest)]
    z_bits = [1 << at for at in range(rest, bits)]
    if len(x_bits) == len(y_bits):
        return ((z_bits, y_bits, x_bits), (z_bits, x_bits, y_bits))
    return ((z_bits, y_bits, x_bits), (z_bits, y_bits, x_bits))


def stage_sizes(peers):
    return [1 << len(bits) for bits in routes(peers)[0]]


def mask_of(bits, turn):
    return sum(bit for at, bit in enumerate(bits) if turn >> at & 1)


def shift(value, stage, turn, peers):
    pairs = []
    for core, path in enumerate(routes(peers)):
        mask = mask_of(path[stage], turn)
        pairs += [(core * peers + at, core * peers + (at ^ mask)) for at in range(peers)]
    return lax.ppermute(value, ("dp", "bal"), pairs)


def swap(value):
    return lax.ppermute(value, "dp", [(0, 1), (1, 0)])


def place_table(peers, core):
    masks = [
        [mask_of(sum(path, []), spot) for spot in range(peers)] for path in routes(peers)
    ]
    masks = jnp.asarray(np.array(masks, np.int32))
    mine = lax.axis_index("bal")
    own = jnp.where(core == 0, masks[0], masks[1])
    far = jnp.where(core == 0, masks[1], masks[0])
    return jnp.concatenate([mine ^ own, mine ^ far, core.reshape(1).astype(jnp.int32)])


def place_kernel(plan, count, spots, *refs):
    parts, outs = refs[:count], refs[count:]
    held, rows, _ = parts[0].shape
    core = spots[count * held]

    for number, part in enumerate(parts):
        side = core if number < count // 2 else 1 - core

        def one_block(at, carry, number=number, part=part, side=side):
            spot = spots[number * held + at]
            for (start, width, kind), out in zip(plan, outs):
                cols = pl.ds(pl.multiple_of(side * width, LANES), width)
                if kind == "stack":
                    out[side, spot] = part[at, :, start : start + width]
                elif kind == "wide":
                    out[spot, :, cols] = part[at, :, start : start + width]
                else:
                    for piece in range(4):
                        begin = start + piece * width
                        out[spot, piece * rows : (piece + 1) * rows, cols] = part[
                            at, :, begin : begin + width
                        ]
            return carry

        lax.fori_loop(0, held, one_block, 0)


def place(spots, parts, plan):
    held, rows, whole = parts[0].shape
    peers = len(parts) * held // 2
    kinds = [
        (start, 4 * width, "stack") if kind == "down" and rows % 16 else (start, width, kind)
        for start, width, kind in plan
    ]
    shapes = {
        "stack": lambda width: (2, peers, rows, width),
        "wide": lambda width: (peers, rows, 2 * width),
        "down": lambda width: (peers, 4 * rows, 2 * width),
    }
    local = pl.BlockSpec(memory_space=pltpu.VMEM)
    placed = pl.pallas_call(
        functools.partial(place_kernel, kinds, len(parts)),
        out_shape=[
            jax.ShapeDtypeStruct(shapes[kind](width), parts[0].dtype) for _, width, kind in kinds
        ],
        grid_spec=pltpu.PrefetchScalarGridSpec(
            num_scalar_prefetch=1,
            grid=(),
            in_specs=[local] * len(parts),
            out_specs=[local] * len(kinds),
        ),
        compiler_params=pltpu.CompilerParams(vmem_limit_bytes=40 << 20),
        cost_estimate=LIGHT,
        name="place",
    )(spots, *parts)
    results = []
    for part, (_, width, kind), (_, _, asked) in zip(placed, kinds, plan):
        if kind != asked:
            part = part.reshape(2, peers, rows, 4, width // 4).transpose(1, 3, 2, 0, 4)
            results.append(part.reshape(peers * rows * 4, width // 2))
        elif kind == "stack":
            results.append(part.reshape(2, peers * rows, width))
        else:
            results.append(part.reshape(-1, 2 * width))
    return results


class Gather:
    def __init__(self, mine, spots, peers, plan):
        self.kept, self.moved = [mine[None]], []
        self.spots, self.peers, self.plan = spots, peers, plan
        self.sizes = stage_sizes(peers)
        self.stage, self.turn = 0, 1

    def done(self):
        return self.stage > len(self.sizes)

    def launch(self, count):
        if self.stage == len(self.sizes):
            return [swap(part) for part in self.kept]
        stop = self.sizes[self.stage]
        stop = stop if count is None else min(stop, self.turn + count)
        turns = range(self.turn, stop)
        self.turn = stop
        return [shift(self.kept[0], self.stage, turn, self.peers) for turn in turns]

    def land(self, moved):
        self.moved += moved
        if self.stage < len(self.sizes) and len(self.moved) < self.sizes[self.stage] - 1:
            return
        whole = self.kept + self.moved
        if self.stage < len(self.sizes) - 1:
            whole = [jnp.concatenate(whole, axis=0)]
        self.kept, self.moved = whole, []
        self.stage, self.turn = self.stage + 1, 1

    def result(self):
        return place(self.spots, self.kept, self.plan)


class Scatter:
    def __init__(self, far, own, spots, peers):
        self.kept = [grads.reshape(peers, -1, grads.shape[1]) for grads in (own, far)]
        self.moved = []
        self.spots, self.peers = spots, peers
        self.sizes = stage_sizes(peers)
        self.stage, self.turn = len(self.sizes), 1

    def done(self):
        return self.stage < 0

    def launch(self, count):
        if self.stage == len(self.sizes):
            return [swap(self.kept[1])]
        stop = self.sizes[self.stage]
        stop = stop if count is None else min(stop, self.turn + count)
        turns = range(self.turn, stop)
        self.turn = stop
        return [shift(self.kept[turn], self.stage, turn, self.peers) for turn in turns]

    def land(self, moved):
        self.moved += moved
        if self.stage == len(self.sizes):
            self.kept = list(fold(self.spots, self.kept[0], self.moved[0], self.sizes[-1]))
        else:
            if len(self.moved) < self.sizes[self.stage] - 1:
                return
            pieces = self.sizes[self.stage - 1] if self.stage else 1
            size = self.kept[0].shape[0] // pieces

            def total(at):
                rows = slice(at * size, (at + 1) * size)
                adds = [part[rows].astype(jnp.float32) for part in [self.kept[0]] + self.moved]
                return sum(adds[1:], adds[0]).astype(jnp.bfloat16)

            self.kept = [total(at) for at in range(pieces)]
        self.moved = []
        self.stage, self.turn = self.stage - 1, 1

    def result(self):
        return self.kept[0][0]


class Lanes:
    def __init__(self):
        self.flying = {}

    def launch(self, *moves):
        for move in moves:
            move, count = move if isinstance(move, tuple) else (move, None)
            if not move.done():
                self.flying[move] = self.flying.get(move, []) + move.launch(count)

    def meet(self, work, *landing, ready=()):
        moves = [move for move in landing if move in self.flying]
        flown = [self.flying.pop(move) for move in moves]
        waiting = [move.kept for move in ready]
        work, flown, waiting = lax.optimization_barrier((work, flown, waiting))
        for move, moved in zip(moves, flown):
            move.land(moved)
        for move, kept in zip(ready, waiting):
            move.kept = kept
        return work

    def settle(self, work, *moves):
        return self.meet(work, ready=moves)

    def finish(self, work, *moves):
        work = self.meet(work, *moves)
        while not all(move.done() for move in moves):
            self.launch(*moves)
            work = self.meet(work, *moves)
        return work


def fold_kernel(spots, own, far, *outs):
    held = outs[0].shape[0]

    def one_block(at, carry):
        for number, out in enumerate(outs):
            spot = spots[number * held + at]
            out[at] = (own[spot].astype(jnp.float32) + far[spot].astype(jnp.float32)).astype(
                out.dtype
            )
        return carry

    lax.fori_loop(0, held, one_block, 0)


def fold(spots, own, far, pieces):
    peers, rows, width = own.shape
    shape = jax.ShapeDtypeStruct((peers // pieces, rows, width), own.dtype)
    local = pl.BlockSpec(memory_space=pltpu.VMEM)
    return pl.pallas_call(
        fold_kernel,
        out_shape=[shape] * pieces,
        grid_spec=pltpu.PrefetchScalarGridSpec(
            num_scalar_prefetch=1,
            grid=(),
            in_specs=[local, local],
            out_specs=[local] * pieces,
        ),
        compiler_params=pltpu.CompilerParams(vmem_limit_bytes=32 << 20),
        cost_estimate=LIGHT,
        name="fold",
    )(spots, own, far)


def both_sides(own, other, core):
    return (jnp.where(core == 0, own, other), jnp.where(core == 0, other, own))


def per_device(
    tokens,
    cotangent,
    seq_lengths,
    token_mask,
    step_count,
    attn_master,
    attn_first,
    attn_second,
    up_master,
    up_first,
    up_second,
    down_master,
    down_first,
    down_second,
    small_master,
    small_first,
    small_second,
):
    core = lax.axis_index("dp")
    peers = lax.axis_size("bal")
    seq_count, length, model_width = tokens.shape
    rows_total = seq_count * length
    spots = place_table(peers, core)
    shard = attn_master.shape[2]
    attn_half = lax.dynamic_slice_in_dim(attn_master, core * (model_width // 2), model_width // 2, 3)
    attn_half = attn_half.astype(jnp.bfloat16).transpose(0, 2, 1, 3).reshape(2, shard, -1)
    small_half = lax.dynamic_slice_in_dim(small_master.reshape(24, shard), core * 12, 12, 0)
    small_half = jnp.pad(small_half.astype(jnp.bfloat16).T, ((0, 0), (0, LANES - 12)))
    wide = attn_half.shape[2]
    lanes = Lanes()
    third = model_width // 2
    hidden_half = up_master.shape[2] // 2

    def down_half(layer):
        half = half_of(down_master[layer], core).astype(jnp.bfloat16)
        return [half[part * shard : (part + 1) * shard] for part in range(4)]

    up_half = [half_of(up_master[layer], core).astype(jnp.bfloat16) for layer in range(2)]
    in_one = Gather(
        jnp.concatenate([attn_half[0, :, : 3 * third], small_half], axis=1),
        spots,
        peers,
        [(0, 3 * third, "stack"), (3 * third, LANES, "stack")],
    )
    out_up_one = Gather(
        jnp.concatenate([attn_half[0, :, 3 * third :], up_half[0]], axis=1),
        spots,
        peers,
        [(0, third, "wide"), (third, hidden_half, "wide")],
    )
    down_one = Gather(
        jnp.concatenate(down_half(0), axis=1), spots, peers, [(0, third, "down")]
    )
    attn_two = Gather(
        attn_half[1], spots, peers, [(0, 3 * third, "stack"), (3 * third, third, "wide")]
    )
    up_two = Gather(up_half[1], spots, peers, [(0, hidden_half, "wide")])
    down_two = Gather(
        jnp.concatenate(down_half(1), axis=1), spots, peers, [(0, third, "down")]
    )
    flat_low = tokens.reshape(rows_total, model_width)
    cot_flat = cotangent.reshape(rows_total, model_width)
    select_rows = row_select(token_mask, MCAP)
    flat_mask = token_mask.reshape(-1, 1) == 1

    lanes.launch(in_one)
    lanes.meet((), in_one, ready=(out_up_one,))
    lanes.launch(in_one, (out_up_one, 2))
    lanes.meet((), in_one, out_up_one)
    lanes.launch(in_one, out_up_one)
    lanes.meet((), in_one, out_up_one, ready=(down_one,))
    lanes.launch(in_one, out_up_one, (down_one, 2))
    lanes.finish((), in_one)
    w_in_one, small_rows = in_one.result()
    small_vals = small_rows[:, :, :12].transpose(0, 2, 1).astype(jnp.float32)
    qkv_one = project_in(flat_low, w_in_one, small_vals[0])
    qkv_one = lanes.meet(qkv_one, out_up_one, down_one, ready=(attn_two,))
    lanes.launch(out_up_one, down_one, (attn_two, 2))
    attended = attend_core(qkv_one[0], qkv_one[1], seq_lengths)
    attended = lanes.meet(attended, out_up_one, down_one, attn_two, ready=(up_two,))
    lanes.launch(out_up_one, down_one, attn_two)
    mixed_one, lse_one = lanes.finish(attended, out_up_one)
    w_out_one, w_up_one = out_up_one.result()
    attended_one = project_norm(mixed_one, w_out_one, flat_low, small_vals[0], 2)
    attended_one = lanes.meet(attended_one, down_one, attn_two, ready=(down_two,))
    attended_one, low_one, attn_xhat_one, attn_inv_one = attended_one
    lanes.launch(down_one, attn_two, (up_two, 2))
    act_one = feed_up(low_one, w_up_one, small_vals[0])
    act_one = lanes.meet(act_one, down_one, attn_two, up_two)
    lanes.launch(down_one, attn_two, up_two, (down_two, 1))
    act_one, slope_one = lanes.finish(act_one, down_one)
    (w_down_one,) = down_one.result()
    layer_one = project_norm(act_one, w_down_one, attended_one, small_vals[0], 9)
    layer_one = lanes.meet(layer_one, attn_two, up_two, down_two)
    lanes.launch(attn_two, up_two, down_two)
    layer_one, layer_low, feed_xhat_one, feed_inv_one = lanes.finish(layer_one, attn_two)
    w_in_two, w_out_two = attn_two.result()
    w_in_two, w_out_two = lanes.meet((w_in_two, w_out_two), up_two, down_two)
    lanes.launch(up_two, down_two)
    qkv_two = project_in(layer_low, w_in_two, small_vals[1])
    attended = attend_core(qkv_two[0], qkv_two[1], seq_lengths)
    mixed_two, lse_two = lanes.meet(attended, up_two, down_two)
    lanes.launch(up_two, down_two)
    attended_two, _, attn_xhat_two, attn_inv_two = project_norm(
        mixed_two, w_out_two, layer_one, small_vals[1], 2
    )
    rows_in = join_low(forward_product(select_rows, split_low(attended_two, 3)), 3)
    d_rows_out = forward_product(select_rows, cot_flat)
    rows_in = lanes.finish(rows_in, up_two)
    rows_in = lanes.meet(rows_in, down_two)
    lanes.launch(down_two)
    (w_up_two,) = up_two.result()
    rows_low = rows_in.astype(jnp.bfloat16)
    act_two, slope_two = feed_up(rows_low, w_up_two, small_vals[1])
    act_two, slope_two = lanes.finish((act_two, slope_two), down_two)
    (w_down_two,) = down_two.result()
    out_rows, feed_xhat_two, feed_inv_two = feed_down(rows_in, act_two, w_down_two, small_vals[1])
    d_resid, d_branch, d_pre, feed_small_two = feed_down_back(
        d_rows_out, feed_xhat_two, feed_inv_two, slope_two, w_down_two, small_vals[1]
    )
    grads = feed_grads(core, rows_low, d_pre, act_two, d_branch, shard)
    grads, d_resid, d_pre = lanes.meet((grads, d_resid, d_pre))
    g_feed_two = Scatter(*grads, spots, peers)
    lanes.launch(g_feed_two)
    d_in_rows = d_resid + back_product(d_pre, w_up_two)
    back = served_back(
        select_rows,
        split_low(d_in_rows, 2),
        cot_flat,
        attn_xhat_two,
        attn_inv_two,
        small_vals[1],
        w_out_two,
    )
    d_resid, d_branch, d_mixed, sums_out = lanes.meet(back, g_feed_two)
    d_mixed = lanes.settle(d_mixed, g_feed_two)
    lanes.launch(g_feed_two)
    back = attend_core_back(
        core, qkv_two, d_mixed, lse_two, layer_low, mixed_two, d_branch, seq_lengths
    )
    (d_qkv, sums, *grads), d_resid = lanes.meet((back, d_resid), g_feed_two)
    attn_sums_two, out_sums_two = sums, sums_out
    g_attn_two = Scatter(*grads, spots, peers)
    d_resid = lanes.settle(d_resid, g_feed_two)
    lanes.launch(g_feed_two, g_attn_two)
    back = layer_back(
        d_resid,
        d_qkv,
        w_in_two,
        feed_xhat_one,
        feed_inv_one,
        small_vals[0],
        w_down_one,
        slope_one,
    )
    d_resid, d_branch, d_pre, feed_small_one = lanes.meet(back, g_attn_two, g_feed_two)
    d_branch = lanes.settle(d_branch, g_attn_two, g_feed_two)
    lanes.launch(g_attn_two, (g_feed_two, 2))
    grads = feed_grads(core, low_one, d_pre, act_one, d_branch, shard)
    grads, d_resid, d_pre = lanes.meet((grads, d_resid, d_pre), g_attn_two, g_feed_two)
    g_feed_one = Scatter(*grads, spots, peers)
    d_pre = lanes.settle(d_pre, g_attn_two)
    lanes.launch(g_feed_one, g_attn_two)
    back = feed_back(
        d_resid, d_pre, w_up_one, attn_xhat_one, attn_inv_one, small_vals[0], w_out_one
    )
    d_resid, d_branch, d_mixed, sums_out = lanes.meet(back, g_feed_one, g_attn_two)
    d_mixed = lanes.settle(d_mixed, g_feed_one, g_attn_two)
    lanes.launch(g_feed_one, (g_attn_two, 2), g_feed_two)
    small_grads = small_tile(
        (sums_out,) + feed_small_one,
        (out_sums_two,) + feed_small_two,
        attn_sums_two,
        model_width,
    )
    back = attend_core_back(
        core, qkv_one, d_mixed, lse_one, flat_low, mixed_one, d_branch, seq_lengths, small_grads
    )
    back = lanes.meet(
        (back, d_resid, attended_two, out_rows), g_feed_one, g_attn_two, g_feed_two
    )
    (d_qkv, sums, *grads), d_resid, attended_two, out_rows = back
    grads = lanes.settle(grads, g_feed_one, g_attn_two)
    g_attn_one = Scatter(*grads, spots, peers)
    lanes.launch(g_attn_one, g_feed_one, g_attn_two)
    d_tokens = project_in_back(d_resid, d_qkv, w_in_one).astype(jnp.bfloat16)
    d_tokens = lanes.meet(d_tokens, g_attn_one)
    lanes.launch(g_attn_one)
    lanes.meet((), g_feed_one, g_attn_two)
    lanes.launch((g_feed_one, 2))
    attended_two, out_rows = lanes.meet((attended_two, out_rows), g_attn_one, g_feed_one)
    lanes.launch(g_attn_one, g_feed_one)
    output_flat = jnp.where(
        flat_mask,
        weight_grad(select_rows, out_rows.astype(jnp.bfloat16)),
        attended_two,
    ).astype(jnp.bfloat16)
    output_flat = lanes.meet(output_flat, g_attn_one, g_feed_one)
    lanes.launch(g_attn_one)
    lanes.finish((), g_feed_one, g_attn_two, g_feed_two, g_attn_one)
    owned = {
        "attn0": g_attn_one.result(),
        "feed0": g_feed_one.result(),
        "attn1": g_attn_two.result(),
        "feed1": g_feed_two.result(),
    }
    partial_squares = sum(jnp.sum(jnp.square(owned[name].astype(jnp.float32))) for name in owned)
    raw = {name: (owned[name], swap(owned[name])) for name in owned}
    both = {name: both_sides(*raw[name], core) for name in raw}

    def joined(name, start, width):
        return jnp.concatenate([part[:, start : start + width] for part in both[name]], axis=1)

    def down_rows(name):
        return jnp.concatenate(
            [joined(name, hidden_half + part * third, third) for part in range(4)], axis=0
        )

    reduced = (
        order_attn(core, raw["attn0"], raw["attn1"], model_width),
        jnp.stack([joined(name, 0, hidden_half) for name in ("feed0", "feed1")]).astype(
            jnp.float32
        ),
        jnp.stack([down_rows(name) for name in ("feed0", "feed1")]),
        jnp.stack([part[:, wide : wide + 12].T for part in both["attn0"]]),
    )
    partial_squares = partial_squares.reshape(1, 1)
    partial_squares = partial_squares + swap(partial_squares)
    hops = [
        (stage, 1 << at)
        for stage, bits in enumerate(routes(peers)[0])
        for at in range(len(bits))
    ]
    for stage, turn in hops[:-1]:
        partial_squares = partial_squares + shift(partial_squares, stage, turn, peers)
    reduced, partial_squares = lax.optimization_barrier((reduced, partial_squares))
    moved = shift(partial_squares, *hops[-1], peers)
    square_total = (partial_squares + moved)[0, 0]
    grad_norm = jnp.sqrt(square_total).reshape(1)
    clip_scale = jnp.minimum(1.0, CLIP_NORM / (grad_norm[0] + 1e-06))
    step_value = step_count[0].astype(jnp.float32)
    attn_new = adam_update(
        attn_master,
        attn_first,
        attn_second,
        reduced[0],
        clip_scale,
        step_value,
        WEIGHT_DECAY,
        LEARN_RATE,
    )
    up_new = adam_update(
        up_master, up_first, up_second, reduced[1], clip_scale, step_value, WEIGHT_DECAY, LEARN_RATE
    )
    down_new = adam_update(
        down_master,
        down_first,
        down_second,
        reduced[2],
        clip_scale,
        step_value,
        WEIGHT_DECAY,
        LEARN_RATE,
    )
    small_new = adam_update(
        small_master, small_first, small_second, reduced[3], clip_scale, step_value, 0.0, SMALL_RATE
    )
    output = output_flat.reshape(seq_count, length, model_width)
    input_grad = d_tokens.reshape(seq_count, length, model_width)
    return (output, input_grad, grad_norm) + attn_new + up_new + down_new + small_new


def solution(mesh):
    return jax.shard_map(
        per_device,
        mesh=mesh,
        in_specs=(
            P(("dp", "bal"), None, None),
            P(("dp", "bal"), None, None),
            P(("dp", "bal")),
            P(("dp", "bal"), None),
            P(),
            P(None, None, "bal", None),
            P(None, None, "bal", None),
            P(None, None, "bal", None),
            P(None, "bal", None),
            P(None, "bal", None),
            P(None, "bal", None),
            P(None, "bal", None),
            P(None, "bal", None),
            P(None, "bal", None),
            P(None, None, "bal"),
            P(None, None, "bal"),
            P(None, None, "bal"),
        ),
        out_specs=(
            P(("dp", "bal"), None, None),
            P(("dp", "bal"), None, None),
            P(),
            P(None, None, "bal", None),
            P(None, None, "bal", None),
            P(None, None, "bal", None),
            P(None, None, "bal", None),
            P(None, "bal", None),
            P(None, "bal", None),
            P(None, "bal", None),
            P(None, "bal", None),
            P(None, "bal", None),
            P(None, "bal", None),
            P(None, "bal", None),
            P(None, "bal", None),
            P(None, None, "bal"),
            P(None, None, "bal"),
            P(None, None, "bal"),
            P(None, None, "bal"),
        ),
        check_vma=False,
    )
```
